32 devices in a mesh: dp: 8 (over z, core), tensor: 4 (over y, x).
Axes of the slice: x: 2, y: 2, z: 4, core: 2. Of those that a mesh axis runs over, the one named last changes fastest.
Arguments:
- hidden_in: bfloat16 [2048, 1536], P(('dp', 'tensor')), may hold values from -0.75 to 0.75
- queries: bfloat16 [2048, 1536], P(('dp', 'tensor')), may hold values from -9 to 9
- draft_kv: bfloat16 [2048, 2, 512], P(('dp', 'tensor')), may hold values from -9 to 9
- cache_kv: bfloat16 [32, 2048, 2, 512], P('dp', 'tensor'), may hold values from -6 to 6
- cache_len: int32 [32], P('dp'), may hold values from 256 to 2048, as said below
- parents: int32 [32, 64], P('dp'), may hold values from -1 to 62, as said below
- path: int32 [32, 8], P('dp'), may hold values from 0 to 56, as said below
- routes: int32 [8, 256, 8], P(None, 'tensor'), may hold values from 0 to 15, all different within a row; in each aligned block of 64 rows (0 to 63, 64 to 127, ..., all dimensions but the last counted through in order) at most 64 rows name the same one
- w_out: bfloat16 [1536, 1536], P('tensor'), may hold values from -0.15625 to 0.15625
- router: float32 [1536, 16], replicated
- norm_gain: float32 [1536], replicated, may hold values from 0.1 to 1.9
- w_gate: bfloat16 [16, 1536, 512], P('dp'), may hold values from -0.15625 to 0.15625
- w_up: bfloat16 [16, 1536, 512], P('dp'), may hold values from -0.15625 to 0.15625
- w_down: bfloat16 [16, 512, 1536], P('dp'), may hold values from -0.25 to 0.25
Outputs:
- hidden_out: bfloat16 [2048, 1536], P(('dp', 'tensor'))
- compacted: bfloat16 [32, 8, 1024], P('dp')
The draws below stay inside these ranges and needn't reach their ends.
Inputs may be any that keep to these rules, and one draw needn't show every extreme that they name: `parents`: the root is token 0 with parent -1; for i >= 1 the parent of token i is one of tokens i - 8 to i - 1 that are not below 0; in request 0 every token i >= 8 has parent i - 8. Row r lists the tokens of depth 0 to 7 along one root-to-node path of request r's tree; the token of depth k is at most 8 * k. `cache_len`: request 0 has exactly 2048 cached positions. `routes`: the 8 experts of a token differ; in each aligned block of 64 tokens (the tokens of one device between sublayers) any expert may be named by every token.
All inputs are finite; a program needn't handle non-finite values.
Results may differ from the reference program's by a relative error of at most 0.028.
Values may be sent and summed in bfloat16 or wider, within the bound.
No kernel may reach another device: no remote copies, remote signals or barrier semaphores. Data moves between devices by JAX's collectives and lax.ppermute only.
A program may use at most 192 MiB of HBM per device.

```python
import math
import jax
import jax.numpy as jnp
import numpy as np
from jax import lax

D = 1536
QH = 24
KVH = 8
HD = 64
FF = 512
TOP = 8
DRAFT = 64
PATH = 8
SINKS = 4
REQ_DEV = 4
CACHE = 2048
WINDOW = 1024
EXPERTS = 16
REQS = 32
TOKENS = 2048
TOK_SUB = 64
CAP = 64
N_DP = 8


def tree_parents(key):
    offsets = jax.random.randint(jax.random.fold_in(key, 11), (REQS, DRAFT), 1, 9)
    first_row = (jnp.arange(REQS, dtype=jnp.int32) == 0)[:, None]
    offsets = jnp.where(first_row, 8, offsets)
    index = jnp.arange(DRAFT, dtype=jnp.int32)[None, :]
    return jnp.where(index == 0, -1, jnp.maximum(index - offsets, 0)).astype(jnp.int32)


def draw_parents(key, part):
    return tree_parents(key)


def draw_path(key, part):
    parents = tree_parents(key)
    ends = (DRAFT - 1 - jax.random.randint(jax.random.fold_in(key, 12), (REQS,), 0, 8)).astype(jnp.int32)
    ends = jnp.where(jnp.arange(REQS, dtype=jnp.int32) == 0, 8 * (PATH - 1), ends).astype(jnp.int32)

    def climb(step, state):
        walked, current = state
        walked = walked.at[:, step].set(current)
        upper = jnp.take_along_axis(parents, jnp.maximum(current, 0)[:, None], axis=1)[:, 0]
        current = jnp.where(current >= 0, upper, -1).astype(jnp.int32)
        return (walked, current)
    walked, unused = lax.fori_loop(0, DRAFT, climb, (jnp.full((REQS, DRAFT), -1, jnp.int32), ends))
    length = jnp.sum((walked >= 0).astype(jnp.int32), axis=1)
    places = length[:, None] - 1 - jnp.arange(PATH, dtype=jnp.int32)[None, :]
    return jnp.take_along_axis(walked, places, axis=1).astype(jnp.int32)


def draw_cache_len(key, part):
    drawn = jax.random.randint(jax.random.fold_in(key, 51), (REQS,), CACHE // 8, CACHE + 1)
    first = jnp.arange(REQS, dtype=jnp.int32) == 0
    return jnp.where(first, CACHE, drawn).astype(jnp.int32)


def draw_queries(key, part):
    values = jax.random.truncated_normal(jax.random.fold_in(key, 31), -6.0, 6.0, (REQS, DRAFT, QH, HD))
    return values.reshape(TOKENS, QH * HD).astype(jnp.bfloat16)


def draw_draft_kv(key, part):
    keys = jax.random.truncated_normal(jax.random.fold_in(key, 41), -6.0, 6.0, (REQS, DRAFT, KVH, HD))
    values = jax.random.truncated_normal(jax.random.fold_in(key, 42), -6.0, 6.0, (REQS, DRAFT, KVH, HD))
    return jnp.stack([keys.reshape(TOKENS, KVH * HD), values.reshape(TOKENS, KVH * HD)], axis=1).astype(jnp.bfloat16)


def draw_router(key, part):
    return jax.random.truncated_normal(jax.random.fold_in(key, 61), -6.0, 6.0, (D, EXPERTS)) * (0.5 * D ** (-0.5))


def shard_levels(key, dims, pieces, low, top_value):
    loudness, own = 1.0, jax.random.fold_in(key, 6)
    for dim, parts in pieces:
        draws = jnp.exp(jax.random.uniform(jax.random.fold_in(own, dim), (parts,), jnp.float32, low / len(pieces), top_value / len(pieces)))
        loudness = loudness * jnp.repeat(draws, dims[dim] // parts).reshape([-1 if axis == dim else 1 for axis in range(len(dims))])
    return loudness


def shared_out(stream_key, own, number, rows, count, top, bound, lean):
    sequence = jax.random.permutation(stream_key, count)
    heavy_load, ordinary = portions_of(count, rows * top, bound, lean, True), portions_of(count, rows * top, bound, lean, False)
    places = jnp.arange(count)

    def named(tallies, rotation):
        used = int((tallies > 0).sum())
        fixed = max(1, used // 4)
        moved = fixed + (places - fixed + rotation * (used - fixed)) % max(1, count - fixed)
        return jnp.zeros((count,), jnp.int32).at[sequence[jnp.where(places < fixed, places, moved)]].set(jnp.asarray(tallies, jnp.int32))

    tallies = jnp.where(number % 4 == 0, named(heavy_load, number // 4), named(ordinary, number - number // 4 - 1))
    mixed = jax.random.permutation(jax.random.fold_in(own, 3), count)
    source_of, sink = mixed[0:count // 2 * 2:2], mixed[1:count // 2 * 2:2]
    margin = jnp.minimum(tallies[source_of] - 1, bound - tallies[sink]) // 2
    margin = jnp.where((source_of == sequence[0]) | (sink == sequence[0]) | (tallies[sink] == 0), 0, jnp.maximum(margin, 0))
    moved = jax.random.randint(jax.random.fold_in(own, 4), (count // 2,), 0, 1 << 20) % (margin + 1)
    tallies = tallies.at[source_of].add(-moved).at[sink].add(moved)
    labels = jnp.searchsorted(jnp.cumsum(tallies), jnp.arange(rows * top), side="right").astype(jnp.int32)
    grid = labels.reshape(top, rows).T
    grid = grid[jax.random.permutation(jax.random.fold_in(own, 1), rows)]
    rotation = jax.random.randint(jax.random.fold_in(own, 2), (rows, 1), 0, top)
    return jnp.take_along_axis(grid, (jnp.arange(top)[None, :] + rotation) % top, axis=1)


def portions_of(count, total, most, lean, full):
    portions = [(1 << 20) // math.isqrt(grade ** lean) + 1 for grade in range(1, count + 1)]
    largest = most if full else min(most, max(-(-total // count), total * portions[0] // sum(portions)))
    least = 1 if total - largest >= count - 1 else 0
    given, rest = [largest] + [least] * (count - 1), total - largest - least * (count - 1)
    while rest > 0:
        candidates = [i for i in range(1, count) if given[i] < largest] or [i for i in range(1, count) if given[i] < most]
        whole, remaining = sum([portions[i] for i in candidates]), rest
        for i in candidates:
            extra = min(most - given[i], max(1, remaining * portions[i] // whole), rest)
            given[i] = given[i] + extra
            rest = rest - extra
    return np.array(given)


def centred(key, shape, spread, most, shards=(), kind=jnp.bfloat16):
    values = spread * jax.random.normal(key, shape, jnp.float32)
    if shards:
        values = values * shard_levels(key, shape, shards, -0.22, 0.18)
    return jnp.clip(values, -most, most).astype(kind)


def setup_inputs(seed: int = 0) -> dict:
    arg_keys = jax.random.split(jax.random.key(seed), 15)
    hidden_in = centred(arg_keys[0], (TOKENS, D), 0.05, 0.75, ((0, 32),))
    queries = draw_queries(jax.random.fold_in(arg_keys[14], 71), 0)
    draft_kv = draw_draft_kv(jax.random.fold_in(arg_keys[14], 71), 0)
    cache_kv = centred(arg_keys[3], (REQS, CACHE, 2, KVH * HD), 1.0, 6.0, ((0, 8), (1, 4)))
    cache_len = draw_cache_len(jax.random.fold_in(arg_keys[14], 71), 0)
    parents = draw_parents(jax.random.fold_in(arg_keys[14], 71), 0)
    path = draw_path(jax.random.fold_in(arg_keys[14], 71), 0)
    routes_keys = jax.random.split(jax.random.fold_in(arg_keys[7], 1), N_DP * (REQ_DEV * DRAFT) // TOK_SUB)
    routes_turns = jax.random.permutation(jax.random.fold_in(arg_keys[7], 3), N_DP * (REQ_DEV * DRAFT) // TOK_SUB)
    routes = jax.vmap(lambda own, number: shared_out(jax.random.fold_in(arg_keys[7], 2), own, number, TOK_SUB, EXPERTS, TOP, CAP, 2))(routes_keys, routes_turns).reshape((N_DP, REQ_DEV * DRAFT, TOP))
    w_out = centred(arg_keys[8], (QH * HD, D), (QH * HD) ** -0.5, 0.15625, ((0, 4),))
    router = draw_router(jax.random.fold_in(arg_keys[14], 71), 0)
    norm_gain = jnp.clip(1.0 + 0.18 * jax.random.normal(arg_keys[10], (D,), jnp.float32), 0.1, 1.9)
    w_gate = centred(arg_keys[11], (EXPERTS, D, FF), D ** -0.5, 0.15625, ((0, 8),))
    w_up = centred(arg_keys[12], (EXPERTS, D, FF), D ** -0.5, 0.15625, ((0, 8),))
    w_down = centred(arg_keys[13], (EXPERTS, FF, D), FF ** -0.5, 0.25, ((0, 8),))
    return dict(hidden_in=hidden_in, queries=queries, draft_kv=draft_kv, cache_kv=cache_kv, cache_len=cache_len, parents=parents, path=path, routes=routes, w_out=w_out, router=router, norm_gain=norm_gain, w_gate=w_gate, w_up=w_up, w_down=w_down)


NEG = -1e+30

def rotate(values, positions):
    half = values.shape[-1] // 2
    inverse = 10000.0 ** (-2.0 * jnp.arange(half, dtype=jnp.float32) / values.shape[-1])
    angle = positions.astype(jnp.float32)[:, None] * inverse[None, :]
    cosine = jnp.cos(angle)[:, None, :]
    sine = jnp.sin(angle)[:, None, :]
    first = values[..., :half]
    second = values[..., half:]
    return jnp.concatenate([first * cosine - second * sine, second * cosine + first * sine], axis=-1)

def closure(parents):
    count = parents.shape[-1]
    index = jnp.arange(count, dtype=jnp.int32)
    linked = (parents[..., :, None] == index).astype(jnp.float32) + jnp.eye(count, dtype=jnp.float32)
    for level in range((count - 1).bit_length()):
        linked = jnp.minimum(jnp.einsum('...ij,...jk->...ik', linked, linked, precision=lax.Precision.HIGHEST), 1.0)
    return linked

def lowered(values):
    rounded = lax.optimization_barrier(values.astype(jnp.bfloat16))
    return rounded.astype(jnp.float32)

def reference(hidden_in, queries, draft_kv, cache_kv, cache_len, parents, path, routes, w_out, router, norm_gain, w_gate, w_up, w_down):
    scale = HD ** (-0.5)
    groups = QH // KVH
    highest = lax.Precision.HIGHEST
    ancestry = closure(parents)
    depth = lax.optimization_barrier(jnp.sum(ancestry, axis=-1)).astype(jnp.int32) - 1
    positions = (cache_len[:, None] + depth).reshape(-1)
    query_rot = rotate(queries.astype(jnp.float32).reshape(TOKENS, QH, HD), positions).reshape(TOKENS, QH * HD).astype(jnp.bfloat16)
    key_rot = rotate(draft_kv[:, 0].astype(jnp.float32).reshape(TOKENS, KVH, HD), positions).reshape(TOKENS, KVH * HD).astype(jnp.bfloat16)
    draft_values = draft_kv[:, 1]
    key_pos = jnp.arange(CACHE, dtype=jnp.int32)

    def attend(items):
        query_block, key_block, value_block, cache_block, length, ancestors, place = items
        query_heads = query_block.astype(jnp.float32).reshape(DRAFT, KVH, groups, HD)
        cache_keys = cache_block[:, 0].astype(jnp.float32).reshape(CACHE, KVH, HD)
        cache_values = cache_block[:, 1].astype(jnp.float32).reshape(CACHE, KVH, HD)
        own_keys = key_block.astype(jnp.float32).reshape(DRAFT, KVH, HD)
        own_values = value_block.astype(jnp.float32).reshape(DRAFT, KVH, HD)
        far_ok = (key_pos[None, :] < length) & ((key_pos[None, :] < SINKS) | (place[:, None] - key_pos[None, :] < WINDOW))
        near_ok = ancestors > 0.5
        far_scores = jnp.einsum('igqd,jgd->gqij', query_heads, cache_keys, precision=highest) * scale
        near_scores = jnp.einsum('igqd,jgd->gqij', query_heads, own_keys, precision=highest) * scale
        far_scores = jnp.where(far_ok[None, None], far_scores, NEG)
        near_scores = jnp.where(near_ok[None, None], near_scores, NEG)
        top = jnp.maximum(lax.optimization_barrier(jnp.max(far_scores, axis=-1)), lax.optimization_barrier(jnp.max(near_scores, axis=-1)))[..., None]
        far_weights = jnp.where(far_ok[None, None], jnp.exp(far_scores - top), 0.0)
        near_weights = jnp.where(near_ok[None, None], jnp.exp(near_scores - top), 0.0)
        totals = lax.optimization_barrier(jnp.sum(far_weights, axis=-1)) + lax.optimization_barrier(jnp.sum(near_weights, axis=-1))
        blended = jnp.einsum('gqij,jgd->igqd', lowered(far_weights), cache_values, precision=highest)
        blended = blended + jnp.einsum('gqij,jgd->igqd', lowered(near_weights), own_values, precision=highest)
        result = blended / jnp.transpose(totals, (2, 0, 1))[..., None]
        return result.reshape(DRAFT, QH * HD).astype(jnp.bfloat16)
    attention = lax.map(attend, (query_rot.reshape(REQS, DRAFT, QH * HD), key_rot.reshape(REQS, DRAFT, KVH * HD), draft_values.reshape(REQS, DRAFT, KVH * HD), cache_kv, cache_len, ancestry, positions.reshape(REQS, DRAFT)))
    attention = attention.reshape(TOKENS, QH * HD)
    mixed_state = hidden_in.astype(jnp.float32) + jnp.dot(attention, w_out, preferred_element_type=jnp.float32)
    normed = (mixed_state * lax.rsqrt(lax.optimization_barrier(jnp.mean(mixed_state * mixed_state, axis=-1, keepdims=True)) + 1e-06) * norm_gain).astype(jnp.bfloat16)
    logits = jnp.dot(normed, router, preferred_element_type=jnp.float32)
    chosen = routes.reshape(TOKENS, TOP)
    gates = jax.nn.softmax(jnp.take_along_axis(logits, chosen, axis=1), axis=-1)
    tile = 256
    flat = chosen.reshape(-1)
    assigned = flat.shape[0]
    order = jnp.argsort(flat, stable=True).astype(jnp.int32)
    ranked = flat[order]
    counts = lax.optimization_barrier(jnp.sum((flat[:, None] == jnp.arange(EXPERTS, dtype=jnp.int32)[None, :]).astype(jnp.int32), axis=0))
    padded = (counts + tile - 1) // tile * tile
    pad_start = jnp.cumsum(padded) - padded
    seg_start = jnp.cumsum(counts) - counts
    place = pad_start[ranked] + jnp.arange(assigned, dtype=jnp.int32) - seg_start[ranked]
    tiles = (assigned + tile - 1) // tile + EXPERTS
    filled = jnp.full((tiles * tile,), assigned, jnp.int32).at[place].set(order)
    tile_expert = lax.optimization_barrier(jnp.sum((pad_start[None, :] <= (jnp.arange(tiles, dtype=jnp.int32) * tile)[:, None]).astype(jnp.int32), axis=1)) - 1
    token_of = jnp.where(filled < assigned, filled // TOP, TOKENS).astype(jnp.int32)
    gate_of = jnp.where(filled < assigned, gates.reshape(-1)[jnp.minimum(filled, assigned - 1)], 0.0)
    normed_pad = jnp.concatenate([normed, jnp.zeros((1, D), jnp.bfloat16)], axis=0)

    def expert_tile(carry, items):
        rows_token, rows_gate, expert = items
        rows = normed_pad[rows_token]
        gate_hidden = jnp.dot(rows, w_gate[expert], preferred_element_type=jnp.float32)
        up_hidden = jnp.dot(rows, w_up[expert], preferred_element_type=jnp.float32)
        activated = (jax.nn.silu(gate_hidden) * up_hidden).astype(jnp.bfloat16)
        produced = jnp.dot(activated, w_down[expert], preferred_element_type=jnp.float32).astype(jnp.bfloat16)
        return (carry.at[rows_token].add(rows_gate[:, None] * produced.astype(jnp.float32)), None)
    moe, unused = lax.scan(expert_tile, jnp.zeros((TOKENS + 1, D), jnp.float32), (token_of.reshape(tiles, tile), gate_of.reshape(tiles, tile), tile_expert))
    hidden_out = (mixed_state + moe[:TOKENS]).astype(jnp.bfloat16)
    packed = jnp.concatenate([key_rot, draft_values], axis=1)
    picks = (jnp.arange(REQS, dtype=jnp.int32)[:, None] * DRAFT + path).reshape(-1)
    compacted = packed[picks].reshape(REQS, PATH, 2 * KVH * HD)
    return (hidden_out, compacted)
```

```python
import functools

import jax
import jax.numpy as jnp
import numpy as np
from jax import lax
from jax.experimental import pallas as pl
from jax.experimental.pallas import tpu as pltpu
from jax.sharding import PartitionSpec as P

QH = 24
KVH = 8
HD = 64
TOP = 8
SINKS = 4
WINDOW = 1024

LANES = 128
PAIRS = KVH * HD // LANES
GROUPS = QH // KVH
CORES = 2
NEG = -1e30
FLOOR = -1e6
BF = jnp.bfloat16
F32 = jnp.float32
LOG2E = 1.4426950408889634
VMEM_LIMIT = 60 * 1024 * 1024

_half = HD // 2
INVERSE = np.tile(
    (10000.0 ** (-2.0 * np.arange(_half, dtype=np.float64) / HD)).astype(np.float32), LANES // _half
).reshape(1, LANES)


def params(**kw):
    return pltpu.CompilerParams(vmem_limit_bytes=VMEM_LIMIT, **kw)


def whole():
    return pl.BlockSpec(memory_space=pltpu.VMEM)


def scalars():
    return pl.BlockSpec(memory_space=pltpu.SMEM)


def exchange(x, axis, size, step):
    return lax.ppermute(x, axis, [(i, i ^ step) for i in range(size)])


def lane_index(shape):
    return lax.broadcasted_iota(jnp.int32, shape, len(shape) - 1)


def prelude_kernel(
    where_ref, len_ref, path_ref, par_ref, inv_ref, q_ref, kv_ref,
    pay_ref, key_ref, val_ref, anc_ref, pos_ref, kv_f, pos_own, anc_all,
):
    requests, draft = par_ref.shape
    n = q_ref.shape[0]
    own_start = where_ref[0] * n
    request = own_start // draft
    offset = own_start % draft
    row = lax.broadcasted_iota(jnp.int32, (draft, draft), 0)
    col = lax.broadcasted_iota(jnp.int32, (draft, draft), 1)
    eye = (row == col).astype(F32)
    linked = [
        ((row == par_ref[r : r + 1, :]).astype(F32) + eye).T.astype(BF) for r in range(requests)
    ]
    for level in range((draft - 1).bit_length()):
        linked = [
            jnp.minimum(jnp.dot(m, m, preferred_element_type=F32), 1.0).astype(BF) for m in linked
        ]
    for r in range(requests):
        ancestry = linked[r].astype(F32)
        depth = jnp.sum(ancestry, axis=-1, keepdims=True) - 1.0
        place = depth + len_ref[r].astype(F32)
        pos_ref[r * draft : (r + 1) * draft, :] = jnp.broadcast_to(place, (draft, LANES))
        anc_all[r] = ancestry
    anc_ref[...] = anc_all[request]
    own = pl.multiple_of(own_start, 8)
    angle = pos_ref[pl.ds(own, n), :] * inv_ref[...]
    lane = lane_index((n, LANES))
    front = lane % HD < HD // 2
    cosine = jnp.cos(angle)
    sine = jnp.sin(angle)
    sine = jnp.where(front, -sine, sine)
    low = lane < HD

    def turned(x):
        partner = jnp.where(
            front, pltpu.roll(x, LANES - HD // 2, axis=1), pltpu.roll(x, HD // 2, axis=1)
        )
        return x * cosine + partner * sine

    kv_f[...] = kv_ref[...].astype(F32)
    picks = []
    slot = lax.broadcasted_iota(jnp.int32, (path_ref.shape[1], n), 0)
    token = lax.broadcasted_iota(jnp.int32, (path_ref.shape[1], n), 1) + offset
    wanted = jnp.full(slot.shape, -1, jnp.int32)
    for k in range(path_ref.shape[1]):
        wanted = jnp.where(slot == k, path_ref[request, k], wanted)
    chooser = (wanted == token).astype(BF)
    keys, vals = [], []
    for b in range(PAIRS):
        keys.append(turned(kv_f[pl.ds(2 * b, n, stride=2 * PAIRS), :]).astype(BF))
        vals.append(kv_f[pl.ds(2 * b + 1, n, stride=2 * PAIRS), :].astype(BF))
        key_ref[:, b * LANES : (b + 1) * LANES] = keys[b]
        val_ref[:, b * LANES : (b + 1) * LANES] = vals[b]
    packed = jnp.concatenate(keys + vals, axis=1)
    picked = jnp.dot(chooser, packed, preferred_element_type=F32).astype(BF)
    pay_ref[n:, : packed.shape[1]] = picked
    pay_ref[n:, packed.shape[1] :] = jnp.zeros(
        (path_ref.shape[1], pay_ref.shape[1] - packed.shape[1]), BF
    )
    for b in range(PAIRS):
        x0, x1, x2 = [
            turned(q_ref[:, (GROUPS * b + i) * LANES : (GROUPS * b + i + 1) * LANES].astype(F32))
            for i in range(GROUPS)
        ]
        y0 = jnp.where(low, x0, x1)
        y1 = jnp.where(low, pltpu.roll(x0, HD, axis=1), pltpu.roll(x2, HD, axis=1))
        y2 = jnp.where(low, x1, x2)
        for i, y in enumerate((y0, y1, y2)):
            pay_ref[:n, (GROUPS * b + i) * LANES : (GROUPS * b + i + 1) * LANES] = y.astype(BF)


def prelude(where, cache_len, path, parents, queries, kv):
    requests, draft = parents.shape
    n, width = queries.shape
    kv_width = KVH * HD
    return pl.pallas_call(
        prelude_kernel,
        out_shape=(
            jax.ShapeDtypeStruct((n + path.shape[1], width), BF),
            jax.ShapeDtypeStruct((n, kv_width), BF),
            jax.ShapeDtypeStruct((n, kv_width), BF),
            jax.ShapeDtypeStruct((draft, draft), F32),
            jax.ShapeDtypeStruct((requests * draft, LANES), F32),
        ),
        in_specs=[scalars(), scalars(), scalars(), whole(), whole(), whole(), whole()],
        out_specs=(whole(),) * 5,
        scratch_shapes=[
            pltpu.VMEM(kv.shape, F32),
            pltpu.VMEM((n, LANES), F32),
            pltpu.VMEM((requests, draft, draft), F32),
        ],
        compiler_params=params(),
        name="prelude",
    )(where, cache_len, path, parents, jnp.asarray(INVERSE), queries, kv)


def attend_kernel(
    step, near, where_ref, len_ref, pay_ref, kv_ref, key_ref, val_ref, anc_ref, pos_ref,
    out_ref, kv_f,
):
    draft = anc_ref.shape[0]
    n = key_ref.shape[0]
    cells = kv_ref.shape[1] // (2 * PAIRS)
    me = where_ref[0]
    start = (me ^ step) * n
    request = start // draft
    key_start = me * cells
    place = pos_ref[pl.ds(pl.multiple_of(start, 8), n), :][:, :1]
    key_pos = (lane_index((n, cells)) + key_start).astype(F32)
    far_ok = (key_pos < len_ref[request].astype(F32)) & (
        (key_pos < SINKS) | (place - key_pos < WINDOW)
    )
    bias = jnp.where(far_ok, 0.0, NEG)
    bias = jnp.concatenate([bias] * (2 * GROUPS), axis=0)
    if near:
        own = me * n
        same = (own // draft) == request
        line = anc_ref[pl.ds(pl.multiple_of(start % draft, 8), n), :]
        if n != draft:
            pick = (
                lax.broadcasted_iota(jnp.int32, (draft, n), 0)
                == lax.broadcasted_iota(jnp.int32, (draft, n), 1) + own % draft
            ).astype(BF)
            line = jnp.dot(line.astype(BF), pick, preferred_element_type=F32)
        seen = jnp.where(same, line, 0.0)
        near_bias = jnp.where(seen > 0.5, 0.0, NEG)
        near_bias = jnp.concatenate([near_bias] * (2 * GROUPS), axis=0)
    kv_f[...] = kv_ref[0].astype(F32)
    low = lane_index((n, LANES)) < HD
    lane = lane_index((n, LANES))
    stats = jnp.zeros((n, LANES), F32)
    turn = (((1,), (1,)), ((), ()))
    factor = HD ** (-0.5) * LOG2E
    for b in range(PAIRS):
        keys = kv_f[pl.ds(2 * b, cells, stride=2 * PAIRS), :].astype(BF)
        vals = kv_f[pl.ds(2 * b + 1, cells, stride=2 * PAIRS), :].astype(BF)
        blocks = [
            pay_ref[:n, (GROUPS * b + i) * LANES : (GROUPS * b + i + 1) * LANES]
            for i in range(GROUPS)
        ]
        zero = jnp.zeros((n, LANES), BF)
        rows = jnp.concatenate(
            [jnp.where(low, x, zero) for x in blocks] + [jnp.where(low, zero, x) for x in blocks],
            axis=0,
        )
        scores = lax.dot_general(rows, keys, turn, preferred_element_type=F32) * factor + bias
        top = jnp.max(scores, axis=-1, keepdims=True)
        if near:
            near_scores = (
                lax.dot_general(
                    rows, key_ref[:, b * LANES : (b + 1) * LANES], turn, preferred_element_type=F32
                )
                * factor
                + near_bias
            )
            top = jnp.maximum(top, jnp.max(near_scores, axis=-1, keepdims=True))
        top = jnp.maximum(top, FLOOR)
        top = (top + jnp.abs(top) * (2.0**-7)).astype(BF).astype(F32)
        weights = jnp.exp2(scores - top)
        total = jnp.sum(weights, axis=-1, keepdims=True)
        blend = jnp.dot(weights.astype(BF), vals, preferred_element_type=F32)
        if near:
            near_weights = jnp.exp2(near_scores - top)
            total = total + jnp.sum(near_weights, axis=-1, keepdims=True)
            blend = blend + jnp.dot(
                near_weights.astype(BF),
                val_ref[:, b * LANES : (b + 1) * LANES],
                preferred_element_type=F32,
            )
        high = total.astype(BF).astype(F32)
        rest = total - high
        for i in range(GROUPS):
            first = slice(i * n, (i + 1) * n)
            second = slice((GROUPS + i) * n, (GROUPS + i + 1) * n)
            block = GROUPS * b + i
            out_ref[:, block * LANES : (block + 1) * LANES] = jnp.where(
                low, blend[first], blend[second]
            ).astype(BF)
            for part, rows_of in enumerate((first, second)):
                at = 2 * block + part
                stats = jnp.where(lane == at, top[rows_of], stats)
                stats = jnp.where(lane == QH + at, high[rows_of], stats)
                stats = jnp.where(lane == 2 * QH + at, rest[rows_of], stats)
    out_ref[:, QH * HD :] = stats.astype(BF)


def attend(step, near, where, cache_len, payload, cache, keys, vals, ancestry, pos):
    n = keys.shape[0]
    draft = ancestry.shape[0]
    span = cache.shape[1]

    def cache_block(i, where_ref, len_ref):
        return ((where_ref[0] ^ step) * n // draft, 0, 0)

    def full(x):
        return pl.BlockSpec(x.shape, lambda i, *_: (0,) * x.ndim)

    return pl.pallas_call(
        functools.partial(attend_kernel, step, near),
        out_shape=jax.ShapeDtypeStruct((n, QH * HD + LANES), BF),
        grid_spec=pltpu.PrefetchScalarGridSpec(
            num_scalar_prefetch=2,
            grid=(1,),
            in_specs=[
                full(payload),
                pl.BlockSpec((1, span, LANES), cache_block),
                full(keys),
                full(vals),
                full(ancestry),
                full(pos),
            ],
            out_specs=pl.BlockSpec((n, QH * HD + LANES), lambda i, *_: (0, 0)),
            scratch_shapes=[pltpu.VMEM((span, LANES), F32)],
        ),
        compiler_params=params(),
        name="attend",
    )(where, cache_len, payload, cache, keys, vals, ancestry, pos)


def join_kernel(count, where_ref, *refs):
    parts, rest = refs[:count], refs[count:]
    pieces, rest = rest[:count], rest[count:]
    hidden_ref, gain_ref, mixed_ref, normed_ref, att, weight, sems = rest
    n = hidden_ref.shape[0]
    depth = pieces[0].shape[0]
    width = QH * HD
    me = where_ref[0]
    copies = []
    for k in range(count):
        at = pl.multiple_of((me ^ k) * depth, 16)
        copies.append(
            pltpu.make_async_copy(pieces[k], weight.at[pl.ds(at, depth), :], sems.at[k])
        )
        copies[-1].start()
    stats = [p[:, width:].astype(F32) for p in parts]
    top = stats[0]
    for s in stats[1:]:
        top = jnp.maximum(top, s)
    scales = [jnp.exp2(s - top) for s in stats]
    total = jnp.zeros((n, LANES), F32)
    for s, scale in zip(stats, scales):
        sums = pltpu.roll(s, LANES - QH, axis=1) + pltpu.roll(s, LANES - 2 * QH, axis=1)
        total = total + scale * sums
    inverse = 1.0 / total
    scales = [scale * inverse for scale in scales]
    low = lane_index((n, LANES)) < HD

    for b in range(PAIRS):
        joined = []
        for i in range(GROUPS):
            block = GROUPS * b + i
            acc = jnp.zeros((n, LANES), F32)
            for p, scale in zip(parts, scales):
                by = jnp.where(
                    low, scale[:, 2 * block : 2 * block + 1], scale[:, 2 * block + 1 : 2 * block + 2]
                )
                acc = acc + by * p[:, block * LANES : (block + 1) * LANES].astype(F32)
            joined.append(acc)
        turned = pltpu.roll(joined[1], HD, axis=1)
        back = (
            jnp.where(low, joined[0], turned),
            jnp.where(low, joined[2], joined[0]),
            jnp.where(low, turned, joined[2]),
        )
        for i in range(GROUPS):
            block = GROUPS * b + i
            att[:, block * LANES : (block + 1) * LANES] = back[i].astype(BF)
    for copy in copies:
        copy.wait()
    attended = jnp.dot(att[...], weight[...], preferred_element_type=F32)
    mixed = hidden_ref[...].astype(F32) + attended
    mixed_ref[...] = mixed
    square = jnp.mean(mixed * mixed, axis=-1, keepdims=True)
    normed_ref[...] = (mixed * lax.rsqrt(square + 1e-06) * gain_ref[...]).astype(BF)


def join(where, parts, pieces, hidden_in, gain):
    n, width = hidden_in.shape
    count = len(parts)
    inner = QH * HD
    return pl.pallas_call(
        functools.partial(join_kernel, count),
        out_shape=(
            jax.ShapeDtypeStruct((n, width), F32),
            jax.ShapeDtypeStruct((n, width), BF),
        ),
        in_specs=[scalars()]
        + [whole()] * count
        + [pl.BlockSpec(memory_space=pl.ANY)] * count
        + [whole(), whole()],
        out_specs=(whole(), whole()),
        scratch_shapes=[
            pltpu.VMEM((n, inner), BF),
            pltpu.VMEM((inner, width), BF),
            pltpu.SemaphoreType.DMA((count,)),
        ],
        compiler_params=params(),
        name="join",
    )(where, *parts, *pieces, hidden_in, gain)


def experts_kernel(
    count, where_ref, routes_ref, router_ref, gate_hbm, up_hbm, down_hbm, *refs
):
    slots, (own_ref, other_ref, x, acc, gates_s, wg, wu, wd, sems) = refs[:count], refs[count:]
    n, width = slots[0].shape
    local = gate_hbm.shape[0]
    experts = router_ref.shape[1]
    me = where_ref[1]
    copies = []
    for e in range(local):
        for j, (src, dst) in enumerate(((gate_hbm, wg), (up_hbm, wu), (down_hbm, wd))):
            copies.append(pltpu.make_async_copy(src.at[e], dst.at[e], sems.at[3 * e + j]))
            copies[-1].start()
    router = router_ref[...]
    router_high = router.astype(BF)
    router_low = (router - router_high.astype(F32)).astype(BF)
    for s in range(count):
        x[s * n : (s + 1) * n, :] = slots[s][...]
    rows = count * n
    logits = jnp.dot(x[...], router_high, preferred_element_type=F32) + jnp.dot(
        x[...], router_low, preferred_element_type=F32
    )
    lane = lane_index((n, experts))
    for s in range(count):
        chosen = routes_ref[me ^ s]
        hit = lane == chosen[:, 0:1]
        for k in range(1, chosen.shape[1]):
            hit = hit | (lane == chosen[:, k : k + 1])
        part = jnp.where(hit, logits[s * n : (s + 1) * n, :], NEG)
        part = jnp.exp(part - jnp.max(part, axis=-1, keepdims=True))
        part = jnp.where(hit, part, 0.0)
        gates_s[s * n : (s + 1) * n, :] = part / jnp.sum(part, axis=-1, keepdims=True)
    tile = min(rows, 256)
    for e in range(local):
        for j in range(3):
            copies[3 * e + j].wait()
        for t in range(rows // tile):
            span = slice(t * tile, (t + 1) * tile)
            block = x[span, :]
            gate_hidden = jnp.dot(block, wg[e], preferred_element_type=F32)
            up_hidden = jnp.dot(block, wu[e], preferred_element_type=F32)
            activated = (gate_hidden / (1.0 + jnp.exp(-gate_hidden)) * up_hidden).astype(BF)
            made = jnp.dot(activated, wd[e], preferred_element_type=F32).astype(BF).astype(F32)
            mine = lane_index((tile, experts)) == me * local + e
            gate = jnp.sum(jnp.where(mine, gates_s[span, :], 0.0), axis=-1, keepdims=True)
            if e == 0:
                acc[span, :] = gate * made
            else:
                acc[span, :] = acc[span, :] + gate * made
    for s in range(count):
        if s % CORES == 0:
            own_ref[s // CORES] = acc[s * n : (s + 1) * n, :]
        else:
            other_ref[s // CORES] = acc[s * n : (s + 1) * n, :].astype(BF)


def experts_part(where, routes, router, w_gate, w_up, w_down, slots):
    count = len(slots)
    n, width = slots[0].shape
    local, _, hidden = w_gate.shape
    return pl.pallas_call(
        functools.partial(experts_kernel, count),
        out_shape=(
            jax.ShapeDtypeStruct((count // CORES, n, width), F32),
            jax.ShapeDtypeStruct((count // CORES, n, width), BF),
        ),
        in_specs=[scalars(), whole(), whole()]
        + [pl.BlockSpec(memory_space=pl.ANY)] * 3
        + [whole()] * count,
        out_specs=(whole(), whole()),
        scratch_shapes=[
            pltpu.VMEM((count * n, width), BF),
            pltpu.VMEM((count * n, width), F32),
            pltpu.VMEM((count * n, router.shape[1]), F32),
            pltpu.VMEM((local, width, hidden), BF),
            pltpu.VMEM((local, width, hidden), BF),
            pltpu.VMEM((local, hidden, width), BF),
            pltpu.SemaphoreType.DMA((3 * local,)),
        ],
        compiler_params=params(),
        name="experts",
    )(where, routes, router, w_gate, w_up, w_down, *slots)


def accepted_kernel(count, n, where_ref, *refs):
    out_ref = refs[count]
    requests = out_ref.shape[0]
    draft = count * n // requests
    out_ref[...] = jnp.zeros(out_ref.shape, out_ref.dtype)
    for k in range(count):
        request = (where_ref[0] ^ k) * n // draft
        out_ref[request] = out_ref[request] + refs[k][:, : out_ref.shape[2]]


def accepted(where, payloads, requests, entries, n):
    count = len(payloads)
    block = pl.BlockSpec((entries, payloads[0].shape[1]), lambda i: (n // entries, 0))
    return pl.pallas_call(
        functools.partial(accepted_kernel, count, n),
        out_shape=jax.ShapeDtypeStruct((requests, entries, 2 * KVH * HD), BF),
        grid=(1,),
        in_specs=[scalars()] + [block] * count,
        out_specs=pl.BlockSpec((requests, entries, 2 * KVH * HD), lambda i: (0, 0, 0)),
        compiler_params=params(),
        name="accepted",
    )(where, *payloads)


def rows_by_lane_block(kv):
    lead, (tokens, two, width) = kv.shape[:-3], kv.shape[-3:]
    split = kv.reshape(*lead, tokens, two, width // LANES, LANES)
    return jnp.swapaxes(split, -3, -2).reshape(*lead, tokens * two * width // LANES, LANES)


def body(
    hidden_in, queries, draft_kv, cache_kv, cache_len, parents, path, routes,
    w_out, router, norm_gain, w_gate, w_up, w_down,
):
    tensor = lax.axis_size("tensor")
    data = lax.axis_size("dp")
    n = queries.shape[0]
    requests, draft = parents.shape
    where = jnp.stack([lax.axis_index("tensor"), lax.axis_index("dp")]).astype(jnp.int32)
    payload, keys, vals, ancestry, pos = prelude(
        where, cache_len, path, parents, queries, rows_by_lane_block(draft_kv)
    )
    cache = rows_by_lane_block(cache_kv)
    payloads = [payload] + [exchange(payload, "tensor", tensor, k) for k in range(1, tensor)]
    pieces = [w_out] + [exchange(w_out, "tensor", tensor, k) for k in range(1, tensor)]
    parts = []
    for k in range(tensor):
        near = k < max(1, draft // n)
        part = attend(k, near, where, cache_len, payloads[k], cache, keys, vals, ancestry, pos)
        parts.append(part if k == 0 else exchange(part, "tensor", tensor, k))
    compacted = accepted(where, payloads, requests, path.shape[1], n)
    mixed, normed = join(where, parts, pieces, hidden_in, norm_gain.reshape(1, -1))

    steps = data // CORES
    lines = [normed] + [exchange(normed, "dp", data, CORES * k) for k in range(1, steps)]
    slots = []
    for line in lines:
        slots += [line, exchange(line, "dp", data, 1)]
    own, other = experts_part(where, routes, router, w_gate, w_up, w_down, slots)
    chip = own + exchange(other, "dp", data, 1).astype(F32)
    total = mixed + chip[0]
    low = chip.astype(BF)
    for k in range(1, steps):
        total = total + exchange(low[k], "dp", data, CORES * k).astype(F32)
    return total.astype(BF), compacted


def solution(mesh):
    in_specs = (
        P(("dp", "tensor"), None),
        P(("dp", "tensor"), None),
        P(("dp", "tensor"), None, None),
        P("dp", "tensor", None, None),
        P("dp"),
        P("dp", None),
        P("dp", None),
        P(None, "tensor", None),
        P("tensor", None),
        P(),
        P(),
        P("dp", None, None),
        P("dp", None, None),
        P("dp", None, None),
    )
    out_specs = (P(("dp", "tensor"), None), P("dp", None, None))
    return jax.shard_map(body, mesh=mesh, in_specs=in_specs, out_specs=out_specs, check_vma=False)
```

```python
import functools

import jax
import jax.numpy as jnp
import numpy as np
from jax import lax
from jax.experimental import pallas as pl
from jax.experimental.pallas import tpu as pltpu
from jax.sharding import PartitionSpec as P

QH = 24
KVH = 8
HD = 64
TOP = 8
SINKS = 4
WINDOW = 1024

LANES = 128
PAIRS = KVH * HD // LANES
GROUPS = QH // KVH
CORES = 2
NEG = -1e30
FLOOR = -1e6
BF = jnp.bfloat16
F32 = jnp.float32
LOG2E = 1.4426950408889634
MIB = 1024 * 1024

_half = HD // 2
INVERSE = np.tile(
    (10000.0 ** (-2.0 * np.arange(_half, dtype=np.float64) / HD)).astype(np.float32), LANES // _half
).reshape(1, LANES)


def params(mib):
    return pltpu.CompilerParams(vmem_limit_bytes=mib * MIB)


def whole():
    return pl.BlockSpec(memory_space=pltpu.VMEM)


def blocked(x):
    return pl.BlockSpec(x.shape, lambda i: (0,) * x.ndim)


def scalars():
    return pl.BlockSpec(memory_space=pltpu.SMEM)


def exchange(x, axis, size, step):
    return lax.ppermute(x, axis, [(i, i ^ step) for i in range(size)])


def lane_index(shape):
    return lax.broadcasted_iota(jnp.int32, shape, len(shape) - 1)


def prelude_kernel(
    where_ref, len_ref, path_ref, par_ref, inv_ref, q_ref, kv_ref,
    pay_ref, key_ref, val_ref, anc_ref, pos_ref, kv_f, pos_own, anc_all,
):
    requests, draft = par_ref.shape
    n = q_ref.shape[0]
    own_start = where_ref[0] * n
    request = own_start // draft
    offset = own_start % draft
    row = lax.broadcasted_iota(jnp.int32, (draft, draft), 0)
    col = lax.broadcasted_iota(jnp.int32, (draft, draft), 1)
    eye = (row == col).astype(F32)
    linked = [
        ((row == par_ref[r : r + 1, :]).astype(F32) + eye).T.astype(BF) for r in range(requests)
    ]
    for level in range((draft - 1).bit_length()):
        linked = [
            jnp.minimum(jnp.dot(m, m, preferred_element_type=F32), 1.0).astype(BF) for m in linked
        ]
    for r in range(requests):
        ancestry = linked[r].astype(F32)
        depth = jnp.sum(ancestry, axis=-1, keepdims=True) - 1.0
        place = depth + len_ref[r].astype(F32)
        pos_ref[r * draft : (r + 1) * draft, :] = jnp.broadcast_to(place, (draft, LANES))
        anc_all[r] = ancestry
    anc_ref[...] = anc_all[request]
    own = pl.multiple_of(own_start, 8)
    angle = pos_ref[pl.ds(own, n), :] * inv_ref[...]
    lane = lane_index((n, LANES))
    front = lane % HD < HD // 2
    cosine = jnp.cos(angle)
    sine = jnp.sin(angle)
    sine = jnp.where(front, -sine, sine)
    low = lane < HD

    def turned(x):
        partner = jnp.where(
            front, pltpu.roll(x, LANES - HD // 2, axis=1), pltpu.roll(x, HD // 2, axis=1)
        )
        return x * cosine + partner * sine

    kv_f[...] = kv_ref[...].astype(F32)
    picks = []
    slot = lax.broadcasted_iota(jnp.int32, (path_ref.shape[1], n), 0)
    token = lax.broadcasted_iota(jnp.int32, (path_ref.shape[1], n), 1) + offset
    wanted = jnp.full(slot.shape, -1, jnp.int32)
    for k in range(path_ref.shape[1]):
        wanted = jnp.where(slot == k, path_ref[request, k], wanted)
    chooser = (wanted == token).astype(BF)
    keys, vals = [], []
    for b in range(PAIRS):
        keys.append(turned(kv_f[pl.ds(2 * b, n, stride=2 * PAIRS), :]).astype(BF))
        vals.append(kv_f[pl.ds(2 * b + 1, n, stride=2 * PAIRS), :].astype(BF))
        key_ref[:, b * LANES : (b + 1) * LANES] = keys[b]
        val_ref[:, b * LANES : (b + 1) * LANES] = vals[b]
    packed = jnp.concatenate(keys + vals, axis=1)
    picked = jnp.dot(chooser, packed, preferred_element_type=F32).astype(BF)
    pay_ref[n:, : packed.shape[1]] = picked
    pay_ref[n:, packed.shape[1] :] = jnp.zeros(
        (path_ref.shape[1], pay_ref.shape[1] - packed.shape[1]), BF
    )
    for b in range(PAIRS):
        x0, x1, x2 = [
            turned(q_ref[:, (GROUPS * b + i) * LANES : (GROUPS * b + i + 1) * LANES].astype(F32))
            for i in range(GROUPS)
        ]
        y0 = jnp.where(low, x0, x1)
        y1 = jnp.where(low, pltpu.roll(x0, HD, axis=1), pltpu.roll(x2, HD, axis=1))
        y2 = jnp.where(low, x1, x2)
        for i, y in enumerate((y0, y1, y2)):
            pay_ref[:n, (GROUPS * b + i) * LANES : (GROUPS * b + i + 1) * LANES] = y.astype(BF)


def prelude(where, cache_len, path, parents, queries, kv):
    requests, draft = parents.shape
    n, width = queries.shape
    kv_width = KVH * HD
    return pl.pallas_call(
        prelude_kernel,
        out_shape=(
            jax.ShapeDtypeStruct((n + path.shape[1], width), BF),
            jax.ShapeDtypeStruct((n, kv_width), BF),
            jax.ShapeDtypeStruct((n, kv_width), BF),
            jax.ShapeDtypeStruct((draft, draft), F32),
            jax.ShapeDtypeStruct((requests * draft, LANES), F32),
        ),
        grid=(1,),
        in_specs=[scalars(), scalars(), scalars()]
        + [blocked(x) for x in (parents, INVERSE, queries, kv)],
        out_specs=(whole(),) * 5,
        scratch_shapes=[
            pltpu.VMEM(kv.shape, F32),
            pltpu.VMEM((n, LANES), F32),
            pltpu.VMEM((requests, draft, draft), F32),
        ],
        compiler_params=params(8),
        name="prelude",
    )(where, cache_len, path, parents, jnp.asarray(INVERSE), queries, kv)


def prepare_kernel(cache_ref, routes_ref, router_ref, out_ref, bias_ref, route_w_ref, kv_f):
    cells = out_ref.shape[2]
    kv_f[...] = cache_ref[0].astype(F32)
    for j in range(2 * PAIRS):
        out_ref[0, j] = kv_f[pl.ds(j, cells, stride=2 * PAIRS), :].astype(BF)

    @pl.when(pl.program_id(0) == 0)
    def _():
        experts = router_ref.shape[0]
        router = router_ref[...]
        high = router.astype(BF)
        route_w_ref[:experts, :] = high
        route_w_ref[experts:, :] = (router - high.astype(F32)).astype(BF)
        for d in range(routes_ref.shape[0]):
            chosen = routes_ref[d]
            expert = lax.broadcasted_iota(jnp.int32, (experts, chosen.shape[1]), 0)
            hit = expert == chosen[0:1, :]
            for k in range(1, chosen.shape[0]):
                hit = hit | (expert == chosen[k : k + 1, :])
            bias_ref[d] = jnp.where(hit, 0.0, NEG).T


def prepare(cache, routes, router):
    requests, span, _ = cache.shape
    cells = span // (2 * PAIRS)
    experts, width = router.shape
    blocks, top, n = routes.shape
    return pl.pallas_call(
        prepare_kernel,
        out_shape=(
            jax.ShapeDtypeStruct((requests, 2 * PAIRS, cells, LANES), BF),
            jax.ShapeDtypeStruct((blocks, n, experts), F32),
            jax.ShapeDtypeStruct((2 * experts, width), BF),
        ),
        grid=(requests,),
        in_specs=[
            pl.BlockSpec((1, span, LANES), lambda r: (r, 0, 0)),
            pl.BlockSpec((blocks, top, n), lambda r: (0, 0, 0)),
            pl.BlockSpec((experts, width), lambda r: (0, 0)),
        ],
        out_specs=(
            pl.BlockSpec((1, 2 * PAIRS, cells, LANES), lambda r: (r, 0, 0, 0)),
            pl.BlockSpec((blocks, n, experts), lambda r: (0, 0, 0)),
            pl.BlockSpec((2 * experts, width), lambda r: (0, 0)),
        ),
        scratch_shapes=[pltpu.VMEM((span, LANES), F32)],
        compiler_params=params(12),
        name="prepare",
    )(cache, routes, router)


def attend_kernel(
    step, near, where_ref, len_ref, pay_ref, kv_ref, key_ref, val_ref, anc_ref, pos_ref, out_ref
):
    draft = anc_ref.shape[0]
    n = key_ref.shape[0]
    cells = kv_ref.shape[2]
    me = where_ref[0]
    start = (me ^ step) * n
    request = start // draft
    key_start = me * cells
    place = pos_ref[pl.ds(pl.multiple_of(start, 8), n), :][:, :1]
    key_pos = (lane_index((n, cells)) + key_start).astype(F32)
    far_ok = (key_pos < len_ref[request].astype(F32)) & (
        (key_pos < SINKS) | (place - key_pos < WINDOW)
    )
    bias = jnp.where(far_ok, 0.0, NEG)
    bias = jnp.concatenate([bias] * (2 * GROUPS), axis=0)
    if near:
        own = me * n
        same = (own // draft) == request
        line = anc_ref[pl.ds(pl.multiple_of(start % draft, 8), n), :]
        if n != draft:
            pick = (
                lax.broadcasted_iota(jnp.int32, (draft, n), 0)
                == lax.broadcasted_iota(jnp.int32, (draft, n), 1) + own % draft
            ).astype(BF)
            line = jnp.dot(line.astype(BF), pick, preferred_element_type=F32)
        seen = jnp.where(same, line, 0.0)
        near_bias = jnp.where(seen > 0.5, 0.0, NEG)
        near_bias = jnp.concatenate([near_bias] * (2 * GROUPS), axis=0)
    low = lane_index((n, LANES)) < HD
    lane = lane_index((n, LANES))
    stats = jnp.zeros((n, LANES), F32)
    turn = (((1,), (1,)), ((), ()))
    factor = HD ** (-0.5) * LOG2E
    for b in range(PAIRS):
        keys = kv_ref[request, 2 * b]
        vals = kv_ref[request, 2 * b + 1]
        blocks = [
            pay_ref[:n, (GROUPS * b + i) * LANES : (GROUPS * b + i + 1) * LANES]
            for i in range(GROUPS)
        ]
        zero = jnp.zeros((n, LANES), BF)
        rows = jnp.concatenate(
            [jnp.where(low, x, zero) for x in blocks] + [jnp.where(low, zero, x) for x in blocks],
            axis=0,
        )
        scores = lax.dot_general(rows, keys, turn, preferred_element_type=F32) * factor + bias
        top = jnp.max(scores, axis=-1, keepdims=True)
        if near:
            near_scores = (
                lax.dot_general(
                    rows, key_ref[:, b * LANES : (b + 1) * LANES], turn, preferred_element_type=F32
                )
                * factor
                + near_bias
            )
            top = jnp.maximum(top, jnp.max(near_scores, axis=-1, keepdims=True))
        top = jnp.maximum(top, FLOOR)
        top = (top + jnp.abs(top) * (2.0**-7)).astype(BF).astype(F32)
        weights = jnp.exp2(scores - top)
        total = jnp.sum(weights, axis=-1, keepdims=True)
        blend = jnp.dot(weights.astype(BF), vals, preferred_element_type=F32)
        if near:
            near_weights = jnp.exp2(near_scores - top)
            total = total + jnp.sum(near_weights, axis=-1, keepdims=True)
            blend = blend + jnp.dot(
                near_weights.astype(BF),
                val_ref[:, b * LANES : (b + 1) * LANES],
                preferred_element_type=F32,
            )
        high = total.astype(BF).astype(F32)
        rest = total - high
        for i in range(GROUPS):
            first = slice(i * n, (i + 1) * n)
            second = slice((GROUPS + i) * n, (GROUPS + i + 1) * n)
            block = GROUPS * b + i
            out_ref[:, block * LANES : (block + 1) * LANES] = jnp.where(
                low, blend[first], blend[second]
            ).astype(BF)
            for part, rows_of in enumerate((first, second)):
                at = 2 * block + part
                stats = jnp.where(lane == at, top[rows_of], stats)
                stats = jnp.where(lane == QH + at, high[rows_of], stats)
                stats = jnp.where(lane == 2 * QH + at, rest[rows_of], stats)
    out_ref[:, QH * HD :] = stats.astype(BF)


def attend(step, near, where, cache_len, payload, cache, keys, vals, ancestry, pos):
    n = keys.shape[0]
    return pl.pallas_call(
        functools.partial(attend_kernel, step, near),
        out_shape=jax.ShapeDtypeStruct((n, QH * HD + LANES), BF),
        in_specs=[scalars(), scalars()] + [whole()] * 6,
        out_specs=whole(),
        compiler_params=params(12),
        name="attend",
    )(where, cache_len, payload, cache, keys, vals, ancestry, pos)


SPAN = 2 * GROUPS


def attend_split_kernel(
    step, near, count, where_ref, len_ref, pay_ref, kv_ref, key_ref, val_ref, anc_ref, pos_ref, *refs
):
    out_refs = refs[-count:]
    n = key_ref.shape[0]
    cells = kv_ref.shape[2]
    me = where_ref[0]
    start = (me ^ step) * n
    request = me ^ step
    place = pos_ref[pl.ds(pl.multiple_of(start, 8), n), :][:, :1]
    key_pos = (lane_index((n, cells)) + me * cells).astype(F32)
    far_ok = (key_pos < len_ref[request].astype(F32)) & (
        (key_pos < SINKS) | (place - key_pos < WINDOW)
    )
    bias = jnp.where(far_ok, 0.0, NEG)
    bias = jnp.concatenate([bias] * SPAN, axis=0)
    if near:
        near_bias = jnp.where(anc_ref[...] > 0.5, 0.0, NEG)
        near_bias = jnp.concatenate([near_bias] * SPAN, axis=0)
    lane = lane_index((n, LANES))
    low = lane < HD
    turn = (((1,), (1,)), ((), ()))
    factor = HD ** (-0.5) * LOG2E
    for j in range(count):
        b = me ^ j
        stats = jnp.zeros((n, LANES), F32) if near else out_refs[j][count * GROUPS].astype(F32)
        blocks = [
            pay_ref[:n, pl.ds(pl.multiple_of((GROUPS * b + i) * LANES, LANES), LANES)]
            for i in range(GROUPS)
        ]
        zero = jnp.zeros((n, LANES), BF)
        rows = jnp.concatenate(
            [jnp.where(low, x, zero) for x in blocks] + [jnp.where(low, zero, x) for x in blocks],
            axis=0,
        )
        scores = (
            lax.dot_general(rows, kv_ref[request, 2 * b], turn, preferred_element_type=F32) * factor
            + bias
        )
        top = jnp.max(scores, axis=-1, keepdims=True)
        if near:
            at_pair = pl.ds(pl.multiple_of(b * LANES, LANES), LANES)
            near_scores = (
                lax.dot_general(rows, key_ref[:, at_pair], turn, preferred_element_type=F32) * factor
                + near_bias
            )
            top = jnp.maximum(top, jnp.max(near_scores, axis=-1, keepdims=True))
        top = jnp.maximum(top, FLOOR)
        top = (top + jnp.abs(top) * (2.0**-7)).astype(BF).astype(F32)
        weights = jnp.exp2(scores - top)
        total = jnp.sum(weights, axis=-1, keepdims=True)
        blend = jnp.dot(weights.astype(BF), kv_ref[request, 2 * b + 1], preferred_element_type=F32)
        if near:
            near_weights = jnp.exp2(near_scores - top)
            total = total + jnp.sum(near_weights, axis=-1, keepdims=True)
            blend = blend + jnp.dot(
                near_weights.astype(BF), val_ref[:, at_pair], preferred_element_type=F32
            )
        high = total.astype(BF).astype(F32)
        rest = total - high
        for i in range(GROUPS):
            first = slice(i * n, (i + 1) * n)
            second = slice((GROUPS + i) * n, (GROUPS + i + 1) * n)
            out_refs[j][step * GROUPS + i] = jnp.where(low, blend[first], blend[second]).astype(BF)
            for part, rows_of in enumerate((first, second)):
                at = 3 * SPAN * step + 2 * i + part
                stats = jnp.where(lane == at, top[rows_of], stats)
                stats = jnp.where(lane == at + SPAN, high[rows_of], stats)
                stats = jnp.where(lane == at + 2 * SPAN, rest[rows_of], stats)
        out_refs[j][count * GROUPS] = stats.astype(BF)


def attend_split(step, count, where, cache_len, payload, cache, keys, vals, ancestry, pos, outs):
    n = keys.shape[0]
    shape = jax.ShapeDtypeStruct((count * GROUPS + 1, n, LANES), BF)
    return pl.pallas_call(
        functools.partial(attend_split_kernel, step, step == 0, count),
        out_shape=(shape,) * count,
        in_specs=[scalars(), scalars()] + [whole()] * (6 + len(outs)),
        out_specs=(whole(),) * count,
        input_output_aliases={8 + j: j for j in range(len(outs))},
        compiler_params=params(12),
        name="attend",
    )(where, cache_len, payload, cache, keys, vals, ancestry, pos, *outs)


def join_split_kernel(count, weight_ref, *refs):
    parts, out_refs, att = refs[:count], refs[count:-1], refs[-1]
    n = parts[0].shape[1]
    lane = lane_index((n, LANES))
    low = lane < HD
    shifts = [p[count * GROUPS].astype(F32) for p in parts]
    totals = [
        pltpu.roll(s, LANES - SPAN, axis=1) + pltpu.roll(s, LANES - 2 * SPAN, axis=1)
        for s in shifts
    ]
    for k in range(count):
        moves = [(LANES - 3 * SPAN * (j ^ k)) % LANES for j in range(count)]
        tops = [pltpu.roll(s, m, axis=1) if m else s for s, m in zip(shifts, moves)]
        sums = [pltpu.roll(s, m, axis=1) if m else s for s, m in zip(totals, moves)]
        top = functools.reduce(jnp.maximum, tops)
        scales = [jnp.exp2(t - top) for t in tops]
        inverse = 1.0 / functools.reduce(jnp.add, [a * b for a, b in zip(scales, sums)])
        scales = [scale * inverse for scale in scales]
        joined = []
        for i in range(GROUPS):
            acc = jnp.zeros((n, LANES), F32)
            for j in range(count):
                by = jnp.where(
                    low, scales[j][:, 2 * i : 2 * i + 1], scales[j][:, 2 * i + 1 : 2 * i + 2]
                )
                acc = acc + by * parts[j][(j ^ k) * GROUPS + i].astype(F32)
            joined.append(acc)
        turned = pltpu.roll(joined[1], HD, axis=1)
        back = (
            jnp.where(low, joined[0], turned),
            jnp.where(low, joined[2], joined[0]),
            jnp.where(low, turned, joined[2]),
        )
        for i in range(GROUPS):
            att[k * n : (k + 1) * n, i * LANES : (i + 1) * LANES] = back[i].astype(BF)
    for k in list(range(1, count)) + [0]:
        product = jnp.dot(att[k * n : (k + 1) * n, :], weight_ref[...], preferred_element_type=F32)
        out_refs[k][...] = product.astype(out_refs[k].dtype)


def join_split(weight, parts):
    count = len(parts)
    n = parts[0].shape[1]
    width = weight.shape[1]
    return pl.pallas_call(
        functools.partial(join_split_kernel, count),
        out_shape=tuple(
            jax.ShapeDtypeStruct((n, width), BF if k else F32) for k in range(count)
        ),
        in_specs=[whole()] * (1 + count),
        out_specs=(whole(),) * count,
        scratch_shapes=[pltpu.VMEM((count * n, weight.shape[0]), BF)],
        compiler_params=params(12),
        name="join",
    )(weight, *parts)


def norm_kernel(hidden_ref, gain_ref, own_ref, *refs):
    others, (mixed_ref, normed_ref) = refs[:-2], refs[-2:]
    mixed = hidden_ref[...].astype(F32) + own_ref[...]
    for other in others:
        mixed = mixed + other[...].astype(F32)
    mixed_ref[...] = mixed
    square = jnp.mean(mixed * mixed, axis=-1, keepdims=True)
    normed_ref[...] = (mixed * lax.rsqrt(square + 1e-06) * gain_ref[...]).astype(BF)


def norm(hidden_in, gain, own, others):
    return pl.pallas_call(
        norm_kernel,
        out_shape=(
            jax.ShapeDtypeStruct(hidden_in.shape, F32),
            jax.ShapeDtypeStruct(hidden_in.shape, BF),
        ),
        in_specs=[whole()] * (3 + len(others)),
        out_specs=(whole(), whole()),
        compiler_params=params(4),
        name="norm",
    )(hidden_in, gain, own, *others)


def join_kernel(count, where_ref, *refs):
    parts, rest = refs[:count], refs[count:]
    shares = 2 * count - 1
    pieces, rest = rest[:shares], rest[shares:]
    hidden_ref, gain_ref, mixed_ref, normed_ref, att, weight, sems = rest
    n = hidden_ref.shape[0]
    depth = pieces[0].shape[0]
    half = depth // CORES
    width = QH * HD
    me = where_ref[0]
    core = where_ref[1] % CORES
    starts = [me * depth]
    for k in range(1, count):
        starts += [(me ^ k) * depth + core * half, (me ^ k) * depth + (1 - core) * half]
    copies = []
    for j, (piece, start) in enumerate(zip(pieces, starts)):
        rows = weight.at[pl.ds(pl.multiple_of(start, 16), piece.shape[0]), :]
        copies.append(pltpu.make_async_copy(piece, rows, sems.at[j]))
        copies[-1].start()
    stats = [p[:, width:].astype(F32) for p in parts]
    top = stats[0]
    for s in stats[1:]:
        top = jnp.maximum(top, s)
    scales = [jnp.exp2(s - top) for s in stats]
    total = jnp.zeros((n, LANES), F32)
    for s, scale in zip(stats, scales):
        sums = pltpu.roll(s, LANES - QH, axis=1) + pltpu.roll(s, LANES - 2 * QH, axis=1)
        total = total + scale * sums
    inverse = 1.0 / total
    scales = [scale * inverse for scale in scales]
    low = lane_index((n, LANES)) < HD

    for b in range(PAIRS):
        joined = []
        for i in range(GROUPS):
            block = GROUPS * b + i
            acc = jnp.zeros((n, LANES), F32)
            for p, scale in zip(parts, scales):
                by = jnp.where(
                    low, scale[:, 2 * block : 2 * block + 1], scale[:, 2 * block + 1 : 2 * block + 2]
                )
                acc = acc + by * p[:, block * LANES : (block + 1) * LANES].astype(F32)
            joined.append(acc)
        turned = pltpu.roll(joined[1], HD, axis=1)
        back = (
            jnp.where(low, joined[0], turned),
            jnp.where(low, joined[2], joined[0]),
            jnp.where(low, turned, joined[2]),
        )
        for i in range(GROUPS):
            block = GROUPS * b + i
            att[:, block * LANES : (block + 1) * LANES] = back[i].astype(BF)
    for copy in copies:
        copy.wait()
    attended = jnp.dot(att[...], weight[...], preferred_element_type=F32)
    mixed = hidden_ref[...].astype(F32) + attended
    mixed_ref[...] = mixed
    square = jnp.mean(mixed * mixed, axis=-1, keepdims=True)
    normed_ref[...] = (mixed * lax.rsqrt(square + 1e-06) * gain_ref[...]).astype(BF)


def join(where, parts, pieces, hidden_in, gain):
    n, width = hidden_in.shape
    count = len(parts)
    inner = QH * HD
    return pl.pallas_call(
        functools.partial(join_kernel, count),
        out_shape=(
            jax.ShapeDtypeStruct((n, width), F32),
            jax.ShapeDtypeStruct((n, width), BF),
        ),
        in_specs=[scalars()]
        + [whole()] * count
        + [pl.BlockSpec(memory_space=pl.ANY)] * len(pieces)
        + [whole(), whole()],
        out_specs=(whole(), whole()),
        scratch_shapes=[
            pltpu.VMEM((n, inner), BF),
            pltpu.VMEM((inner, width), BF),
            pltpu.SemaphoreType.DMA((len(pieces),)),
        ],
        compiler_params=params(14),
        name="join",
    )(where, *parts, *pieces, hidden_in, gain)


def experts_kernel(
    step, where_ref, bias_ref, route_ref, wg, wu, wd, a_ref, b_ref, own_ref, other_ref
):
    n, width = a_ref.shape
    local = wg.shape[0]
    experts = bias_ref.shape[2]
    me = where_ref[1]
    x = jnp.concatenate([a_ref[...], b_ref[...]], axis=0)
    logits = lax.dot_general(
        x, route_ref[...], (((1,), (1,)), ((), ())), preferred_element_type=F32
    )
    logits = logits[:, :experts] + logits[:, experts:]
    first = CORES * step
    logits = logits + jnp.concatenate([bias_ref[me ^ first], bias_ref[me ^ (first + 1)]], axis=0)
    gates = jnp.exp(logits - jnp.max(logits, axis=-1, keepdims=True))
    gates = gates / jnp.sum(gates, axis=-1, keepdims=True)
    lane = lane_index(gates.shape)
    acc = None
    for e in range(local):
        gate_hidden = jnp.dot(x, wg[e], preferred_element_type=F32)
        up_hidden = jnp.dot(x, wu[e], preferred_element_type=F32)
        activated = (gate_hidden / (1.0 + jnp.exp(-gate_hidden)) * up_hidden).astype(BF)
        made = jnp.dot(activated, wd[e], preferred_element_type=F32).astype(BF).astype(F32)
        gate = jnp.sum(jnp.where(lane == me * local + e, gates, 0.0), axis=-1, keepdims=True)
        acc = gate * made if acc is None else acc + gate * made
    own_ref[...] = acc[:n]
    other_ref[...] = acc[n:].astype(BF)


def experts_part(step, where, bias, route, w_gate, w_up, w_down, a, b):
    n, width = a.shape
    return pl.pallas_call(
        functools.partial(experts_kernel, step),
        out_shape=(
            jax.ShapeDtypeStruct((n, width), F32),
            jax.ShapeDtypeStruct((n, width), BF),
        ),
        in_specs=[scalars()] + [whole()] * 7,
        out_specs=(whole(), whole()),
        compiler_params=params(12),
        name="experts",
    )(where, bias, route, w_gate, w_up, w_down, a, b)


def accepted_kernel(count, n, where_ref, *refs):
    out_ref = refs[count]
    requests = out_ref.shape[0]
    draft = count * n // requests
    out_ref[...] = jnp.zeros(out_ref.shape, out_ref.dtype)
    for k in range(count):
        request = (where_ref[0] ^ k) * n // draft
        out_ref[request] = out_ref[request] + refs[k][:, : out_ref.shape[2]]


def accepted(where, payloads, requests, entries, n):
    count = len(payloads)
    block = pl.BlockSpec((entries, payloads[0].shape[1]), lambda i: (n // entries, 0))
    return pl.pallas_call(
        functools.partial(accepted_kernel, count, n),
        out_shape=jax.ShapeDtypeStruct((requests, entries, 2 * KVH * HD), BF),
        grid=(1,),
        in_specs=[scalars()] + [block] * count,
        out_specs=pl.BlockSpec((requests, entries, 2 * KVH * HD), lambda i: (0, 0, 0)),
        compiler_params=params(4),
        name="accepted",
    )(where, *payloads)


def rows_by_lane_block(kv):
    lead, (tokens, two, width) = kv.shape[:-3], kv.shape[-3:]
    split = kv.reshape(*lead, tokens, two, width // LANES, LANES)
    return jnp.swapaxes(split, -3, -2).reshape(*lead, tokens * two * width // LANES, LANES)


def body(
    hidden_in, queries, draft_kv, cache_kv, cache_len, parents, path, routes,
    w_out, router, norm_gain, w_gate, w_up, w_down,
):
    tensor = lax.axis_size("tensor")
    data = lax.axis_size("dp")
    n = queries.shape[0]
    requests, draft = parents.shape
    where = jnp.stack([lax.axis_index("tensor"), lax.axis_index("dp")]).astype(jnp.int32)
    payload, keys, vals, ancestry, pos = prelude(
        where, cache_len, path, parents, queries, rows_by_lane_block(draft_kv)
    )
    cache = rows_by_lane_block(cache_kv)
    payloads = [payload] + [exchange(payload, "tensor", tensor, k) for k in range(1, tensor)]
    unpacked, bias, route = prepare(cache, jnp.swapaxes(routes, 1, 2), router.T)
    gain = norm_gain.reshape(1, -1)
    if n == draft and tensor == PAIRS:
        parts = ()
        for k in range(tensor):
            parts = attend_split(
                k, tensor, where, cache_len, payloads[k], unpacked, keys, vals, ancestry, pos, parts
            )
        parts = [parts[0]] + [exchange(parts[j], "tensor", tensor, j) for j in range(1, tensor)]
        products = join_split(w_out, parts)
        others = [exchange(products[k], "tensor", tensor, k) for k in range(1, tensor)]
        mixed, normed = norm(hidden_in, gain, products[0], others)
    else:
        half = w_out.shape[0] // CORES
        mine = lax.dynamic_slice_in_dim(w_out, lax.axis_index("dp") % CORES * half, half, 0)
        mine = lax.optimization_barrier((mine, *payloads[1:]))[0]
        fetched = [exchange(mine, "tensor", tensor, k) for k in range(1, tensor)]
        parts = []
        for k in range(tensor):
            near = k < max(1, draft // n)
            part = attend(k, near, where, cache_len, payloads[k], unpacked, keys, vals, ancestry, pos)
            parts.append(part if k == 0 else exchange(part, "tensor", tensor, k))
        pieces = [w_out]
        for piece in fetched:
            pieces += [piece, exchange(piece, "dp", data, 1)]
        mixed, normed = join(where, parts, pieces, hidden_in, gain)
    compacted = accepted(where, payloads, requests, path.shape[1], n)

    steps = data // CORES
    lines = {0: normed}
    reach = steps // 2
    while reach:
        for k in [k for k in lines if k % (2 * reach) == 0]:
            lines[k + reach] = exchange(lines[k], "dp", data, CORES * reach)
        reach //= 2
    total = mixed
    last = None
    for k in sorted(lines, key=lambda k: (bin(k).count("1"), k)):
        line = lines[k]
        if last is not None:
            line = lax.optimization_barrier((line, last))[0]
        twin = exchange(line, "dp", data, 1)
        own, other = experts_part(k, where, bias, route, w_gate, w_up, w_down, line, twin)
        last = own
        chip = own + exchange(other, "dp", data, 1).astype(F32)
        if k:
            chip = exchange(chip.astype(BF), "dp", data, CORES * k).astype(F32)
        total = total + chip
    return total.astype(BF), compacted


def solution(mesh):
    in_specs = (
        P(("dp", "tensor"), None),
        P(("dp", "tensor"), None),
        P(("dp", "tensor"), None, None),
        P("dp", "tensor", None, None),
        P("dp"),
        P("dp", None),
        P("dp", None),
        P(None, "tensor", None),
        P("tensor", None),
        P(),
        P(),
        P("dp", None, None),
        P("dp", None, None),
        P("dp", None, None),
    )
    out_specs = (P(("dp", "tensor"), None), P("dp", None, None))
    return jax.shard_map(body, mesh=mesh, in_specs=in_specs, out_specs=out_specs, check_vma=False)
```

```python
import functools

import jax
import jax.numpy as jnp
import numpy as np
from jax import lax
from jax.experimental import pallas as pl
from jax.experimental.pallas import tpu as pltpu
from jax.sharding import PartitionSpec as P

QH = 24
KVH = 8
HD = 64
TOP = 8
SINKS = 4
WINDOW = 1024

LANES = 128
PAIRS = KVH * HD // LANES
GROUPS = QH // KVH
CORES = 2
NEG = -1e30
FLOOR = -1e6
BF = jnp.bfloat16
F32 = jnp.float32
LOG2E = 1.4426950408889634
MIB = 1024 * 1024

INVERSE = [
    float(x)
    for x in (10000.0 ** (-2.0 * np.arange(HD // 2, dtype=np.float64) / HD)).astype(np.float32)
]


def params(mib):
    return pltpu.CompilerParams(vmem_limit_bytes=mib * MIB)


def whole():
    return pl.BlockSpec(memory_space=pltpu.VMEM)


def in_hbm():
    return pl.BlockSpec(memory_space=pltpu.HBM)


def fixed(x):
    return pltpu.with_memory_space_constraint(x, pltpu.HBM)


def cost(flops):
    return pl.CostEstimate(flops=int(flops), bytes_accessed=0, transcendentals=0)


def exchange(x, axis, size, step):
    return lax.ppermute(x, axis, [(i, i ^ step) for i in range(size)])


def lane_index(shape):
    return lax.broadcasted_iota(jnp.int32, shape, len(shape) - 1)


def prelude_kernel(
    len_hbm, path_hbm, par_hbm, q_hbm, kv_hbm,
    pay_ref, key_ref, val_ref, anc_ref, pos_ref, lim_ref,
    len_ref, path_ref, par_ref, q_ref, kv_ref, kv_f, anc_all, sems,
):
    copies = [
        pltpu.make_async_copy(src, dst, sems.at[j])
        for j, (src, dst) in enumerate(
            (
                (par_hbm, par_ref), (len_hbm, len_ref), (path_hbm, path_ref),
                (kv_hbm, kv_ref), (q_hbm, q_ref),
            )
        )
    ]
    for copy in copies:
        copy.start()
    for copy in copies[:3]:
        copy.wait()
    requests, draft = par_ref.shape
    n = q_ref.shape[0]
    own_start = lax.axis_index("tensor") * n
    request = own_start // draft
    offset = own_start % draft
    row = lax.broadcasted_iota(jnp.int32, (draft, draft), 0)
    col = lax.broadcasted_iota(jnp.int32, (draft, draft), 1)
    eye = (row == col).astype(F32)
    linked = [
        ((row == par_ref[r : r + 1, :]).astype(F32) + eye).T.astype(BF) for r in range(requests)
    ]
    for level in range((draft - 1).bit_length()):
        linked = [
            jnp.minimum(jnp.dot(m, m, preferred_element_type=F32), 1.0).astype(BF) for m in linked
        ]
    for r in range(requests):
        ancestry = linked[r].astype(F32)
        depth = jnp.sum(ancestry, axis=-1, keepdims=True) - 1.0
        place = depth + len_ref[r].astype(F32)
        pos_ref[r * draft : (r + 1) * draft, :] = jnp.broadcast_to(place, (draft, LANES))
        lim_ref[r] = jnp.full((8, LANES), len_ref[r].astype(F32))
        anc_all[r] = ancestry
    anc_ref[...] = anc_all[request]
    own = pl.multiple_of(own_start, 8)
    lane = lane_index((n, LANES))
    step = lane_index((8, LANES)) % (HD // 2)
    inverse = jnp.full(step.shape, INVERSE[0], F32)
    for k in range(1, HD // 2):
        inverse = jnp.where(step == k, INVERSE[k], inverse)
    angle = pos_ref[pl.ds(own, n), :] * inverse[:1, :]
    front = lane % HD < HD // 2
    cosine = jnp.cos(angle)
    sine = jnp.sin(angle)
    sine = jnp.where(front, -sine, sine)
    low = lane < HD

    def turned(x):
        partner = jnp.where(
            front, pltpu.roll(x, LANES - HD // 2, axis=1), pltpu.roll(x, HD // 2, axis=1)
        )
        return x * cosine + partner * sine

    copies[3].wait()
    kv_f[...] = kv_ref[...].astype(F32)
    slot = lax.broadcasted_iota(jnp.int32, (path_ref.shape[1], n), 0)
    token = lax.broadcasted_iota(jnp.int32, (path_ref.shape[1], n), 1) + offset
    wanted = jnp.full(slot.shape, -1, jnp.int32)
    for k in range(path_ref.shape[1]):
        wanted = jnp.where(slot == k, path_ref[request, k], wanted)
    chooser = (wanted == token).astype(BF)
    keys, vals = [], []
    for b in range(PAIRS):
        keys.append(turned(kv_f[pl.ds(2 * b, n, stride=2 * PAIRS), :]).astype(BF))
        vals.append(kv_f[pl.ds(2 * b + 1, n, stride=2 * PAIRS), :].astype(BF))
        key_ref[:, b * LANES : (b + 1) * LANES] = keys[b]
        val_ref[:, b * LANES : (b + 1) * LANES] = vals[b]
    copies[4].wait()
    packed = jnp.concatenate(keys + vals, axis=1)
    picked = jnp.dot(chooser, packed, preferred_element_type=F32).astype(BF)
    pay_ref[n:, : packed.shape[1]] = picked
    pay_ref[n:, packed.shape[1] :] = jnp.zeros(
        (path_ref.shape[1], pay_ref.shape[1] - packed.shape[1]), BF
    )
    for b in range(PAIRS):
        x0, x1, x2 = [
            turned(q_ref[:, (GROUPS * b + i) * LANES : (GROUPS * b + i + 1) * LANES].astype(F32))
            for i in range(GROUPS)
        ]
        y0 = jnp.where(low, x0, x1)
        y1 = jnp.where(low, pltpu.roll(x0, HD, axis=1), pltpu.roll(x2, HD, axis=1))
        y2 = jnp.where(low, x1, x2)
        for i, y in enumerate((y0, y1, y2)):
            pay_ref[:n, (GROUPS * b + i) * LANES : (GROUPS * b + i + 1) * LANES] = y.astype(BF)


def prelude(cache_len, path, parents, queries, kv):
    requests, draft = parents.shape
    n, width = queries.shape
    kv_width = KVH * HD
    return pl.pallas_call(
        prelude_kernel,
        out_shape=(
            jax.ShapeDtypeStruct((n + path.shape[1], width), BF),
            jax.ShapeDtypeStruct((n, kv_width), BF),
            jax.ShapeDtypeStruct((n, kv_width), BF),
            jax.ShapeDtypeStruct((draft, draft), F32),
            jax.ShapeDtypeStruct((requests * draft, LANES), F32),
            jax.ShapeDtypeStruct((requests, 8, LANES), F32),
        ),
        in_specs=[in_hbm()] * 5,
        out_specs=(whole(),) * 6,
        scratch_shapes=[
            pltpu.SMEM(cache_len.shape, jnp.int32),
            pltpu.SMEM(path.shape, jnp.int32),
            pltpu.VMEM(parents.shape, jnp.int32),
            pltpu.VMEM(queries.shape, BF),
            pltpu.VMEM(kv.shape, BF),
            pltpu.VMEM(kv.shape, F32),
            pltpu.VMEM((requests, draft, draft), F32),
            pltpu.SemaphoreType.DMA((5,)),
        ],
        compiler_params=params(8),
        cost_estimate=cost(1e7),
        name="prelude",
    )(*[fixed(x) for x in (cache_len, path, parents, queries, kv)])


def prepare_kernel(
    cache_hbm, routes_hbm, router_hbm, out_ref, bias_ref, route_w_ref,
    packed, kv_f, routes_ref, router_ref, sems,
):
    requests, _, cells, _ = out_ref.shape
    copies = [
        pltpu.make_async_copy(cache_hbm.at[r], packed.at[r], sems.at[r]) for r in range(requests)
    ]
    copies.append(pltpu.make_async_copy(routes_hbm, routes_ref, sems.at[requests]))
    copies.append(pltpu.make_async_copy(router_hbm, router_ref, sems.at[requests + 1]))
    for copy in copies:
        copy.start()
    for r in range(requests):
        copies[r].wait()
        kv_f[...] = packed[r].astype(F32)
        for j in range(2 * PAIRS):
            out_ref[r, j] = kv_f[pl.ds(j, cells, stride=2 * PAIRS), :].astype(BF)
    copies[requests].wait()
    copies[requests + 1].wait()
    experts = router_ref.shape[0]
    router = router_ref[...]
    high = router.astype(BF)
    route_w_ref[:experts, :] = high
    route_w_ref[experts:, :] = (router - high.astype(F32)).astype(BF)
    for d in range(routes_ref.shape[0]):
        chosen = routes_ref[d]
        expert = lax.broadcasted_iota(jnp.int32, (experts, chosen.shape[1]), 0)
        hit = expert == chosen[0:1, :]
        for k in range(1, chosen.shape[0]):
            hit = hit | (expert == chosen[k : k + 1, :])
        bias_ref[d] = jnp.where(hit, 0.0, NEG).T


def prepare(cache, routes, router):
    requests, span, _ = cache.shape
    cells = span // (2 * PAIRS)
    experts, width = router.shape
    blocks, top, n = routes.shape
    return pl.pallas_call(
        prepare_kernel,
        out_shape=(
            jax.ShapeDtypeStruct((requests, 2 * PAIRS, cells, LANES), BF),
            jax.ShapeDtypeStruct((blocks, n, experts), F32),
            jax.ShapeDtypeStruct((2 * experts, width), BF),
        ),
        in_specs=[in_hbm()] * 3,
        out_specs=(whole(),) * 3,
        scratch_shapes=[
            pltpu.VMEM(cache.shape, BF),
            pltpu.VMEM((span, LANES), F32),
            pltpu.VMEM(routes.shape, jnp.int32),
            pltpu.VMEM(router.shape, F32),
            pltpu.SemaphoreType.DMA((requests + 2,)),
        ],
        compiler_params=params(16),
        cost_estimate=cost(1e8),
        name="prepare",
    )(*[fixed(x) for x in (cache, routes, router)])


def attend_kernel(
    step, near, pay_ref, kv_ref, key_ref, val_ref, anc_ref, pos_ref, lim_ref, out_ref
):
    draft = anc_ref.shape[0]
    n = key_ref.shape[0]
    cells = kv_ref.shape[2]
    me = lax.axis_index("tensor")
    start = (me ^ step) * n
    request = start // draft
    key_start = me * cells
    place = pos_ref[pl.ds(pl.multiple_of(start, 8), n), :][:, :1]
    key_pos = (lane_index((n, cells)) + key_start).astype(F32)
    far_ok = (key_pos < lim_ref[request][:1, :1]) & (
        (key_pos < SINKS) | (place - key_pos < WINDOW)
    )
    bias = jnp.where(far_ok, 0.0, NEG)
    bias = jnp.concatenate([bias] * (2 * GROUPS), axis=0)
    if near:
        own = me * n
        same = (own // draft) == request
        line = anc_ref[pl.ds(pl.multiple_of(start % draft, 8), n), :]
        if n != draft:
            pick = (
                lax.broadcasted_iota(jnp.int32, (draft, n), 0)
                == lax.broadcasted_iota(jnp.int32, (draft, n), 1) + own % draft
            ).astype(BF)
            line = jnp.dot(line.astype(BF), pick, preferred_element_type=F32)
        seen = jnp.where(same, line, 0.0)
        near_bias = jnp.where(seen > 0.5, 0.0, NEG)
        near_bias = jnp.concatenate([near_bias] * (2 * GROUPS), axis=0)
    low = lane_index((n, LANES)) < HD
    lane = lane_index((n, LANES))
    stats = jnp.zeros((n, LANES), F32)
    turn = (((1,), (1,)), ((), ()))
    factor = HD ** (-0.5) * LOG2E
    for b in range(PAIRS):
        keys = kv_ref[request, 2 * b]
        vals = kv_ref[request, 2 * b + 1]
        blocks = [
            pay_ref[:n, (GROUPS * b + i) * LANES : (GROUPS * b + i + 1) * LANES]
            for i in range(GROUPS)
        ]
        zero = jnp.zeros((n, LANES), BF)
        rows = jnp.concatenate(
            [jnp.where(low, x, zero) for x in blocks] + [jnp.where(low, zero, x) for x in blocks],
            axis=0,
        )
        scores = lax.dot_general(rows, keys, turn, preferred_element_type=F32) * factor + bias
        top = jnp.max(scores, axis=-1, keepdims=True)
        if near:
            near_scores = (
                lax.dot_general(
                    rows, key_ref[:, b * LANES : (b + 1) * LANES], turn, preferred_element_type=F32
                )
                * factor
                + near_bias
            )
            top = jnp.maximum(top, jnp.max(near_scores, axis=-1, keepdims=True))
        top = jnp.maximum(top, FLOOR)
        top = (top + jnp.abs(top) * (2.0**-7)).astype(BF).astype(F32)
        weights = jnp.exp2(scores - top)
        total = jnp.sum(weights, axis=-1, keepdims=True)
        blend = jnp.dot(weights.astype(BF), vals, preferred_element_type=F32)
        if near:
            near_weights = jnp.exp2(near_scores - top)
            total = total + jnp.sum(near_weights, axis=-1, keepdims=True)
            blend = blend + jnp.dot(
                near_weights.astype(BF),
                val_ref[:, b * LANES : (b + 1) * LANES],
                preferred_element_type=F32,
            )
        high = total.astype(BF).astype(F32)
        rest = total - high
        for i in range(GROUPS):
            first = slice(i * n, (i + 1) * n)
            second = slice((GROUPS + i) * n, (GROUPS + i + 1) * n)
            block = GROUPS * b + i
            out_ref[:, block * LANES : (block + 1) * LANES] = jnp.where(
                low, blend[first], blend[second]
            ).astype(BF)
            for part, rows_of in enumerate((first, second)):
                at = 2 * block + part
                stats = jnp.where(lane == at, top[rows_of], stats)
                stats = jnp.where(lane == QH + at, high[rows_of], stats)
                stats = jnp.where(lane == 2 * QH + at, rest[rows_of], stats)
    out_ref[:, QH * HD :] = stats.astype(BF)


def attend(step, near, payload, cache, keys, vals, ancestry, pos, limit):
    n = keys.shape[0]
    return pl.pallas_call(
        functools.partial(attend_kernel, step, near),
        out_shape=jax.ShapeDtypeStruct((n, QH * HD + LANES), BF),
        in_specs=[whole()] * 7,
        out_specs=whole(),
        compiler_params=params(12),
        name="attend",
    )(payload, cache, keys, vals, ancestry, pos, limit)


SPAN = 2 * GROUPS


def attend_split_kernel(
    step, near, count, pay_ref, kv_ref, key_ref, val_ref, anc_ref, pos_ref, lim_ref, *refs
):
    out_refs = refs[-count:]
    n = key_ref.shape[0]
    cells = kv_ref.shape[2]
    me = lax.axis_index("tensor")
    start = (me ^ step) * n
    request = me ^ step
    place = pos_ref[pl.ds(pl.multiple_of(start, 8), n), :][:, :1]
    key_pos = (lane_index((n, cells)) + me * cells).astype(F32)
    far_ok = (key_pos < lim_ref[request][:1, :1]) & (
        (key_pos < SINKS) | (place - key_pos < WINDOW)
    )
    bias = jnp.where(far_ok, 0.0, NEG)
    bias = jnp.concatenate([bias] * SPAN, axis=0)
    if near:
        near_bias = jnp.where(anc_ref[...] > 0.5, 0.0, NEG)
        near_bias = jnp.concatenate([near_bias] * SPAN, axis=0)
    lane = lane_index((n, LANES))
    low = lane < HD
    turn = (((1,), (1,)), ((), ()))
    factor = HD ** (-0.5) * LOG2E
    for j in range(count):
        b = me ^ j
        stats = jnp.zeros((n, LANES), F32) if near else out_refs[j][count * GROUPS].astype(F32)
        blocks = [
            pay_ref[:n, pl.ds(pl.multiple_of((GROUPS * b + i) * LANES, LANES), LANES)]
            for i in range(GROUPS)
        ]
        zero = jnp.zeros((n, LANES), BF)
        rows = jnp.concatenate(
            [jnp.where(low, x, zero) for x in blocks] + [jnp.where(low, zero, x) for x in blocks],
            axis=0,
        )
        scores = (
            lax.dot_general(rows, kv_ref[request, 2 * b], turn, preferred_element_type=F32) * factor
            + bias
        )
        top = jnp.max(scores, axis=-1, keepdims=True)
        if near:
            at_pair = pl.ds(pl.multiple_of(b * LANES, LANES), LANES)
            near_scores = (
                lax.dot_general(rows, key_ref[:, at_pair], turn, preferred_element_type=F32) * factor
                + near_bias
            )
            top = jnp.maximum(top, jnp.max(near_scores, axis=-1, keepdims=True))
        top = jnp.maximum(top, FLOOR)
        top = (top + jnp.abs(top) * (2.0**-7)).astype(BF).astype(F32)
        weights = jnp.exp2(scores - top)
        total = jnp.sum(weights, axis=-1, keepdims=True)
        blend = jnp.dot(weights.astype(BF), kv_ref[request, 2 * b + 1], preferred_element_type=F32)
        if near:
            near_weights = jnp.exp2(near_scores - top)
            total = total + jnp.sum(near_weights, axis=-1, keepdims=True)
            blend = blend + jnp.dot(
                near_weights.astype(BF), val_ref[:, at_pair], preferred_element_type=F32
            )
        high = total.astype(BF).astype(F32)
        rest = total - high
        for i in range(GROUPS):
            first = slice(i * n, (i + 1) * n)
            second = slice((GROUPS + i) * n, (GROUPS + i + 1) * n)
            out_refs[j][step * GROUPS + i] = jnp.where(low, blend[first], blend[second]).astype(BF)
            for part, rows_of in enumerate((first, second)):
                at = 3 * SPAN * step + 2 * i + part
                stats = jnp.where(lane == at, top[rows_of], stats)
                stats = jnp.where(lane == at + SPAN, high[rows_of], stats)
                stats = jnp.where(lane == at + 2 * SPAN, rest[rows_of], stats)
        out_refs[j][count * GROUPS] = stats.astype(BF)


def attend_split(step, count, payload, cache, keys, vals, ancestry, pos, limit, outs):
    n = keys.shape[0]
    shape = jax.ShapeDtypeStruct((count * GROUPS + 1, n, LANES), BF)
    return pl.pallas_call(
        functools.partial(attend_split_kernel, step, step == 0, count),
        out_shape=(shape,) * count,
        in_specs=[whole()] * (7 + len(outs)),
        out_specs=(whole(),) * count,
        input_output_aliases={7 + j: j for j in range(len(outs))},
        compiler_params=params(12),
        cost_estimate=cost(4e8),
        name="attend",
    )(payload, cache, keys, vals, ancestry, pos, limit, *outs)


def join_split_kernel(count, weight_ref, *refs):
    parts, out_refs, att = refs[:count], refs[count:-1], refs[-1]
    n = parts[0].shape[1]
    lane = lane_index((n, LANES))
    low = lane < HD
    shifts = [p[count * GROUPS].astype(F32) for p in parts]
    totals = [
        pltpu.roll(s, LANES - SPAN, axis=1) + pltpu.roll(s, LANES - 2 * SPAN, axis=1)
        for s in shifts
    ]
    for k in range(count):
        moves = [(LANES - 3 * SPAN * (j ^ k)) % LANES for j in range(count)]
        tops = [pltpu.roll(s, m, axis=1) if m else s for s, m in zip(shifts, moves)]
        sums = [pltpu.roll(s, m, axis=1) if m else s for s, m in zip(totals, moves)]
        top = functools.reduce(jnp.maximum, tops)
        scales = [jnp.exp2(t - top) for t in tops]
        inverse = 1.0 / functools.reduce(jnp.add, [a * b for a, b in zip(scales, sums)])
        scales = [scale * inverse for scale in scales]
        joined = []
        for i in range(GROUPS):
            acc = jnp.zeros((n, LANES), F32)
            for j in range(count):
                by = jnp.where(
                    low, scales[j][:, 2 * i : 2 * i + 1], scales[j][:, 2 * i + 1 : 2 * i + 2]
                )
                acc = acc + by * parts[j][(j ^ k) * GROUPS + i].astype(F32)
            joined.append(acc)
        turned = pltpu.roll(joined[1], HD, axis=1)
        back = (
            jnp.where(low, joined[0], turned),
            jnp.where(low, joined[2], joined[0]),
            jnp.where(low, turned, joined[2]),
        )
        for i in range(GROUPS):
            att[k * n : (k + 1) * n, i * LANES : (i + 1) * LANES] = back[i].astype(BF)
    for k in list(range(1, count)) + [0]:
        product = jnp.dot(att[k * n : (k + 1) * n, :], weight_ref[...], preferred_element_type=F32)
        out_refs[k][...] = product.astype(out_refs[k].dtype)


def join_split(weight, parts):
    count = len(parts)
    n = parts[0].shape[1]
    width = weight.shape[1]
    return pl.pallas_call(
        functools.partial(join_split_kernel, count),
        out_shape=tuple(
            jax.ShapeDtypeStruct((n, width), BF if k else F32) for k in range(count)
        ),
        in_specs=[whole()] * (1 + count),
        out_specs=(whole(),) * count,
        scratch_shapes=[pltpu.VMEM((count * n, weight.shape[0]), BF)],
        compiler_params=params(12),
        cost_estimate=cost(4e8),
        name="join",
    )(weight, *parts)


def norm_kernel(hidden_ref, gain_ref, own_ref, *refs):
    others, (mixed_ref, normed_ref) = refs[:-2], refs[-2:]
    mixed = hidden_ref[...].astype(F32) + own_ref[...]
    for other in others:
        mixed = mixed + other[...].astype(F32)
    mixed_ref[...] = mixed
    square = jnp.mean(mixed * mixed, axis=-1, keepdims=True)
    normed_ref[...] = (mixed * lax.rsqrt(square + 1e-06) * gain_ref[...]).astype(BF)


def norm(hidden_in, gain, own, others):
    return pl.pallas_call(
        norm_kernel,
        out_shape=(
            jax.ShapeDtypeStruct(hidden_in.shape, F32),
            jax.ShapeDtypeStruct(hidden_in.shape, BF),
        ),
        in_specs=[whole()] * (3 + len(others)),
        out_specs=(whole(), whole()),
        compiler_params=params(4),
        cost_estimate=cost(1e6),
        name="norm",
    )(hidden_in, gain, own, *others)


def join_kernel(count, *refs):
    parts, rest = refs[:count], refs[count:]
    shares = 2 * count - 1
    pieces, rest = rest[:shares], rest[shares:]
    hidden_ref, gain_ref, mixed_ref, normed_ref, att, weight, sems = rest
    n = hidden_ref.shape[0]
    depth = pieces[0].shape[0]
    half = depth // CORES
    width = QH * HD
    me = lax.axis_index("tensor")
    core = lax.axis_index("dp") % CORES
    starts = [me * depth]
    for k in range(1, count):
        starts += [(me ^ k) * depth + core * half, (me ^ k) * depth + (1 - core) * half]
    copies = []
    for j, (piece, start) in enumerate(zip(pieces, starts)):
        rows = weight.at[pl.ds(pl.multiple_of(start, 16), piece.shape[0]), :]
        copies.append(pltpu.make_async_copy(piece, rows, sems.at[j]))
        copies[-1].start()
    stats = [p[:, width:].astype(F32) for p in parts]
    top = stats[0]
    for s in stats[1:]:
        top = jnp.maximum(top, s)
    scales = [jnp.exp2(s - top) for s in stats]
    total = jnp.zeros((n, LANES), F32)
    for s, scale in zip(stats, scales):
        sums = pltpu.roll(s, LANES - QH, axis=1) + pltpu.roll(s, LANES - 2 * QH, axis=1)
        total = total + scale * sums
    inverse = 1.0 / total
    scales = [scale * inverse for scale in scales]
    low = lane_index((n, LANES)) < HD

    for b in range(PAIRS):
        joined = []
        for i in range(GROUPS):
            block = GROUPS * b + i
            acc = jnp.zeros((n, LANES), F32)
            for p, scale in zip(parts, scales):
                by = jnp.where(
                    low, scale[:, 2 * block : 2 * block + 1], scale[:, 2 * block + 1 : 2 * block + 2]
                )
                acc = acc + by * p[:, block * LANES : (block + 1) * LANES].astype(F32)
            joined.append(acc)
        turned = pltpu.roll(joined[1], HD, axis=1)
        back = (
            jnp.where(low, joined[0], turned),
            jnp.where(low, joined[2], joined[0]),
            jnp.where(low, turned, joined[2]),
        )
        for i in range(GROUPS):
            block = GROUPS * b + i
            att[:, block * LANES : (block + 1) * LANES] = back[i].astype(BF)
    for copy in copies:
        copy.wait()
    attended = jnp.dot(att[...], weight[...], preferred_element_type=F32)
    mixed = hidden_ref[...].astype(F32) + attended
    mixed_ref[...] = mixed
    square = jnp.mean(mixed * mixed, axis=-1, keepdims=True)
    normed_ref[...] = (mixed * lax.rsqrt(square + 1e-06) * gain_ref[...]).astype(BF)


def join(parts, pieces, hidden_in, gain):
    n, width = hidden_in.shape
    count = len(parts)
    inner = QH * HD
    return pl.pallas_call(
        functools.partial(join_kernel, count),
        out_shape=(
            jax.ShapeDtypeStruct((n, width), F32),
            jax.ShapeDtypeStruct((n, width), BF),
        ),
        in_specs=[whole()] * count
        + [pl.BlockSpec(memory_space=pl.ANY)] * len(pieces)
        + [whole(), whole()],
        out_specs=(whole(), whole()),
        scratch_shapes=[
            pltpu.VMEM((n, inner), BF),
            pltpu.VMEM((inner, width), BF),
            pltpu.SemaphoreType.DMA((len(pieces),)),
        ],
        compiler_params=params(14),
        name="join",
    )(*parts, *pieces, hidden_in, gain)


def experts_kernel(
    step, bias_ref, route_ref, wg, wu, wd, a_ref, b_ref, own_ref, other_ref
):
    n, width = a_ref.shape
    local = wg.shape[0]
    experts = bias_ref.shape[2]
    me = lax.axis_index("dp")
    x = jnp.concatenate([a_ref[...], b_ref[...]], axis=0)
    logits = lax.dot_general(
        x, route_ref[...], (((1,), (1,)), ((), ())), preferred_element_type=F32
    )
    logits = logits[:, :experts] + logits[:, experts:]
    first = CORES * step
    logits = logits + jnp.concatenate([bias_ref[me ^ first], bias_ref[me ^ (first + 1)]], axis=0)
    gates = jnp.exp(logits - jnp.max(logits, axis=-1, keepdims=True))
    gates = gates / jnp.sum(gates, axis=-1, keepdims=True)
    lane = lane_index(gates.shape)
    acc = None
    for e in range(local):
        gate_hidden = jnp.dot(x, wg[e], preferred_element_type=F32)
        up_hidden = jnp.dot(x, wu[e], preferred_element_type=F32)
        activated = (gate_hidden / (1.0 + jnp.exp(-gate_hidden)) * up_hidden).astype(BF)
        made = jnp.dot(activated, wd[e], preferred_element_type=F32).astype(BF).astype(F32)
        gate = jnp.sum(jnp.where(lane == me * local + e, gates, 0.0), axis=-1, keepdims=True)
        acc = gate * made if acc is None else acc + gate * made
    own_ref[...] = acc[:n]
    other_ref[...] = acc[n:].astype(BF)


def experts_part(step, bias, route, w_gate, w_up, w_down, a, b):
    n, width = a.shape
    return pl.pallas_call(
        functools.partial(experts_kernel, step),
        out_shape=(
            jax.ShapeDtypeStruct((n, width), F32),
            jax.ShapeDtypeStruct((n, width), BF),
        ),
        in_specs=[whole()] * 7,
        out_specs=(whole(), whole()),
        compiler_params=params(12),
        cost_estimate=cost(12e8),
        name="experts",
    )(bias, route, w_gate, w_up, w_down, a, b)


def accepted_kernel(count, n, *refs):
    out_ref = refs[count]
    requests = out_ref.shape[0]
    draft = count * n // requests
    out_ref[...] = jnp.zeros(out_ref.shape, out_ref.dtype)
    for k in range(count):
        request = (lax.axis_index("tensor") ^ k) * n // draft
        out_ref[request] = out_ref[request] + refs[k][:, : out_ref.shape[2]]


def accepted(payloads, requests, entries, n):
    count = len(payloads)
    block = pl.BlockSpec((entries, payloads[0].shape[1]), lambda i: (n // entries, 0))
    return pl.pallas_call(
        functools.partial(accepted_kernel, count, n),
        out_shape=jax.ShapeDtypeStruct((requests, entries, 2 * KVH * HD), BF),
        grid=(1,),
        in_specs=[block] * count,
        out_specs=pl.BlockSpec((requests, entries, 2 * KVH * HD), lambda i: (0, 0, 0)),
        compiler_params=params(4),
        cost_estimate=cost(1e6),
        name="accepted",
    )(*payloads)


def rows_by_lane_block(kv):
    lead, (tokens, two, width) = kv.shape[:-3], kv.shape[-3:]
    split = kv.reshape(*lead, tokens, two, width // LANES, LANES)
    return jnp.swapaxes(split, -3, -2).reshape(*lead, tokens * two * width // LANES, LANES)


def body(
    hidden_in, queries, draft_kv, cache_kv, cache_len, parents, path, routes,
    w_out, router, norm_gain, w_gate, w_up, w_down,
):
    tensor = lax.axis_size("tensor")
    data = lax.axis_size("dp")
    n = queries.shape[0]
    requests, draft = parents.shape
    payload, keys, vals, ancestry, pos, limit = prelude(
        cache_len, path, parents, queries, rows_by_lane_block(draft_kv)
    )
    cache = rows_by_lane_block(cache_kv)
    payloads = [payload] + [exchange(payload, "tensor", tensor, k) for k in range(1, tensor)]
    unpacked, bias, route = prepare(cache, jnp.swapaxes(routes, 1, 2), router.T)
    gain = norm_gain.reshape(1, -1)
    if n == draft and tensor == PAIRS:
        parts = ()
        for k in range(tensor):
            parts = attend_split(
                k, tensor, payloads[k], unpacked, keys, vals, ancestry, pos, limit, parts
            )
        parts = [parts[0]] + [exchange(parts[j], "tensor", tensor, j) for j in range(1, tensor)]
        products = join_split(w_out, parts)
        others = [exchange(products[k], "tensor", tensor, k) for k in range(1, tensor)]
        mixed, normed = norm(hidden_in, gain, products[0], others)
    else:
        half = w_out.shape[0] // CORES
        mine = lax.dynamic_slice_in_dim(w_out, lax.axis_index("dp") % CORES * half, half, 0)
        mine = lax.optimization_barrier((mine, *payloads[1:]))[0]
        fetched = [exchange(mine, "tensor", tensor, k) for k in range(1, tensor)]
        parts = []
        for k in range(tensor):
            near = k < max(1, draft // n)
            part = attend(k, near, payloads[k], unpacked, keys, vals, ancestry, pos, limit)
            parts.append(part if k == 0 else exchange(part, "tensor", tensor, k))
        pieces = [w_out]
        for piece in fetched:
            pieces += [piece, exchange(piece, "dp", data, 1)]
        mixed, normed = join(parts, pieces, hidden_in, gain)
    compacted = accepted(payloads, requests, path.shape[1], n)

    steps = data // CORES
    lines = {0: normed}
    reach = steps // 2
    while reach:
        for k in [k for k in lines if k % (2 * reach) == 0]:
            lines[k + reach] = exchange(lines[k], "dp", data, CORES * reach)
        reach //= 2
    single = [k for k in lines if k and k & (k - 1) == 0]
    total = mixed
    last = None
    for k in sorted(lines, key=lambda k: (bin(k).count("1"), -k)):
        if k == max(single) or (k and k not in single):
            names = single if k in single else [k]
            tied = lax.optimization_barrier([lines[name] for name in names] + [last])
            lines.update(zip(names, tied))
        line = lines[k]
        twin = exchange(line, "dp", data, 1)
        own, other = experts_part(k, bias, route, w_gate, w_up, w_down, line, twin)
        last = own
        chip = own + exchange(other, "dp", data, 1).astype(F32)
        if k:
            chip = exchange(chip.astype(BF), "dp", data, CORES * k).astype(F32)
        total = total + chip
    return total.astype(BF), compacted


def solution(mesh):
    in_specs = (
        P(("dp", "tensor"), None),
        P(("dp", "tensor"), None),
        P(("dp", "tensor"), None, None),
        P("dp", "tensor", None, None),
        P("dp"),
        P("dp", None),
        P("dp", None),
        P(None, "tensor", None),
        P("tensor", None),
        P(),
        P(),
        P("dp", None, None),
        P("dp", None, None),
        P("dp", None, None),
    )
    out_specs = (P(("dp", "tensor"), None), P("dp", None, None))
    return jax.shard_map(body, mesh=mesh, in_specs=in_specs, out_specs=out_specs, check_vma=False)
```

```python
import functools

import jax
import jax.numpy as jnp
import numpy as np
from jax import lax
from jax.experimental import pallas as pl
from jax.experimental.pallas import tpu as pltpu
from jax.sharding import PartitionSpec as P

QH = 24
KVH = 8
HD = 64
TOP = 8
SINKS = 4
WINDOW = 1024

LANES = 128
PAIRS = KVH * HD // LANES
GROUPS = QH // KVH
CORES = 2
NEG = -1e30
FLOOR = -1e6
BF = jnp.bfloat16
F32 = jnp.float32
LOG2E = 1.4426950408889634
MIB = 1024 * 1024

INVERSE = [
    float(x)
    for x in (10000.0 ** (-2.0 * np.arange(HD // 2, dtype=np.float64) / HD)).astype(np.float32)
]


def params(mib):
    return pltpu.CompilerParams(vmem_limit_bytes=mib * MIB)


def whole():
    return pl.BlockSpec(memory_space=pltpu.VMEM)


def in_hbm():
    return pl.BlockSpec(memory_space=pltpu.HBM)


def fixed(x):
    return pltpu.with_memory_space_constraint(x, pltpu.HBM)


def cost(flops):
    return pl.CostEstimate(flops=int(flops), bytes_accessed=0, transcendentals=0)


def exchange(x, axis, size, step):
    return lax.ppermute(x, axis, [(i, i ^ step) for i in range(size)])


def lane_index(shape):
    return lax.broadcasted_iota(jnp.int32, shape, len(shape) - 1)


def prelude_kernel(
    len_hbm, path_hbm, par_hbm, q_hbm, kv_hbm, cache_hbm,
    pay_ref, key_ref, val_ref, anc_ref, pos_ref, lim_ref, packed_ref,
    len_ref, path_ref, par_ref, q_ref, kv_ref, kv_f, anc_all, sems,
):
    copies = [
        pltpu.make_async_copy(src, dst, sems.at[j])
        for j, (src, dst) in enumerate(
            (
                (par_hbm, par_ref), (len_hbm, len_ref), (path_hbm, path_ref),
                (kv_hbm, kv_ref), (q_hbm, q_ref), (cache_hbm, packed_ref),
            )
        )
    ]
    for copy in copies:
        copy.start()
    for copy in copies[:3]:
        copy.wait()
    requests, draft = par_ref.shape
    n = q_ref.shape[0]
    own_start = lax.axis_index("tensor") * n
    request = own_start // draft
    offset = own_start % draft
    row = lax.broadcasted_iota(jnp.int32, (draft, draft), 0)
    col = lax.broadcasted_iota(jnp.int32, (draft, draft), 1)
    eye = (row == col).astype(F32)
    linked = [
        ((row == par_ref[r : r + 1, :]).astype(F32) + eye).T.astype(BF) for r in range(requests)
    ]
    for level in range((draft - 1).bit_length()):
        linked = [
            jnp.minimum(jnp.dot(m, m, preferred_element_type=F32), 1.0).astype(BF) for m in linked
        ]
    for r in range(requests):
        ancestry = linked[r].astype(F32)
        depth = jnp.sum(ancestry, axis=-1, keepdims=True) - 1.0
        place = depth + len_ref[r].astype(F32)
        pos_ref[r * draft : (r + 1) * draft, :] = jnp.broadcast_to(place, (draft, LANES))
        lim_ref[r] = jnp.full((8, LANES), len_ref[r].astype(F32))
        anc_all[r] = ancestry
    anc_ref[...] = anc_all[request]
    own = pl.multiple_of(own_start, 8)
    lane = lane_index((n, LANES))
    step = lane_index((8, LANES)) % (HD // 2)
    inverse = jnp.full(step.shape, INVERSE[0], F32)
    for k in range(1, HD // 2):
        inverse = jnp.where(step == k, INVERSE[k], inverse)
    angle = pos_ref[pl.ds(own, n), :] * inverse[:1, :]
    front = lane % HD < HD // 2
    cosine = jnp.cos(angle)
    sine = jnp.sin(angle)
    sine = jnp.where(front, -sine, sine)
    low = lane < HD

    def turned(x):
        partner = jnp.where(
            front, pltpu.roll(x, LANES - HD // 2, axis=1), pltpu.roll(x, HD // 2, axis=1)
        )
        return x * cosine + partner * sine

    copies[3].wait()
    kv_f[...] = kv_ref[...].astype(F32)
    slot = lax.broadcasted_iota(jnp.int32, (path_ref.shape[1], n), 0)
    token = lax.broadcasted_iota(jnp.int32, (path_ref.shape[1], n), 1) + offset
    wanted = jnp.full(slot.shape, -1, jnp.int32)
    for k in range(path_ref.shape[1]):
        wanted = jnp.where(slot == k, path_ref[request, k], wanted)
    chooser = (wanted == token).astype(BF)
    keys, vals = [], []
    for b in range(PAIRS):
        keys.append(turned(kv_f[pl.ds(2 * b, n, stride=2 * PAIRS), :]).astype(BF))
        vals.append(kv_f[pl.ds(2 * b + 1, n, stride=2 * PAIRS), :].astype(BF))
        key_ref[:, b * LANES : (b + 1) * LANES] = keys[b]
        val_ref[:, b * LANES : (b + 1) * LANES] = vals[b]
    copies[4].wait()
    packed = jnp.concatenate(keys + vals, axis=1)
    picked = jnp.dot(chooser, packed, preferred_element_type=F32).astype(BF)
    pay_ref[n:, : packed.shape[1]] = picked
    pay_ref[n:, packed.shape[1] :] = jnp.zeros(
        (path_ref.shape[1], pay_ref.shape[1] - packed.shape[1]), BF
    )
    for b in range(PAIRS):
        x0, x1, x2 = [
            turned(q_ref[:, (GROUPS * b + i) * LANES : (GROUPS * b + i + 1) * LANES].astype(F32))
            for i in range(GROUPS)
        ]
        y0 = jnp.where(low, x0, x1)
        y1 = jnp.where(low, pltpu.roll(x0, HD, axis=1), pltpu.roll(x2, HD, axis=1))
        y2 = jnp.where(low, x1, x2)
        for i, y in enumerate((y0, y1, y2)):
            pay_ref[:n, (GROUPS * b + i) * LANES : (GROUPS * b + i + 1) * LANES] = y.astype(BF)
    copies[5].wait()


def prelude(cache_len, path, parents, queries, kv, cache):
    requests, draft = parents.shape
    n, width = queries.shape
    kv_width = KVH * HD
    return pl.pallas_call(
        prelude_kernel,
        out_shape=(
            jax.ShapeDtypeStruct((n + path.shape[1], width), BF),
            jax.ShapeDtypeStruct((n, kv_width), BF),
            jax.ShapeDtypeStruct((n, kv_width), BF),
            jax.ShapeDtypeStruct((draft, draft), F32),
            jax.ShapeDtypeStruct((requests * draft, LANES), F32),
            jax.ShapeDtypeStruct((requests, 8, LANES), F32),
            jax.ShapeDtypeStruct(cache.shape, BF),
        ),
        in_specs=[in_hbm()] * 6,
        out_specs=(whole(),) * 7,
        scratch_shapes=[
            pltpu.SMEM(cache_len.shape, jnp.int32),
            pltpu.SMEM(path.shape, jnp.int32),
            pltpu.VMEM(parents.shape, jnp.int32),
            pltpu.VMEM(queries.shape, BF),
            pltpu.VMEM(kv.shape, BF),
            pltpu.VMEM(kv.shape, F32),
            pltpu.VMEM((requests, draft, draft), F32),
            pltpu.SemaphoreType.DMA((6,)),
        ],
        compiler_params=params(8),
        cost_estimate=cost(1e7),
        name="prelude",
    )(*[fixed(x) for x in (cache_len, path, parents, queries, kv, cache)])


def unpack_kernel(packed_ref, out_ref, kv_f):
    requests, _, cells, _ = out_ref.shape
    for r in range(requests):
        kv_f[r % 2] = packed_ref[r].astype(F32)
        for j in range(2 * PAIRS):
            out_ref[r, j] = kv_f[r % 2, pl.ds(j, cells, stride=2 * PAIRS), :].astype(BF)


def unpack(packed):
    requests, span, _ = packed.shape
    return pl.pallas_call(
        unpack_kernel,
        out_shape=jax.ShapeDtypeStruct(
            (requests, 2 * PAIRS, span // (2 * PAIRS), LANES), BF
        ),
        in_specs=[whole()],
        out_specs=whole(),
        scratch_shapes=[pltpu.VMEM((2, span, LANES), F32)],
        compiler_params=params(8),
        cost_estimate=cost(1e8),
        name="unpack",
    )(packed)


def routing_kernel(routes_hbm, router_hbm, bias_ref, route_w_ref, routes_ref, router_ref, sems):
    copies = [
        pltpu.make_async_copy(routes_hbm, routes_ref, sems.at[0]),
        pltpu.make_async_copy(router_hbm, router_ref, sems.at[1]),
    ]
    for copy in copies:
        copy.start()
    for copy in copies:
        copy.wait()
    experts = router_ref.shape[0]
    router = router_ref[...]
    high = router.astype(BF)
    route_w_ref[:experts, :] = high
    route_w_ref[experts:, :] = (router - high.astype(F32)).astype(BF)
    for d in range(routes_ref.shape[0]):
        chosen = routes_ref[d]
        expert = lax.broadcasted_iota(jnp.int32, (experts, chosen.shape[1]), 0)
        hit = expert == chosen[0:1, :]
        for k in range(1, chosen.shape[0]):
            hit = hit | (expert == chosen[k : k + 1, :])
        bias_ref[d] = jnp.where(hit, 0.0, NEG).T


def routing(routes, router):
    experts, width = router.shape
    blocks, top, n = routes.shape
    return pl.pallas_call(
        routing_kernel,
        out_shape=(
            jax.ShapeDtypeStruct((blocks, n, experts), F32),
            jax.ShapeDtypeStruct((2 * experts, width), BF),
        ),
        in_specs=[in_hbm()] * 2,
        out_specs=(whole(),) * 2,
        scratch_shapes=[
            pltpu.VMEM(routes.shape, jnp.int32),
            pltpu.VMEM(router.shape, F32),
            pltpu.SemaphoreType.DMA((2,)),
        ],
        compiler_params=params(8),
        cost_estimate=cost(1e6),
        name="routing",
    )(fixed(routes), fixed(router))


def attend_kernel(
    step, near, pay_ref, kv_ref, key_ref, val_ref, anc_ref, pos_ref, lim_ref, out_ref
):
    draft = anc_ref.shape[0]
    n = key_ref.shape[0]
    cells = kv_ref.shape[2]
    me = lax.axis_index("tensor")
    start = (me ^ step) * n
    request = start // draft
    key_start = me * cells
    place = pos_ref[pl.ds(pl.multiple_of(start, 8), n), :][:, :1]
    key_pos = (lane_index((n, cells)) + key_start).astype(F32)
    far_ok = (key_pos < lim_ref[request][:1, :1]) & (
        (key_pos < SINKS) | (place - key_pos < WINDOW)
    )
    bias = jnp.where(far_ok, 0.0, NEG)
    bias = jnp.concatenate([bias] * (2 * GROUPS), axis=0)
    if near:
        own = me * n
        same = (own // draft) == request
        line = anc_ref[pl.ds(pl.multiple_of(start % draft, 8), n), :]
        if n != draft:
            pick = (
                lax.broadcasted_iota(jnp.int32, (draft, n), 0)
                == lax.broadcasted_iota(jnp.int32, (draft, n), 1) + own % draft
            ).astype(BF)
            line = jnp.dot(line.astype(BF), pick, preferred_element_type=F32)
        seen = jnp.where(same, line, 0.0)
        near_bias = jnp.where(seen > 0.5, 0.0, NEG)
        near_bias = jnp.concatenate([near_bias] * (2 * GROUPS), axis=0)
    low = lane_index((n, LANES)) < HD
    lane = lane_index((n, LANES))
    stats = jnp.zeros((n, LANES), F32)
    turn = (((1,), (1,)), ((), ()))
    factor = HD ** (-0.5) * LOG2E
    for b in range(PAIRS):
        keys = kv_ref[request, 2 * b]
        vals = kv_ref[request, 2 * b + 1]
        blocks = [
            pay_ref[:n, (GROUPS * b + i) * LANES : (GROUPS * b + i + 1) * LANES]
            for i in range(GROUPS)
        ]
        zero = jnp.zeros((n, LANES), BF)
        rows = jnp.concatenate(
            [jnp.where(low, x, zero) for x in blocks] + [jnp.where(low, zero, x) for x in blocks],
            axis=0,
        )
        scores = lax.dot_general(rows, keys, turn, preferred_element_type=F32) * factor + bias
        top = jnp.max(scores, axis=-1, keepdims=True)
        if near:
            near_scores = (
                lax.dot_general(
                    rows, key_ref[:, b * LANES : (b + 1) * LANES], turn, preferred_element_type=F32
                )
                * factor
                + near_bias
            )
            top = jnp.maximum(top, jnp.max(near_scores, axis=-1, keepdims=True))
        top = jnp.maximum(top, FLOOR)
        top = (top + jnp.abs(top) * (2.0**-7)).astype(BF).astype(F32)
        weights = jnp.exp2(scores - top)
        total = jnp.sum(weights, axis=-1, keepdims=True)
        blend = jnp.dot(weights.astype(BF), vals, preferred_element_type=F32)
        if near:
            near_weights = jnp.exp2(near_scores - top)
            total = total + jnp.sum(near_weights, axis=-1, keepdims=True)
            blend = blend + jnp.dot(
                near_weights.astype(BF),
                val_ref[:, b * LANES : (b + 1) * LANES],
                preferred_element_type=F32,
            )
        high = total.astype(BF).astype(F32)
        rest = total - high
        for i in range(GROUPS):
            first = slice(i * n, (i + 1) * n)
            second = slice((GROUPS + i) * n, (GROUPS + i + 1) * n)
            block = GROUPS * b + i
            out_ref[:, block * LANES : (block + 1) * LANES] = jnp.where(
                low, blend[first], blend[second]
            ).astype(BF)
            for part, rows_of in enumerate((first, second)):
                at = 2 * block + part
                stats = jnp.where(lane == at, top[rows_of], stats)
                stats = jnp.where(lane == QH + at, high[rows_of], stats)
                stats = jnp.where(lane == 2 * QH + at, rest[rows_of], stats)
    out_ref[:, QH * HD :] = stats.astype(BF)


def attend(step, near, payload, cache, keys, vals, ancestry, pos, limit):
    n = keys.shape[0]
    return pl.pallas_call(
        functools.partial(attend_kernel, step, near),
        out_shape=jax.ShapeDtypeStruct((n, QH * HD + LANES), BF),
        in_specs=[whole()] * 7,
        out_specs=whole(),
        compiler_params=params(12),
        name="attend",
    )(payload, cache, keys, vals, ancestry, pos, limit)


SPAN = 2 * GROUPS


def attend_split_kernel(
    step, near, count, pay_ref, kv_ref, key_ref, val_ref, anc_ref, pos_ref, lim_ref, *refs
):
    out_refs = refs[-count:]
    n = key_ref.shape[0]
    cells = kv_ref.shape[2]
    me = lax.axis_index("tensor")
    start = (me ^ step) * n
    request = me ^ step
    place = pos_ref[pl.ds(pl.multiple_of(start, 8), n), :][:, :1]
    key_pos = (lane_index((n, cells)) + me * cells).astype(F32)
    far_ok = (key_pos < lim_ref[request][:1, :1]) & (
        (key_pos < SINKS) | (place - key_pos < WINDOW)
    )
    bias = jnp.where(far_ok, 0.0, NEG)
    bias = jnp.concatenate([bias] * SPAN, axis=0)
    if near:
        near_bias = jnp.where(anc_ref[...] > 0.5, 0.0, NEG)
        near_bias = jnp.concatenate([near_bias] * SPAN, axis=0)
    lane = lane_index((n, LANES))
    low = lane < HD
    turn = (((1,), (1,)), ((), ()))
    factor = HD ** (-0.5) * LOG2E
    for j in range(count):
        b = me ^ j
        stats = jnp.zeros((n, LANES), F32) if near else out_refs[j][count * GROUPS].astype(F32)
        blocks = [
            pay_ref[:n, pl.ds(pl.multiple_of((GROUPS * b + i) * LANES, LANES), LANES)]
            for i in range(GROUPS)
        ]
        zero = jnp.zeros((n, LANES), BF)
        rows = jnp.concatenate(
            [jnp.where(low, x, zero) for x in blocks] + [jnp.where(low, zero, x) for x in blocks],
            axis=0,
        )
        scores = (
            lax.dot_general(rows, kv_ref[request, 2 * b], turn, preferred_element_type=F32) * factor
            + bias
        )
        top = jnp.max(scores, axis=-1, keepdims=True)
        if near:
            at_pair = pl.ds(pl.multiple_of(b * LANES, LANES), LANES)
            near_scores = (
                lax.dot_general(rows, key_ref[:, at_pair], turn, preferred_element_type=F32) * factor
                + near_bias
            )
            top = jnp.maximum(top, jnp.max(near_scores, axis=-1, keepdims=True))
        top = jnp.maximum(top, FLOOR)
        top = (top + jnp.abs(top) * (2.0**-7)).astype(BF).astype(F32)
        weights = jnp.exp2(scores - top)
        total = jnp.sum(weights, axis=-1, keepdims=True)
        blend = jnp.dot(weights.astype(BF), kv_ref[request, 2 * b + 1], preferred_element_type=F32)
        if near:
            near_weights = jnp.exp2(near_scores - top)
            total = total + jnp.sum(near_weights, axis=-1, keepdims=True)
            blend = blend + jnp.dot(
                near_weights.astype(BF), val_ref[:, at_pair], preferred_element_type=F32
            )
        high = total.astype(BF).astype(F32)
        rest = total - high
        for i in range(GROUPS):
            first = slice(i * n, (i + 1) * n)
            second = slice((GROUPS + i) * n, (GROUPS + i + 1) * n)
            out_refs[j][step * GROUPS + i] = jnp.where(low, blend[first], blend[second]).astype(BF)
            for part, rows_of in enumerate((first, second)):
                at = 3 * SPAN * step + 2 * i + part
                stats = jnp.where(lane == at, top[rows_of], stats)
                stats = jnp.where(lane == at + SPAN, high[rows_of], stats)
                stats = jnp.where(lane == at + 2 * SPAN, rest[rows_of], stats)
        out_refs[j][count * GROUPS] = stats.astype(BF)


def attend_split(step, count, payload, cache, keys, vals, ancestry, pos, limit, outs):
    n = keys.shape[0]
    shape = jax.ShapeDtypeStruct((count * GROUPS + 1, n, LANES), BF)
    return pl.pallas_call(
        functools.partial(attend_split_kernel, step, step == 0, count),
        out_shape=(shape,) * count,
        in_specs=[whole()] * (7 + len(outs)),
        out_specs=(whole(),) * count,
        input_output_aliases={7 + j: j for j in range(len(outs))},
        compiler_params=params(12),
        cost_estimate=cost(4e8),
        name="attend",
    )(payload, cache, keys, vals, ancestry, pos, limit, *outs)


def join_split_kernel(count, weight_ref, *refs):
    parts, out_refs, att = refs[:count], refs[count:-1], refs[-1]
    n = parts[0].shape[1]
    lane = lane_index((n, LANES))
    low = lane < HD
    shifts = [p[count * GROUPS].astype(F32) for p in parts]
    totals = [
        pltpu.roll(s, LANES - SPAN, axis=1) + pltpu.roll(s, LANES - 2 * SPAN, axis=1)
        for s in shifts
    ]
    for k in range(count):
        moves = [(LANES - 3 * SPAN * (j ^ k)) % LANES for j in range(count)]
        tops = [pltpu.roll(s, m, axis=1) if m else s for s, m in zip(shifts, moves)]
        sums = [pltpu.roll(s, m, axis=1) if m else s for s, m in zip(totals, moves)]
        top = functools.reduce(jnp.maximum, tops)
        scales = [jnp.exp2(t - top) for t in tops]
        inverse = 1.0 / functools.reduce(jnp.add, [a * b for a, b in zip(scales, sums)])
        scales = [scale * inverse for scale in scales]
        joined = []
        for i in range(GROUPS):
            acc = jnp.zeros((n, LANES), F32)
            for j in range(count):
                by = jnp.where(
                    low, scales[j][:, 2 * i : 2 * i + 1], scales[j][:, 2 * i + 1 : 2 * i + 2]
                )
                acc = acc + by * parts[j][(j ^ k) * GROUPS + i].astype(F32)
            joined.append(acc)
        turned = pltpu.roll(joined[1], HD, axis=1)
        back = (
            jnp.where(low, joined[0], turned),
            jnp.where(low, joined[2], joined[0]),
            jnp.where(low, turned, joined[2]),
        )
        for i in range(GROUPS):
            att[k * n : (k + 1) * n, i * LANES : (i + 1) * LANES] = back[i].astype(BF)
    for k in list(range(1, count)) + [0]:
        product = jnp.dot(att[k * n : (k + 1) * n, :], weight_ref[...], preferred_element_type=F32)
        out_refs[k][...] = product.astype(out_refs[k].dtype)


def join_split(weight, parts):
    count = len(parts)
    n = parts[0].shape[1]
    width = weight.shape[1]
    return pl.pallas_call(
        functools.partial(join_split_kernel, count),
        out_shape=tuple(
            jax.ShapeDtypeStruct((n, width), BF if k else F32) for k in range(count)
        ),
        in_specs=[whole()] * (1 + count),
        out_specs=(whole(),) * count,
        scratch_shapes=[pltpu.VMEM((count * n, weight.shape[0]), BF)],
        compiler_params=params(12),
        cost_estimate=cost(4e8),
        name="join",
    )(weight, *parts)


def norm_kernel(hidden_ref, gain_ref, own_ref, *refs):
    others, (mixed_ref, normed_ref) = refs[:-2], refs[-2:]
    mixed = hidden_ref[...].astype(F32) + own_ref[...]
    for other in others:
        mixed = mixed + other[...].astype(F32)
    mixed_ref[...] = mixed
    square = jnp.mean(mixed * mixed, axis=-1, keepdims=True)
    normed_ref[...] = (mixed * lax.rsqrt(square + 1e-06) * gain_ref[...]).astype(BF)


def norm(hidden_in, gain, own, others):
    return pl.pallas_call(
        norm_kernel,
        out_shape=(
            jax.ShapeDtypeStruct(hidden_in.shape, F32),
            jax.ShapeDtypeStruct(hidden_in.shape, BF),
        ),
        in_specs=[whole()] * (3 + len(others)),
        out_specs=(whole(), whole()),
        compiler_params=params(4),
        cost_estimate=cost(1e6),
        name="norm",
    )(hidden_in, gain, own, *others)


def join_kernel(count, *refs):
    parts, rest = refs[:count], refs[count:]
    shares = 2 * count - 1
    pieces, rest = rest[:shares], rest[shares:]
    hidden_ref, gain_ref, mixed_ref, normed_ref, att, weight, sems = rest
    n = hidden_ref.shape[0]
    depth = pieces[0].shape[0]
    half = depth // CORES
    width = QH * HD
    me = lax.axis_index("tensor")
    core = lax.axis_index("dp") % CORES
    starts = [me * depth]
    for k in range(1, count):
        starts += [(me ^ k) * depth + core * half, (me ^ k) * depth + (1 - core) * half]
    copies = []
    for j, (piece, start) in enumerate(zip(pieces, starts)):
        rows = weight.at[pl.ds(pl.multiple_of(start, 16), piece.shape[0]), :]
        copies.append(pltpu.make_async_copy(piece, rows, sems.at[j]))
        copies[-1].start()
    stats = [p[:, width:].astype(F32) for p in parts]
    top = stats[0]
    for s in stats[1:]:
        top = jnp.maximum(top, s)
    scales = [jnp.exp2(s - top) for s in stats]
    total = jnp.zeros((n, LANES), F32)
    for s, scale in zip(stats, scales):
        sums = pltpu.roll(s, LANES - QH, axis=1) + pltpu.roll(s, LANES - 2 * QH, axis=1)
        total = total + scale * sums
    inverse = 1.0 / total
    scales = [scale * inverse for scale in scales]
    low = lane_index((n, LANES)) < HD

    for b in range(PAIRS):
        joined = []
        for i in range(GROUPS):
            block = GROUPS * b + i
            acc = jnp.zeros((n, LANES), F32)
            for p, scale in zip(parts, scales):
                by = jnp.where(
                    low, scale[:, 2 * block : 2 * block + 1], scale[:, 2 * block + 1 : 2 * block + 2]
                )
                acc = acc + by * p[:, block * LANES : (block + 1) * LANES].astype(F32)
            joined.append(acc)
        turned = pltpu.roll(joined[1], HD, axis=1)
        back = (
            jnp.where(low, joined[0], turned),
            jnp.where(low, joined[2], joined[0]),
            jnp.where(low, turned, joined[2]),
        )
        for i in range(GROUPS):
            block = GROUPS * b + i
            att[:, block * LANES : (block + 1) * LANES] = back[i].astype(BF)
    for copy in copies:
        copy.wait()
    attended = jnp.dot(att[...], weight[...], preferred_element_type=F32)
    mixed = hidden_ref[...].astype(F32) + attended
    mixed_ref[...] = mixed
    square = jnp.mean(mixed * mixed, axis=-1, keepdims=True)
    normed_ref[...] = (mixed * lax.rsqrt(square + 1e-06) * gain_ref[...]).astype(BF)


def join(parts, pieces, hidden_in, gain):
    n, width = hidden_in.shape
    count = len(parts)
    inner = QH * HD
    return pl.pallas_call(
        functools.partial(join_kernel, count),
        out_shape=(
            jax.ShapeDtypeStruct((n, width), F32),
            jax.ShapeDtypeStruct((n, width), BF),
        ),
        in_specs=[whole()] * count
        + [pl.BlockSpec(memory_space=pl.ANY)] * len(pieces)
        + [whole(), whole()],
        out_specs=(whole(), whole()),
        scratch_shapes=[
            pltpu.VMEM((n, inner), BF),
            pltpu.VMEM((inner, width), BF),
            pltpu.SemaphoreType.DMA((len(pieces),)),
        ],
        compiler_params=params(14),
        name="join",
    )(*parts, *pieces, hidden_in, gain)


def experts_kernel(
    step, bias_ref, route_ref, wg, wu, wd, a_ref, b_ref, own_ref, other_ref
):
    n, width = a_ref.shape
    local = wg.shape[0]
    experts = bias_ref.shape[2]
    me = lax.axis_index("dp")
    x = jnp.concatenate([a_ref[...], b_ref[...]], axis=0)
    logits = lax.dot_general(
        x, route_ref[...], (((1,), (1,)), ((), ())), preferred_element_type=F32
    )
    logits = logits[:, :experts] + logits[:, experts:]
    first = CORES * step
    logits = logits + jnp.concatenate([bias_ref[me ^ first], bias_ref[me ^ (first + 1)]], axis=0)
    gates = jnp.exp(logits - jnp.max(logits, axis=-1, keepdims=True))
    gates = gates / jnp.sum(gates, axis=-1, keepdims=True)
    lane = lane_index(gates.shape)
    acc = None
    for e in range(local):
        gate_hidden = jnp.dot(x, wg[e], preferred_element_type=F32)
        up_hidden = jnp.dot(x, wu[e], preferred_element_type=F32)
        activated = (gate_hidden / (1.0 + jnp.exp(-gate_hidden)) * up_hidden).astype(BF)
        made = jnp.dot(activated, wd[e], preferred_element_type=F32).astype(BF).astype(F32)
        gate = jnp.sum(jnp.where(lane == me * local + e, gates, 0.0), axis=-1, keepdims=True)
        acc = gate * made if acc is None else acc + gate * made
    own_ref[...] = acc[:n]
    other_ref[...] = acc[n:].astype(BF)


def experts_part(step, bias, route, w_gate, w_up, w_down, a, b):
    n, width = a.shape
    return pl.pallas_call(
        functools.partial(experts_kernel, step),
        out_shape=(
            jax.ShapeDtypeStruct((n, width), F32),
            jax.ShapeDtypeStruct((n, width), BF),
        ),
        in_specs=[whole()] * 7,
        out_specs=(whole(), whole()),
        compiler_params=params(12),
        cost_estimate=cost(12e8),
        name="experts",
    )(bias, route, w_gate, w_up, w_down, a, b)


def accepted_kernel(count, n, *refs):
    out_ref = refs[count]
    requests = out_ref.shape[0]
    draft = count * n // requests
    out_ref[...] = jnp.zeros(out_ref.shape, out_ref.dtype)
    for k in range(count):
        request = (lax.axis_index("tensor") ^ k) * n // draft
        out_ref[request] = out_ref[request] + refs[k][:, : out_ref.shape[2]]


def accepted(payloads, requests, entries, n):
    count = len(payloads)
    block = pl.BlockSpec((entries, payloads[0].shape[1]), lambda i: (n // entries, 0))
    return pl.pallas_call(
        functools.partial(accepted_kernel, count, n),
        out_shape=jax.ShapeDtypeStruct((requests, entries, 2 * KVH * HD), BF),
        grid=(1,),
        in_specs=[block] * count,
        out_specs=pl.BlockSpec((requests, entries, 2 * KVH * HD), lambda i: (0, 0, 0)),
        compiler_params=params(4),
        cost_estimate=cost(1e6),
        name="accepted",
    )(*payloads)


def rows_by_lane_block(kv):
    lead, (tokens, two, width) = kv.shape[:-3], kv.shape[-3:]
    split = kv.reshape(*lead, tokens, two, width // LANES, LANES)
    return jnp.swapaxes(split, -3, -2).reshape(*lead, tokens * two * width // LANES, LANES)


def body(
    hidden_in, queries, draft_kv, cache_kv, cache_len, parents, path, routes,
    w_out, router, norm_gain, w_gate, w_up, w_down,
):
    tensor = lax.axis_size("tensor")
    data = lax.axis_size("dp")
    n = queries.shape[0]
    requests, draft = parents.shape
    payload, keys, vals, ancestry, pos, limit, packed = prelude(
        cache_len,
        path,
        parents,
        queries,
        rows_by_lane_block(draft_kv),
        rows_by_lane_block(cache_kv),
    )
    payloads = [payload] + [exchange(payload, "tensor", tensor, k) for k in range(1, tensor)]
    unpacked = unpack(packed)
    tables = jnp.swapaxes(routes, 1, 2), router.T
    gain = norm_gain.reshape(1, -1)
    if n == draft and tensor == PAIRS:
        parts = ()
        for k in range(tensor):
            parts = attend_split(
                k, tensor, payloads[k], unpacked, keys, vals, ancestry, pos, limit, parts
            )
        tables = lax.optimization_barrier((*tables, parts[0]))[:2]
        parts = [parts[0]] + [exchange(parts[j], "tensor", tensor, j) for j in range(1, tensor)]
        bias, route = routing(*tables)
        parts, bias, route = lax.optimization_barrier((parts, bias, route))
        products = join_split(w_out, parts)
        others = [exchange(products[k], "tensor", tensor, k) for k in range(1, tensor)]
        mixed, normed = norm(hidden_in, gain, products[0], others)
    else:
        half = w_out.shape[0] // CORES
        mine = lax.dynamic_slice_in_dim(w_out, lax.axis_index("dp") % CORES * half, half, 0)
        mine = lax.optimization_barrier((mine, *payloads[1:]))[0]
        fetched = [exchange(mine, "tensor", tensor, k) for k in range(1, tensor)]
        parts = []
        for k in range(tensor):
            near = k < max(1, draft // n)
            part = attend(k, near, payloads[k], unpacked, keys, vals, ancestry, pos, limit)
            parts.append(part if k == 0 else exchange(part, "tensor", tensor, k))
        pieces = [w_out]
        for piece in fetched:
            pieces += [piece, exchange(piece, "dp", data, 1)]
        mixed, normed = join(parts, pieces, hidden_in, gain)
        bias, route = routing(*tables)
    compacted = accepted(payloads, requests, path.shape[1], n)

    steps = data // CORES
    lines = {0: normed}
    reach = steps // 2
    while reach:
        for k in [k for k in lines if k % (2 * reach) == 0]:
            lines[k + reach] = exchange(lines[k], "dp", data, CORES * reach)
        reach //= 2
    single = [k for k in lines if k and k & (k - 1) == 0]
    total = mixed
    last = None
    for k in sorted(lines, key=lambda k: (bin(k).count("1"), -k)):
        if k == max(single) or (k and k not in single):
            names = single if k in single else [k]
            tied = lax.optimization_barrier([lines[name] for name in names] + [last])
            lines.update(zip(names, tied))
        line = lines[k]
        twin = exchange(line, "dp", data, 1)
        own, other = experts_part(k, bias, route, w_gate, w_up, w_down, line, twin)
        last = own
        chip = own + exchange(other, "dp", data, 1).astype(F32)
        if k:
            chip = exchange(chip.astype(BF), "dp", data, CORES * k).astype(F32)
        total = total + chip
    return total.astype(BF), compacted


def solution(mesh):
    in_specs = (
        P(("dp", "tensor"), None),
        P(("dp", "tensor"), None),
        P(("dp", "tensor"), None, None),
        P("dp", "tensor", None, None),
        P("dp"),
        P("dp", None),
        P("dp", None),
        P(None, "tensor", None),
        P("tensor", None),
        P(),
        P(),
        P("dp", None, None),
        P("dp", None, None),
        P("dp", None, None),
    )
    out_specs = (P(("dp", "tensor"), None), P("dp", None, None))
    return jax.shard_map(body, mesh=mesh, in_specs=in_specs, out_specs=out_specs, check_vma=False)
```

```python
import functools

import jax
import jax.numpy as jnp
import numpy as np
from jax import lax
from jax.experimental import pallas as pl
from jax.experimental.pallas import tpu as pltpu
from jax.sharding import PartitionSpec as P

QH = 24
KVH = 8
HD = 64
TOP = 8
SINKS = 4
WINDOW = 1024

LANES = 128
PAIRS = KVH * HD // LANES
GROUPS = QH // KVH
CORES = 2
NEG = -1e30
FLOOR = -1e6
BF = jnp.bfloat16
F32 = jnp.float32
LOG2E = 1.4426950408889634
MIB = 1024 * 1024

INVERSE = [
    float(x)
    for x in (10000.0 ** (-2.0 * np.arange(HD // 2, dtype=np.float64) / HD)).astype(np.float32)
]


def params(mib):
    return pltpu.CompilerParams(vmem_limit_bytes=mib * MIB)


def whole():
    return pl.BlockSpec(memory_space=pltpu.VMEM)


def in_hbm():
    return pl.BlockSpec(memory_space=pltpu.HBM)


def fixed(x):
    return pltpu.with_memory_space_constraint(x, pltpu.HBM)


def cost(flops):
    return pl.CostEstimate(flops=int(flops), bytes_accessed=0, transcendentals=0)


def exchange(x, axis, size, step):
    return lax.ppermute(x, axis, [(i, i ^ step) for i in range(size)])


def lane_index(shape):
    return lax.broadcasted_iota(jnp.int32, shape, len(shape) - 1)


def prelude_kernel(
    len_hbm, path_hbm, par_hbm, q_hbm, kv_hbm, cache_hbm,
    pay_ref, key_ref, val_ref, anc_ref, pos_ref, lim_ref, packed_ref, pick_ref,
    len_ref, path_ref, par_ref, q_ref, kv_ref, kv_f, anc_all, sems,
):
    copies = [
        pltpu.make_async_copy(src, dst, sems.at[j])
        for j, (src, dst) in enumerate(
            (
                (par_hbm, par_ref), (len_hbm, len_ref), (path_hbm, path_ref),
                (kv_hbm, kv_ref), (q_hbm, q_ref), (cache_hbm, packed_ref),
            )
        )
    ]
    for copy in copies:
        copy.start()
    for copy in copies[:3]:
        copy.wait()
    requests, draft = par_ref.shape
    n = q_ref.shape[0]
    own_start = lax.axis_index("tensor") * n
    request = own_start // draft
    offset = own_start % draft
    row = lax.broadcasted_iota(jnp.int32, (draft, draft), 0)
    col = lax.broadcasted_iota(jnp.int32, (draft, draft), 1)
    eye = (row == col).astype(F32)
    linked = [
        ((row == par_ref[r : r + 1, :]).astype(F32) + eye).T.astype(BF) for r in range(requests)
    ]
    for level in range((draft - 1).bit_length()):
        linked = [
            jnp.minimum(jnp.dot(m, m, preferred_element_type=F32), 1.0).astype(BF) for m in linked
        ]
    for r in range(requests):
        ancestry = linked[r].astype(F32)
        depth = jnp.sum(ancestry, axis=-1, keepdims=True) - 1.0
        place = depth + len_ref[r].astype(F32)
        pos_ref[r * draft : (r + 1) * draft, :] = jnp.broadcast_to(place, (draft, LANES))
        lim_ref[r] = jnp.full((8, LANES), len_ref[r].astype(F32))
        anc_all[r] = ancestry
    anc_ref[...] = anc_all[request]
    own = pl.multiple_of(own_start, 8)
    lane = lane_index((n, LANES))
    step = lane_index((8, LANES)) % (HD // 2)
    inverse = jnp.full(step.shape, INVERSE[0], F32)
    for k in range(1, HD // 2):
        inverse = jnp.where(step == k, INVERSE[k], inverse)
    angle = pos_ref[pl.ds(own, n), :] * inverse[:1, :]
    front = lane % HD < HD // 2
    cosine = jnp.cos(angle)
    sine = jnp.sin(angle)
    sine = jnp.where(front, -sine, sine)
    low = lane < HD

    def turned(x):
        partner = jnp.where(
            front, pltpu.roll(x, LANES - HD // 2, axis=1), pltpu.roll(x, HD // 2, axis=1)
        )
        return x * cosine + partner * sine

    copies[3].wait()
    kv_f[...] = kv_ref[...].astype(F32)
    slot = lax.broadcasted_iota(jnp.int32, (path_ref.shape[1], n), 0)
    token = lax.broadcasted_iota(jnp.int32, (path_ref.shape[1], n), 1) + offset
    wanted = jnp.full(slot.shape, -1, jnp.int32)
    for k in range(path_ref.shape[1]):
        wanted = jnp.where(slot == k, path_ref[request, k], wanted)
    chooser = (wanted == token).astype(BF)
    keys, vals = [], []
    for b in range(PAIRS):
        keys.append(turned(kv_f[pl.ds(2 * b, n, stride=2 * PAIRS), :]).astype(BF))
        vals.append(kv_f[pl.ds(2 * b + 1, n, stride=2 * PAIRS), :].astype(BF))
        key_ref[:, b * LANES : (b + 1) * LANES] = keys[b]
        val_ref[:, b * LANES : (b + 1) * LANES] = vals[b]
    copies[4].wait()
    packed = jnp.concatenate(keys + vals, axis=1)
    pick_ref[...] = jnp.dot(chooser, packed, preferred_element_type=F32).astype(BF)
    for b in range(PAIRS):
        x0, x1, x2 = [
            turned(q_ref[:, (GROUPS * b + i) * LANES : (GROUPS * b + i + 1) * LANES].astype(F32))
            for i in range(GROUPS)
        ]
        y0 = jnp.where(low, x0, x1)
        y1 = jnp.where(low, pltpu.roll(x0, HD, axis=1), pltpu.roll(x2, HD, axis=1))
        y2 = jnp.where(low, x1, x2)
        for i, y in enumerate((y0, y1, y2)):
            pay_ref[:, (GROUPS * b + i) * LANES : (GROUPS * b + i + 1) * LANES] = y.astype(BF)
    copies[5].wait()


def prelude(cache_len, path, parents, queries, kv, cache):
    requests, draft = parents.shape
    n, width = queries.shape
    kv_width = KVH * HD
    return pl.pallas_call(
        prelude_kernel,
        out_shape=(
            jax.ShapeDtypeStruct((n, width), BF),
            jax.ShapeDtypeStruct((n, kv_width), BF),
            jax.ShapeDtypeStruct((n, kv_width), BF),
            jax.ShapeDtypeStruct((draft, draft), F32),
            jax.ShapeDtypeStruct((requests * draft, LANES), F32),
            jax.ShapeDtypeStruct((requests, 8, LANES), F32),
            jax.ShapeDtypeStruct(cache.shape, BF),
            jax.ShapeDtypeStruct((path.shape[1], 2 * kv_width), BF),
        ),
        in_specs=[in_hbm()] * 6,
        out_specs=(whole(),) * 8,
        scratch_shapes=[
            pltpu.SMEM(cache_len.shape, jnp.int32),
            pltpu.SMEM(path.shape, jnp.int32),
            pltpu.VMEM(parents.shape, jnp.int32),
            pltpu.VMEM(queries.shape, BF),
            pltpu.VMEM(kv.shape, BF),
            pltpu.VMEM(kv.shape, F32),
            pltpu.VMEM((requests, draft, draft), F32),
            pltpu.SemaphoreType.DMA((6,)),
        ],
        compiler_params=params(8),
        cost_estimate=cost(1e7),
        name="prelude",
    )(*[fixed(x) for x in (cache_len, path, parents, queries, kv, cache)])


def unpack_kernel(packed_ref, out_ref, kv_f):
    requests, _, cells, _ = out_ref.shape
    for r in range(requests):
        kv_f[r % 2] = packed_ref[r].astype(F32)
        for j in range(2 * PAIRS):
            out_ref[r, j] = kv_f[r % 2, pl.ds(j, cells, stride=2 * PAIRS), :].astype(BF)


def unpack(packed):
    requests, span, _ = packed.shape
    return pl.pallas_call(
        unpack_kernel,
        out_shape=jax.ShapeDtypeStruct(
            (requests, 2 * PAIRS, span // (2 * PAIRS), LANES), BF
        ),
        in_specs=[whole()],
        out_specs=whole(),
        scratch_shapes=[pltpu.VMEM((2, span, LANES), F32)],
        compiler_params=params(8),
        cost_estimate=cost(1e8),
        name="unpack",
    )(packed)


def routing_kernel(routes_hbm, router_hbm, bias_ref, route_w_ref, routes_ref, router_ref, sems):
    copies = [
        pltpu.make_async_copy(routes_hbm, routes_ref, sems.at[0]),
        pltpu.make_async_copy(router_hbm, router_ref, sems.at[1]),
    ]
    for copy in copies:
        copy.start()
    for copy in copies:
        copy.wait()
    experts = router_ref.shape[0]
    router = router_ref[...]
    high = router.astype(BF)
    route_w_ref[:experts, :] = high
    route_w_ref[experts:, :] = (router - high.astype(F32)).astype(BF)
    for d in range(routes_ref.shape[0]):
        chosen = routes_ref[d]
        expert = lax.broadcasted_iota(jnp.int32, (experts, chosen.shape[1]), 0)
        hit = expert == chosen[0:1, :]
        for k in range(1, chosen.shape[0]):
            hit = hit | (expert == chosen[k : k + 1, :])
        bias_ref[d] = jnp.where(hit, 0.0, NEG).T


def routing(routes, router):
    experts, width = router.shape
    blocks, top, n = routes.shape
    return pl.pallas_call(
        routing_kernel,
        out_shape=(
            jax.ShapeDtypeStruct((blocks, n, experts), F32),
            jax.ShapeDtypeStruct((2 * experts, width), BF),
        ),
        in_specs=[in_hbm()] * 2,
        out_specs=(whole(),) * 2,
        scratch_shapes=[
            pltpu.VMEM(routes.shape, jnp.int32),
            pltpu.VMEM(router.shape, F32),
            pltpu.SemaphoreType.DMA((2,)),
        ],
        compiler_params=params(8),
        cost_estimate=cost(1e6),
        name="routing",
    )(fixed(routes), fixed(router))


def attend_kernel(
    step, near, pay_ref, kv_ref, key_ref, val_ref, anc_ref, pos_ref, lim_ref, out_ref
):
    draft = anc_ref.shape[0]
    n = key_ref.shape[0]
    cells = kv_ref.shape[2]
    me = lax.axis_index("tensor")
    start = (me ^ step) * n
    request = start // draft
    key_start = me * cells
    place = pos_ref[pl.ds(pl.multiple_of(start, 8), n), :][:, :1]
    key_pos = (lane_index((n, cells)) + key_start).astype(F32)
    far_ok = (key_pos < lim_ref[request][:1, :1]) & (
        (key_pos < SINKS) | (place - key_pos < WINDOW)
    )
    bias = jnp.where(far_ok, 0.0, NEG)
    bias = jnp.concatenate([bias] * (2 * GROUPS), axis=0)
    if near:
        own = me * n
        same = (own // draft) == request
        line = anc_ref[pl.ds(pl.multiple_of(start % draft, 8), n), :]
        if n != draft:
            pick = (
                lax.broadcasted_iota(jnp.int32, (draft, n), 0)
                == lax.broadcasted_iota(jnp.int32, (draft, n), 1) + own % draft
            ).astype(BF)
            line = jnp.dot(line.astype(BF), pick, preferred_element_type=F32)
        seen = jnp.where(same, line, 0.0)
        near_bias = jnp.where(seen > 0.5, 0.0, NEG)
        near_bias = jnp.concatenate([near_bias] * (2 * GROUPS), axis=0)
    low = lane_index((n, LANES)) < HD
    lane = lane_index((n, LANES))
    stats = jnp.zeros((n, LANES), F32)
    turn = (((1,), (1,)), ((), ()))
    factor = HD ** (-0.5) * LOG2E
    for b in range(PAIRS):
        keys = kv_ref[request, 2 * b]
        vals = kv_ref[request, 2 * b + 1]
        blocks = [
            pay_ref[:n, (GROUPS * b + i) * LANES : (GROUPS * b + i + 1) * LANES]
            for i in range(GROUPS)
        ]
        zero = jnp.zeros((n, LANES), BF)
        rows = jnp.concatenate(
            [jnp.where(low, x, zero) for x in blocks] + [jnp.where(low, zero, x) for x in blocks],
            axis=0,
        )
        scores = lax.dot_general(rows, keys, turn, preferred_element_type=F32) * factor + bias
        top = jnp.max(scores, axis=-1, keepdims=True)
        if near:
            near_scores = (
                lax.dot_general(
                    rows, key_ref[:, b * LANES : (b + 1) * LANES], turn, preferred_element_type=F32
                )
                * factor
                + near_bias
            )
            top = jnp.maximum(top, jnp.max(near_scores, axis=-1, keepdims=True))
        top = jnp.maximum(top, FLOOR)
        top = (top + jnp.abs(top) * (2.0**-7)).astype(BF).astype(F32)
        weights = jnp.exp2(scores - top)
        total = jnp.sum(weights, axis=-1, keepdims=True)
        blend = jnp.dot(weights.astype(BF), vals, preferred_element_type=F32)
        if near:
            near_weights = jnp.exp2(near_scores - top)
            total = total + jnp.sum(near_weights, axis=-1, keepdims=True)
            blend = blend + jnp.dot(
                near_weights.astype(BF),
                val_ref[:, b * LANES : (b + 1) * LANES],
                preferred_element_type=F32,
            )
        high = total.astype(BF).astype(F32)
        rest = total - high
        for i in range(GROUPS):
            first = slice(i * n, (i + 1) * n)
            second = slice((GROUPS + i) * n, (GROUPS + i + 1) * n)
            block = GROUPS * b + i
            out_ref[:, block * LANES : (block + 1) * LANES] = jnp.where(
                low, blend[first], blend[second]
            ).astype(BF)
            for part, rows_of in enumerate((first, second)):
                at = 2 * block + part
                stats = jnp.where(lane == at, top[rows_of], stats)
                stats = jnp.where(lane == QH + at, high[rows_of], stats)
                stats = jnp.where(lane == 2 * QH + at, rest[rows_of], stats)
    out_ref[:, QH * HD :] = stats.astype(BF)


def attend(step, near, payload, cache, keys, vals, ancestry, pos, limit):
    n = keys.shape[0]
    return pl.pallas_call(
        functools.partial(attend_kernel, step, near),
        out_shape=jax.ShapeDtypeStruct((n, QH * HD + LANES), BF),
        in_specs=[whole()] * 7,
        out_specs=whole(),
        compiler_params=params(12),
        name="attend",
    )(payload, cache, keys, vals, ancestry, pos, limit)


SPAN = 2 * GROUPS


def attend_split_kernel(
    step, near, count, pay_ref, kv_ref, key_ref, val_ref, anc_ref, pos_ref, lim_ref, *refs
):
    out_refs = refs[-count:]
    n = key_ref.shape[0]
    cells = kv_ref.shape[2]
    me = lax.axis_index("tensor")
    start = (me ^ step) * n
    request = me ^ step
    place = pos_ref[pl.ds(pl.multiple_of(start, 8), n), :][:, :1]
    key_pos = (lane_index((n, cells)) + me * cells).astype(F32)
    far_ok = (key_pos < lim_ref[request][:1, :1]) & (
        (key_pos < SINKS) | (place - key_pos < WINDOW)
    )
    bias = jnp.where(far_ok, 0.0, NEG)
    bias = jnp.concatenate([bias] * SPAN, axis=0)
    if near:
        near_bias = jnp.where(anc_ref[...] > 0.5, 0.0, NEG)
        near_bias = jnp.concatenate([near_bias] * SPAN, axis=0)
    lane = lane_index((n, LANES))
    low = lane < HD
    turn = (((1,), (1,)), ((), ()))
    factor = HD ** (-0.5) * LOG2E
    for j in range(count):
        b = me ^ j
        stats = jnp.zeros((n, LANES), F32) if near else out_refs[j][count * GROUPS].astype(F32)
        blocks = [
            pay_ref[:n, pl.ds(pl.multiple_of((GROUPS * b + i) * LANES, LANES), LANES)]
            for i in range(GROUPS)
        ]
        zero = jnp.zeros((n, LANES), BF)
        rows = jnp.concatenate(
            [jnp.where(low, x, zero) for x in blocks] + [jnp.where(low, zero, x) for x in blocks],
            axis=0,
        )
        scores = (
            lax.dot_general(rows, kv_ref[request, 2 * b], turn, preferred_element_type=F32) * factor
            + bias
        )
        top = jnp.max(scores, axis=-1, keepdims=True)
        if near:
            at_pair = pl.ds(pl.multiple_of(b * LANES, LANES), LANES)
            near_scores = (
                lax.dot_general(rows, key_ref[:, at_pair], turn, preferred_element_type=F32) * factor
                + near_bias
            )
            top = jnp.maximum(top, jnp.max(near_scores, axis=-1, keepdims=True))
        top = jnp.maximum(top, FLOOR)
        top = (top + jnp.abs(top) * (2.0**-7)).astype(BF).astype(F32)
        weights = jnp.exp2(scores - top)
        total = jnp.sum(weights, axis=-1, keepdims=True)
        blend = jnp.dot(weights.astype(BF), kv_ref[request, 2 * b + 1], preferred_element_type=F32)
        if near:
            near_weights = jnp.exp2(near_scores - top)
            total = total + jnp.sum(near_weights, axis=-1, keepdims=True)
            blend = blend + jnp.dot(
                near_weights.astype(BF), val_ref[:, at_pair], preferred_element_type=F32
            )
        high = total.astype(BF).astype(F32)
        rest = total - high
        for i in range(GROUPS):
            first = slice(i * n, (i + 1) * n)
            second = slice((GROUPS + i) * n, (GROUPS + i + 1) * n)
            out_refs[j][step * GROUPS + i] = jnp.where(low, blend[first], blend[second]).astype(BF)
            for part, rows_of in enumerate((first, second)):
                at = 3 * SPAN * step + 2 * i + part
                stats = jnp.where(lane == at, top[rows_of], stats)
                stats = jnp.where(lane == at + SPAN, high[rows_of], stats)
                stats = jnp.where(lane == at + 2 * SPAN, rest[rows_of], stats)
        out_refs[j][count * GROUPS] = stats.astype(BF)


def attend_split(step, count, payload, cache, keys, vals, ancestry, pos, limit, outs):
    n = keys.shape[0]
    shape = jax.ShapeDtypeStruct((count * GROUPS + 1, n, LANES), BF)
    return pl.pallas_call(
        functools.partial(attend_split_kernel, step, step == 0, count),
        out_shape=(shape,) * count,
        in_specs=[whole()] * (7 + len(outs)),
        out_specs=(whole(),) * count,
        input_output_aliases={7 + j: j for j in range(len(outs))},
        compiler_params=params(12),
        cost_estimate=cost(4e8),
        name="attend",
    )(payload, cache, keys, vals, ancestry, pos, limit, *outs)


def join_split_kernel(count, weight_ref, *refs):
    parts, out_refs, att = refs[:count], refs[count:-1], refs[-1]
    n = parts[0].shape[1]
    lane = lane_index((n, LANES))
    low = lane < HD
    shifts = [p[count * GROUPS].astype(F32) for p in parts]
    totals = [
        pltpu.roll(s, LANES - SPAN, axis=1) + pltpu.roll(s, LANES - 2 * SPAN, axis=1)
        for s in shifts
    ]
    for k in range(count):
        moves = [(LANES - 3 * SPAN * (j ^ k)) % LANES for j in range(count)]
        tops = [pltpu.roll(s, m, axis=1) if m else s for s, m in zip(shifts, moves)]
        sums = [pltpu.roll(s, m, axis=1) if m else s for s, m in zip(totals, moves)]
        top = functools.reduce(jnp.maximum, tops)
        scales = [jnp.exp2(t - top) for t in tops]
        inverse = 1.0 / functools.reduce(jnp.add, [a * b for a, b in zip(scales, sums)])
        scales = [scale * inverse for scale in scales]
        joined = []
        for i in range(GROUPS):
            acc = jnp.zeros((n, LANES), F32)
            for j in range(count):
                by = jnp.where(
                    low, scales[j][:, 2 * i : 2 * i + 1], scales[j][:, 2 * i + 1 : 2 * i + 2]
                )
                acc = acc + by * parts[j][(j ^ k) * GROUPS + i].astype(F32)
            joined.append(acc)
        turned = pltpu.roll(joined[1], HD, axis=1)
        back = (
            jnp.where(low, joined[0], turned),
            jnp.where(low, joined[2], joined[0]),
            jnp.where(low, turned, joined[2]),
        )
        for i in range(GROUPS):
            att[k * n : (k + 1) * n, i * LANES : (i + 1) * LANES] = back[i].astype(BF)
    for k in list(range(1, count)) + [0]:
        product = jnp.dot(att[k * n : (k + 1) * n, :], weight_ref[...], preferred_element_type=F32)
        out_refs[k][...] = product.astype(out_refs[k].dtype)


def join_split(weight, parts):
    count = len(parts)
    n = parts[0].shape[1]
    width = weight.shape[1]
    return pl.pallas_call(
        functools.partial(join_split_kernel, count),
        out_shape=tuple(
            jax.ShapeDtypeStruct((n, width), BF if k else F32) for k in range(count)
        ),
        in_specs=[whole()] * (1 + count),
        out_specs=(whole(),) * count,
        scratch_shapes=[pltpu.VMEM((count * n, weight.shape[0]), BF)],
        compiler_params=params(12),
        cost_estimate=cost(4e8),
        name="join",
    )(weight, *parts)


def norm_kernel(hidden_ref, gain_ref, own_ref, *refs):
    others, (mixed_ref, normed_ref) = refs[:-2], refs[-2:]
    mixed = hidden_ref[...].astype(F32) + own_ref[...]
    for other in others:
        mixed = mixed + other[...].astype(F32)
    mixed_ref[...] = mixed
    square = jnp.mean(mixed * mixed, axis=-1, keepdims=True)
    normed_ref[...] = (mixed * lax.rsqrt(square + 1e-06) * gain_ref[...]).astype(BF)


def norm(hidden_in, gain, own, others):
    return pl.pallas_call(
        norm_kernel,
        out_shape=(
            jax.ShapeDtypeStruct(hidden_in.shape, F32),
            jax.ShapeDtypeStruct(hidden_in.shape, BF),
        ),
        in_specs=[whole()] * (3 + len(others)),
        out_specs=(whole(), whole()),
        compiler_params=params(4),
        cost_estimate=cost(1e6),
        name="norm",
    )(hidden_in, gain, own, *others)


def join_kernel(count, *refs):
    parts, rest = refs[:count], refs[count:]
    shares = 2 * count - 1
    pieces, rest = rest[:shares], rest[shares:]
    hidden_ref, gain_ref, mixed_ref, normed_ref, att, weight, sems = rest
    n = hidden_ref.shape[0]
    depth = pieces[0].shape[0]
    half = depth // CORES
    width = QH * HD
    me = lax.axis_index("tensor")
    core = lax.axis_index("dp") % CORES
    starts = [me * depth]
    for k in range(1, count):
        starts += [(me ^ k) * depth + core * half, (me ^ k) * depth + (1 - core) * half]
    copies = []
    for j, (piece, start) in enumerate(zip(pieces, starts)):
        rows = weight.at[pl.ds(pl.multiple_of(start, 16), piece.shape[0]), :]
        copies.append(pltpu.make_async_copy(piece, rows, sems.at[j]))
        copies[-1].start()
    stats = [p[:, width:].astype(F32) for p in parts]
    top = stats[0]
    for s in stats[1:]:
        top = jnp.maximum(top, s)
    scales = [jnp.exp2(s - top) for s in stats]
    total = jnp.zeros((n, LANES), F32)
    for s, scale in zip(stats, scales):
        sums = pltpu.roll(s, LANES - QH, axis=1) + pltpu.roll(s, LANES - 2 * QH, axis=1)
        total = total + scale * sums
    inverse = 1.0 / total
    scales = [scale * inverse for scale in scales]
    low = lane_index((n, LANES)) < HD

    for b in range(PAIRS):
        joined = []
        for i in range(GROUPS):
            block = GROUPS * b + i
            acc = jnp.zeros((n, LANES), F32)
            for p, scale in zip(parts, scales):
                by = jnp.where(
                    low, scale[:, 2 * block : 2 * block + 1], scale[:, 2 * block + 1 : 2 * block + 2]
                )
                acc = acc + by * p[:, block * LANES : (block + 1) * LANES].astype(F32)
            joined.append(acc)
        turned = pltpu.roll(joined[1], HD, axis=1)
        back = (
            jnp.where(low, joined[0], turned),
            jnp.where(low, joined[2], joined[0]),
            jnp.where(low, turned, joined[2]),
        )
        for i in range(GROUPS):
            block = GROUPS * b + i
            att[:, block * LANES : (block + 1) * LANES] = back[i].astype(BF)
    for copy in copies:
        copy.wait()
    attended = jnp.dot(att[...], weight[...], preferred_element_type=F32)
    mixed = hidden_ref[...].astype(F32) + attended
    mixed_ref[...] = mixed
    square = jnp.mean(mixed * mixed, axis=-1, keepdims=True)
    normed_ref[...] = (mixed * lax.rsqrt(square + 1e-06) * gain_ref[...]).astype(BF)


def join(parts, pieces, hidden_in, gain):
    n, width = hidden_in.shape
    count = len(parts)
    inner = QH * HD
    return pl.pallas_call(
        functools.partial(join_kernel, count),
        out_shape=(
            jax.ShapeDtypeStruct((n, width), F32),
            jax.ShapeDtypeStruct((n, width), BF),
        ),
        in_specs=[whole()] * count
        + [pl.BlockSpec(memory_space=pl.ANY)] * len(pieces)
        + [whole(), whole()],
        out_specs=(whole(), whole()),
        scratch_shapes=[
            pltpu.VMEM((n, inner), BF),
            pltpu.VMEM((inner, width), BF),
            pltpu.SemaphoreType.DMA((len(pieces),)),
        ],
        compiler_params=params(14),
        name="join",
    )(*parts, *pieces, hidden_in, gain)


def experts_kernel(
    step, bias_ref, route_ref, wg, wu, wd, a_ref, b_ref, own_ref, other_ref
):
    n, width = a_ref.shape
    local = wg.shape[0]
    experts = bias_ref.shape[2]
    me = lax.axis_index("dp")
    x = jnp.concatenate([a_ref[...], b_ref[...]], axis=0)
    logits = lax.dot_general(
        x, route_ref[...], (((1,), (1,)), ((), ())), preferred_element_type=F32
    )
    logits = logits[:, :experts] + logits[:, experts:]
    first = CORES * step
    logits = logits + jnp.concatenate([bias_ref[me ^ first], bias_ref[me ^ (first + 1)]], axis=0)
    gates = jnp.exp(logits - jnp.max(logits, axis=-1, keepdims=True))
    gates = gates / jnp.sum(gates, axis=-1, keepdims=True)
    lane = lane_index(gates.shape)
    acc = None
    for e in range(local):
        gate_hidden = jnp.dot(x, wg[e], preferred_element_type=F32)
        up_hidden = jnp.dot(x, wu[e], preferred_element_type=F32)
        activated = (gate_hidden / (1.0 + jnp.exp(-gate_hidden)) * up_hidden).astype(BF)
        made = jnp.dot(activated, wd[e], preferred_element_type=F32).astype(BF).astype(F32)
        gate = jnp.sum(jnp.where(lane == me * local + e, gates, 0.0), axis=-1, keepdims=True)
        acc = gate * made if acc is None else acc + gate * made
    own_ref[...] = acc[:n]
    other_ref[...] = acc[n:].astype(BF)


def experts_part(step, bias, route, w_gate, w_up, w_down, a, b):
    n, width = a.shape
    return pl.pallas_call(
        functools.partial(experts_kernel, step),
        out_shape=(
            jax.ShapeDtypeStruct((n, width), F32),
            jax.ShapeDtypeStruct((n, width), BF),
        ),
        in_specs=[whole()] * 7,
        out_specs=(whole(), whole()),
        compiler_params=params(12),
        cost_estimate=cost(12e8),
        name="experts",
    )(bias, route, w_gate, w_up, w_down, a, b)


def accepted_kernel(n, picks_ref, out_ref):
    requests, entries, _ = out_ref.shape
    count = picks_ref.shape[0] // entries
    draft = count * n // requests
    out_ref[...] = jnp.zeros(out_ref.shape, out_ref.dtype)
    for k in range(count):
        request = (lax.axis_index("tensor") ^ k) * n // draft
        out_ref[request] = out_ref[request] + picks_ref[k * entries : (k + 1) * entries, :]


def accepted(picks, requests, entries, n):
    return pl.pallas_call(
        functools.partial(accepted_kernel, n),
        out_shape=jax.ShapeDtypeStruct((requests, entries, picks.shape[1]), BF),
        in_specs=[whole()],
        out_specs=whole(),
        compiler_params=params(4),
        cost_estimate=cost(1e6),
        name="accepted",
    )(picks)


def rows_by_lane_block(kv):
    lead, (tokens, two, width) = kv.shape[:-3], kv.shape[-3:]
    split = kv.reshape(*lead, tokens, two, width // LANES, LANES)
    return jnp.swapaxes(split, -3, -2).reshape(*lead, tokens * two * width // LANES, LANES)


def body(
    hidden_in, queries, draft_kv, cache_kv, cache_len, parents, path, routes,
    w_out, router, norm_gain, w_gate, w_up, w_down,
):
    tensor = lax.axis_size("tensor")
    data = lax.axis_size("dp")
    n = queries.shape[0]
    requests, draft = parents.shape
    payload, keys, vals, ancestry, pos, limit, packed, picks = prelude(
        cache_len,
        path,
        parents,
        queries,
        rows_by_lane_block(draft_kv),
        rows_by_lane_block(cache_kv),
    )
    payloads = [payload] + [exchange(payload, "tensor", tensor, k) for k in range(1, tensor)]
    unpacked = unpack(packed)
    tables = jnp.swapaxes(routes, 1, 2), router.T
    gain = norm_gain.reshape(1, -1)
    if n == draft and tensor == PAIRS:
        parts = ()
        for k in range(tensor):
            parts = attend_split(
                k, tensor, payloads[k], unpacked, keys, vals, ancestry, pos, limit, parts
            )
        tables = lax.optimization_barrier((*tables, parts[0]))[:2]
        parts = [parts[0]] + [exchange(parts[j], "tensor", tensor, j) for j in range(1, tensor)]
        bias, route = routing(*tables)
        parts, bias, route = lax.optimization_barrier((parts, bias, route))
        products = join_split(w_out, parts)
        others = [exchange(products[k], "tensor", tensor, k) for k in range(1, tensor)]
        mixed, normed = norm(hidden_in, gain, products[0], others)
    else:
        half = w_out.shape[0] // CORES
        mine = lax.dynamic_slice_in_dim(w_out, lax.axis_index("dp") % CORES * half, half, 0)
        mine = lax.optimization_barrier((mine, *payloads[1:]))[0]
        fetched = [exchange(mine, "tensor", tensor, k) for k in range(1, tensor)]
        parts = []
        for k in range(tensor):
            near = k < max(1, draft // n)
            part = attend(k, near, payloads[k], unpacked, keys, vals, ancestry, pos, limit)
            parts.append(part if k == 0 else exchange(part, "tensor", tensor, k))
        pieces = [w_out]
        for piece in fetched:
            pieces += [piece, exchange(piece, "dp", data, 1)]
        mixed, normed = join(parts, pieces, hidden_in, gain)
        bias, route = routing(*tables)

    steps = data // CORES
    lines = {0: normed}
    reach = steps // 2
    while reach:
        for k in [k for k in lines if k % (2 * reach) == 0]:
            lines[k + reach] = exchange(lines[k], "dp", data, CORES * reach)
        reach //= 2
    single = [k for k in lines if k and k & (k - 1) == 0]
    total = mixed
    last = None
    for k in sorted(lines, key=lambda k: (bin(k).count("1"), -k)):
        if k == max(single) or (k and k not in single):
            names = single if k in single else [k]
            tied = lax.optimization_barrier([lines[name] for name in names] + [last])
            lines.update(zip(names, tied))
        line = lines[k]
        twin = exchange(line, "dp", data, 1)
        own, other = experts_part(k, bias, route, w_gate, w_up, w_down, line, twin)
        last = own
        if k == 1:
            picks = lax.optimization_barrier((picks, own))[0]
        chip = own + exchange(other, "dp", data, 1).astype(F32)
        if k:
            chip = chip.astype(BF)
            chip = exchange(chip, "dp", data, CORES * k).astype(F32)
        total = total + chip
    reach = 1
    while reach < tensor:
        picks = jnp.concatenate([picks, exchange(picks, "tensor", tensor, reach)], axis=0)
        reach *= 2
    compacted = accepted(picks, requests, path.shape[1], n)
    return total.astype(BF), compacted


def solution(mesh):
    in_specs = (
        P(("dp", "tensor"), None),
        P(("dp", "tensor"), None),
        P(("dp", "tensor"), None, None),
        P("dp", "tensor", None, None),
        P("dp"),
        P("dp", None),
        P("dp", None),
        P(None, "tensor", None),
        P("tensor", None),
        P(),
        P(),
        P("dp", None, None),
        P("dp", None, None),
        P("dp", None, None),
    )
    out_specs = (P(("dp", "tensor"), None), P("dp", None, None))
    return jax.shard_map(body, mesh=mesh, in_specs=in_specs, out_specs=out_specs, check_vma=False)
```

```python
import functools

import jax
import jax.numpy as jnp
import numpy as np
from jax import lax
from jax.experimental import pallas as pl
from jax.experimental.pallas import tpu as pltpu
from jax.sharding import PartitionSpec as P

QH = 24
KVH = 8
HD = 64
TOP = 8
SINKS = 4
WINDOW = 1024

LANES = 128
PAIRS = KVH * HD // LANES
GROUPS = QH // KVH
CORES = 2
NEG = -1e30
FLOOR = -1e6
BF = jnp.bfloat16
F32 = jnp.float32
LOG2E = 1.4426950408889634
MIB = 1024 * 1024

INVERSE = [
    float(x)
    for x in (10000.0 ** (-2.0 * np.arange(HD // 2, dtype=np.float64) / HD)).astype(np.float32)
]


def params(mib):
    return pltpu.CompilerParams(vmem_limit_bytes=mib * MIB)


def whole():
    return pl.BlockSpec(memory_space=pltpu.VMEM)


def in_hbm():
    return pl.BlockSpec(memory_space=pltpu.HBM)


def fixed(x):
    return pltpu.with_memory_space_constraint(x, pltpu.HBM)


def cost(flops):
    return pl.CostEstimate(flops=int(flops), bytes_accessed=0, transcendentals=0)


def exchange(x, axis, size, step):
    return lax.ppermute(x, axis, [(i, i ^ step) for i in range(size)])


def lane_index(shape):
    return lax.broadcasted_iota(jnp.int32, shape, len(shape) - 1)


def prelude_kernel(
    len_hbm, path_hbm, par_hbm, q_hbm, kv_hbm, cache_hbm,
    pay_ref, key_ref, val_ref, anc_ref, pos_ref, lim_ref, packed_ref, pick_ref,
    len_ref, path_ref, par_ref, q_ref, kv_ref, kv_f, anc_all, sems,
):
    copies = [
        pltpu.make_async_copy(src, dst, sems.at[j])
        for j, (src, dst) in enumerate(
            (
                (par_hbm, par_ref), (len_hbm, len_ref), (path_hbm, path_ref),
                (kv_hbm, kv_ref), (q_hbm, q_ref), (cache_hbm, packed_ref),
            )
        )
    ]
    for copy in copies:
        copy.start()
    for copy in copies[:3]:
        copy.wait()
    requests, draft = par_ref.shape
    n = q_ref.shape[0]
    own_start = lax.axis_index("tensor") * n
    request = own_start // draft
    offset = own_start % draft
    row = lax.broadcasted_iota(jnp.int32, (draft, draft), 0)
    col = lax.broadcasted_iota(jnp.int32, (draft, draft), 1)
    eye = (row == col).astype(F32)
    linked = [
        ((row == par_ref[r : r + 1, :]).astype(F32) + eye).T.astype(BF) for r in range(requests)
    ]
    for level in range((draft - 1).bit_length()):
        linked = [
            jnp.minimum(jnp.dot(m, m, preferred_element_type=F32), 1.0).astype(BF) for m in linked
        ]
    for r in range(requests):
        ancestry = linked[r].astype(F32)
        depth = jnp.sum(ancestry, axis=-1, keepdims=True) - 1.0
        place = depth + len_ref[r].astype(F32)
        pos_ref[r * draft : (r + 1) * draft, :] = jnp.broadcast_to(place, (draft, LANES))
        lim_ref[r] = jnp.full((8, LANES), len_ref[r].astype(F32))
        anc_all[r] = ancestry
    anc_ref[...] = anc_all[request]
    own = pl.multiple_of(own_start, 8)
    lane = lane_index((n, LANES))
    step = lane_index((8, LANES)) % (HD // 2)
    inverse = jnp.full(step.shape, INVERSE[0], F32)
    for k in range(1, HD // 2):
        inverse = jnp.where(step == k, INVERSE[k], inverse)
    angle = pos_ref[pl.ds(own, n), :] * inverse[:1, :]
    front = lane % HD < HD // 2
    cosine = jnp.cos(angle)
    sine = jnp.sin(angle)
    sine = jnp.where(front, -sine, sine)
    low = lane < HD

    def turned(x):
        partner = jnp.where(
            front, pltpu.roll(x, LANES - HD // 2, axis=1), pltpu.roll(x, HD // 2, axis=1)
        )
        return x * cosine + partner * sine

    copies[3].wait()
    kv_f[...] = kv_ref[...].astype(F32)
    slot = lax.broadcasted_iota(jnp.int32, (path_ref.shape[1], n), 0)
    token = lax.broadcasted_iota(jnp.int32, (path_ref.shape[1], n), 1) + offset
    wanted = jnp.full(slot.shape, -1, jnp.int32)
    for k in range(path_ref.shape[1]):
        wanted = jnp.where(slot == k, path_ref[request, k], wanted)
    chooser = (wanted == token).astype(BF)
    keys, vals = [], []
    for b in range(PAIRS):
        keys.append(turned(kv_f[pl.ds(2 * b, n, stride=2 * PAIRS), :]).astype(BF))
        vals.append(kv_f[pl.ds(2 * b + 1, n, stride=2 * PAIRS), :].astype(BF))
        key_ref[:, b * LANES : (b + 1) * LANES] = keys[b]
        val_ref[:, b * LANES : (b + 1) * LANES] = vals[b]
    copies[4].wait()
    packed = jnp.concatenate(keys + vals, axis=1)
    pick_ref[...] = jnp.dot(chooser, packed, preferred_element_type=F32).astype(BF)
    for b in range(PAIRS):
        x0, x1, x2 = [
            turned(q_ref[:, (GROUPS * b + i) * LANES : (GROUPS * b + i + 1) * LANES].astype(F32))
            for i in range(GROUPS)
        ]
        y0 = jnp.where(low, x0, x1)
        y1 = jnp.where(low, pltpu.roll(x0, HD, axis=1), pltpu.roll(x2, HD, axis=1))
        y2 = jnp.where(low, x1, x2)
        for i, y in enumerate((y0, y1, y2)):
            pay_ref[:, (GROUPS * b + i) * LANES : (GROUPS * b + i + 1) * LANES] = y.astype(BF)
    copies[5].wait()


def prelude(cache_len, path, parents, queries, kv, cache):
    requests, draft = parents.shape
    n, width = queries.shape
    kv_width = KVH * HD
    return pl.pallas_call(
        prelude_kernel,
        out_shape=(
            jax.ShapeDtypeStruct((n, width), BF),
            jax.ShapeDtypeStruct((n, kv_width), BF),
            jax.ShapeDtypeStruct((n, kv_width), BF),
            jax.ShapeDtypeStruct((draft, draft), F32),
            jax.ShapeDtypeStruct((requests * draft, LANES), F32),
            jax.ShapeDtypeStruct((requests, 8, LANES), F32),
            jax.ShapeDtypeStruct(cache.shape, BF),
            jax.ShapeDtypeStruct((path.shape[1], 2 * kv_width), BF),
        ),
        in_specs=[in_hbm()] * 6,
        out_specs=(whole(),) * 8,
        scratch_shapes=[
            pltpu.SMEM(cache_len.shape, jnp.int32),
            pltpu.SMEM(path.shape, jnp.int32),
            pltpu.VMEM(parents.shape, jnp.int32),
            pltpu.VMEM(queries.shape, BF),
            pltpu.VMEM(kv.shape, BF),
            pltpu.VMEM(kv.shape, F32),
            pltpu.VMEM((requests, draft, draft), F32),
            pltpu.SemaphoreType.DMA((6,)),
        ],
        compiler_params=params(8),
        cost_estimate=cost(1e7),
        name="prelude",
    )(*[fixed(x) for x in (cache_len, path, parents, queries, kv, cache)])


def unpack_kernel(packed_ref, out_ref, kv_f):
    requests, _, cells, _ = out_ref.shape
    for r in range(requests):
        kv_f[r % 2] = packed_ref[r].astype(F32)
        for j in range(2 * PAIRS):
            out_ref[r, j] = kv_f[r % 2, pl.ds(j, cells, stride=2 * PAIRS), :].astype(BF)


def unpack(packed):
    requests, span, _ = packed.shape
    return pl.pallas_call(
        unpack_kernel,
        out_shape=jax.ShapeDtypeStruct(
            (requests, 2 * PAIRS, span // (2 * PAIRS), LANES), BF
        ),
        in_specs=[whole()],
        out_specs=whole(),
        scratch_shapes=[pltpu.VMEM((2, span, LANES), F32)],
        compiler_params=params(8),
        cost_estimate=cost(1e8),
        name="unpack",
    )(packed)


def routing_kernel(routes_hbm, router_hbm, bias_ref, route_w_ref, routes_ref, router_ref, sems):
    copies = [
        pltpu.make_async_copy(routes_hbm, routes_ref, sems.at[0]),
        pltpu.make_async_copy(router_hbm, router_ref, sems.at[1]),
    ]
    for copy in copies:
        copy.start()
    for copy in copies:
        copy.wait()
    experts = router_ref.shape[0]
    router = router_ref[...]
    high = router.astype(BF)
    route_w_ref[:experts, :] = high
    route_w_ref[experts:, :] = (router - high.astype(F32)).astype(BF)
    for d in range(routes_ref.shape[0]):
        chosen = routes_ref[d]
        expert = lax.broadcasted_iota(jnp.int32, (experts, chosen.shape[1]), 0)
        hit = expert == chosen[0:1, :]
        for k in range(1, chosen.shape[0]):
            hit = hit | (expert == chosen[k : k + 1, :])
        bias_ref[d] = jnp.where(hit, 0.0, NEG).T


def routing(routes, router):
    experts, width = router.shape
    blocks, top, n = routes.shape
    return pl.pallas_call(
        routing_kernel,
        out_shape=(
            jax.ShapeDtypeStruct((blocks, n, experts), F32),
            jax.ShapeDtypeStruct((2 * experts, width), BF),
        ),
        in_specs=[in_hbm()] * 2,
        out_specs=(whole(),) * 2,
        scratch_shapes=[
            pltpu.VMEM(routes.shape, jnp.int32),
            pltpu.VMEM(router.shape, F32),
            pltpu.SemaphoreType.DMA((2,)),
        ],
        compiler_params=params(8),
        cost_estimate=cost(1e6),
        name="routing",
    )(fixed(routes), fixed(router))


def attend_kernel(
    step, near, pay_ref, kv_ref, key_ref, val_ref, anc_ref, pos_ref, lim_ref, out_ref
):
    draft = anc_ref.shape[0]
    n = key_ref.shape[0]
    cells = kv_ref.shape[2]
    me = lax.axis_index("tensor")
    start = (me ^ step) * n
    request = start // draft
    key_start = me * cells
    place = pos_ref[pl.ds(pl.multiple_of(start, 8), n), :][:, :1]
    key_pos = (lane_index((n, cells)) + key_start).astype(F32)
    far_ok = (key_pos < lim_ref[request][:1, :1]) & (
        (key_pos < SINKS) | (place - key_pos < WINDOW)
    )
    bias = jnp.where(far_ok, 0.0, NEG)
    bias = jnp.concatenate([bias] * (2 * GROUPS), axis=0)
    if near:
        own = me * n
        same = (own // draft) == request
        line = anc_ref[pl.ds(pl.multiple_of(start % draft, 8), n), :]
        if n != draft:
            pick = (
                lax.broadcasted_iota(jnp.int32, (draft, n), 0)
                == lax.broadcasted_iota(jnp.int32, (draft, n), 1) + own % draft
            ).astype(BF)
            line = jnp.dot(line.astype(BF), pick, preferred_element_type=F32)
        seen = jnp.where(same, line, 0.0)
        near_bias = jnp.where(seen > 0.5, 0.0, NEG)
        near_bias = jnp.concatenate([near_bias] * (2 * GROUPS), axis=0)
    low = lane_index((n, LANES)) < HD
    lane = lane_index((n, LANES))
    stats = jnp.zeros((n, LANES), F32)
    turn = (((1,), (1,)), ((), ()))
    factor = HD ** (-0.5) * LOG2E
    for b in range(PAIRS):
        keys = kv_ref[request, 2 * b]
        vals = kv_ref[request, 2 * b + 1]
        blocks = [
            pay_ref[:n, (GROUPS * b + i) * LANES : (GROUPS * b + i + 1) * LANES]
            for i in range(GROUPS)
        ]
        zero = jnp.zeros((n, LANES), BF)
        rows = jnp.concatenate(
            [jnp.where(low, x, zero) for x in blocks] + [jnp.where(low, zero, x) for x in blocks],
            axis=0,
        )
        scores = lax.dot_general(rows, keys, turn, preferred_element_type=F32) * factor + bias
        top = jnp.max(scores, axis=-1, keepdims=True)
        if near:
            near_scores = (
                lax.dot_general(
                    rows, key_ref[:, b * LANES : (b + 1) * LANES], turn, preferred_element_type=F32
                )
                * factor
                + near_bias
            )
            top = jnp.maximum(top, jnp.max(near_scores, axis=-1, keepdims=True))
        top = jnp.maximum(top, FLOOR)
        top = (top + jnp.abs(top) * (2.0**-7)).astype(BF).astype(F32)
        weights = jnp.exp2(scores - top)
        total = jnp.sum(weights, axis=-1, keepdims=True)
        blend = jnp.dot(weights.astype(BF), vals, preferred_element_type=F32)
        if near:
            near_weights = jnp.exp2(near_scores - top)
            total = total + jnp.sum(near_weights, axis=-1, keepdims=True)
            blend = blend + jnp.dot(
                near_weights.astype(BF),
                val_ref[:, b * LANES : (b + 1) * LANES],
                preferred_element_type=F32,
            )
        high = total.astype(BF).astype(F32)
        rest = total - high
        for i in range(GROUPS):
            first = slice(i * n, (i + 1) * n)
            second = slice((GROUPS + i) * n, (GROUPS + i + 1) * n)
            block = GROUPS * b + i
            out_ref[:, block * LANES : (block + 1) * LANES] = jnp.where(
                low, blend[first], blend[second]
            ).astype(BF)
            for part, rows_of in enumerate((first, second)):
                at = 2 * block + part
                stats = jnp.where(lane == at, top[rows_of], stats)
                stats = jnp.where(lane == QH + at, high[rows_of], stats)
                stats = jnp.where(lane == 2 * QH + at, rest[rows_of], stats)
    out_ref[:, QH * HD :] = stats.astype(BF)


def attend(step, near, payload, cache, keys, vals, ancestry, pos, limit):
    n = keys.shape[0]
    return pl.pallas_call(
        functools.partial(attend_kernel, step, near),
        out_shape=jax.ShapeDtypeStruct((n, QH * HD + LANES), BF),
        in_specs=[whole()] * 7,
        out_specs=whole(),
        compiler_params=params(12),
        name="attend",
    )(payload, cache, keys, vals, ancestry, pos, limit)


SPAN = 2 * GROUPS


def attend_split_kernel(
    step, near, count, pay_ref, kv_ref, key_ref, val_ref, anc_ref, pos_ref, lim_ref, *refs
):
    out_refs = refs[-count:]
    n = key_ref.shape[0]
    cells = kv_ref.shape[2]
    me = lax.axis_index("tensor")
    start = (me ^ step) * n
    request = me ^ step
    place = pos_ref[pl.ds(pl.multiple_of(start, 8), n), :][:, :1]
    key_pos = (lane_index((n, cells)) + me * cells).astype(F32)
    far_ok = (key_pos < lim_ref[request][:1, :1]) & (
        (key_pos < SINKS) | (place - key_pos < WINDOW)
    )
    bias = jnp.where(far_ok, 0.0, NEG)
    bias = jnp.concatenate([bias] * SPAN, axis=0)
    if near:
        near_bias = jnp.where(anc_ref[...] > 0.5, 0.0, NEG)
        near_bias = jnp.concatenate([near_bias] * SPAN, axis=0)
    lane = lane_index((n, LANES))
    low = lane < HD
    turn = (((1,), (1,)), ((), ()))
    factor = HD ** (-0.5) * LOG2E
    for j in range(count):
        b = me ^ j
        stats = jnp.zeros((n, LANES), F32) if near else out_refs[j][count * GROUPS].astype(F32)
        blocks = [
            pay_ref[:n, pl.ds(pl.multiple_of((GROUPS * b + i) * LANES, LANES), LANES)]
            for i in range(GROUPS)
        ]
        zero = jnp.zeros((n, LANES), BF)
        rows = jnp.concatenate(
            [jnp.where(low, x, zero) for x in blocks] + [jnp.where(low, zero, x) for x in blocks],
            axis=0,
        )
        scores = (
            lax.dot_general(rows, kv_ref[request, 2 * b], turn, preferred_element_type=F32) * factor
            + bias
        )
        top = jnp.max(scores, axis=-1, keepdims=True)
        if near:
            at_pair = pl.ds(pl.multiple_of(b * LANES, LANES), LANES)
            near_scores = (
                lax.dot_general(rows, key_ref[:, at_pair], turn, preferred_element_type=F32) * factor
                + near_bias
            )
            top = jnp.maximum(top, jnp.max(near_scores, axis=-1, keepdims=True))
        top = jnp.maximum(top, FLOOR)
        top = (top + jnp.abs(top) * (2.0**-7)).astype(BF).astype(F32)
        weights = jnp.exp2(scores - top)
        total = jnp.sum(weights, axis=-1, keepdims=True)
        blend = jnp.dot(weights.astype(BF), kv_ref[request, 2 * b + 1], preferred_element_type=F32)
        if near:
            near_weights = jnp.exp2(near_scores - top)
            total = total + jnp.sum(near_weights, axis=-1, keepdims=True)
            blend = blend + jnp.dot(
                near_weights.astype(BF), val_ref[:, at_pair], preferred_element_type=F32
            )
        high = total.astype(BF).astype(F32)
        rest = total - high
        for i in range(GROUPS):
            first = slice(i * n, (i + 1) * n)
            second = slice((GROUPS + i) * n, (GROUPS + i + 1) * n)
            out_refs[j][step * GROUPS + i] = jnp.where(low, blend[first], blend[second]).astype(BF)
            for part, rows_of in enumerate((first, second)):
                at = 3 * SPAN * step + 2 * i + part
                stats = jnp.where(lane == at, top[rows_of], stats)
                stats = jnp.where(lane == at + SPAN, high[rows_of], stats)
                stats = jnp.where(lane == at + 2 * SPAN, rest[rows_of], stats)
        out_refs[j][count * GROUPS] = stats.astype(BF)


def attend_split(step, count, payload, cache, keys, vals, ancestry, pos, limit, outs):
    n = keys.shape[0]
    shape = jax.ShapeDtypeStruct((count * GROUPS + 1, n, LANES), BF)
    return pl.pallas_call(
        functools.partial(attend_split_kernel, step, step == 0, count),
        out_shape=(shape,) * count,
        in_specs=[whole()] * (7 + len(outs)),
        out_specs=(whole(),) * count,
        input_output_aliases={7 + j: j for j in range(len(outs))},
        compiler_params=params(12),
        cost_estimate=cost(4e8),
        name="attend",
    )(payload, cache, keys, vals, ancestry, pos, limit, *outs)


def join_split_kernel(count, weight_ref, *refs):
    parts, out_refs, att = refs[:count], refs[count:-1], refs[-1]
    n = parts[0].shape[1]
    lane = lane_index((n, LANES))
    low = lane < HD
    shifts = [p[count * GROUPS].astype(F32) for p in parts]
    totals = [
        pltpu.roll(s, LANES - SPAN, axis=1) + pltpu.roll(s, LANES - 2 * SPAN, axis=1)
        for s in shifts
    ]
    for k in range(count):
        moves = [(LANES - 3 * SPAN * (j ^ k)) % LANES for j in range(count)]
        tops = [pltpu.roll(s, m, axis=1) if m else s for s, m in zip(shifts, moves)]
        sums = [pltpu.roll(s, m, axis=1) if m else s for s, m in zip(totals, moves)]
        top = functools.reduce(jnp.maximum, tops)
        scales = [jnp.exp2(t - top) for t in tops]
        inverse = 1.0 / functools.reduce(jnp.add, [a * b for a, b in zip(scales, sums)])
        scales = [scale * inverse for scale in scales]
        joined = []
        for i in range(GROUPS):
            acc = jnp.zeros((n, LANES), F32)
            for j in range(count):
                by = jnp.where(
                    low, scales[j][:, 2 * i : 2 * i + 1], scales[j][:, 2 * i + 1 : 2 * i + 2]
                )
                acc = acc + by * parts[j][(j ^ k) * GROUPS + i].astype(F32)
            joined.append(acc)
        turned = pltpu.roll(joined[1], HD, axis=1)
        back = (
            jnp.where(low, joined[0], turned),
            jnp.where(low, joined[2], joined[0]),
            jnp.where(low, turned, joined[2]),
        )
        for i in range(GROUPS):
            att[k * n : (k + 1) * n, i * LANES : (i + 1) * LANES] = back[i].astype(BF)
    for k in list(range(1, count)) + [0]:
        product = jnp.dot(att[k * n : (k + 1) * n, :], weight_ref[...], preferred_element_type=F32)
        out_refs[k][...] = product.astype(out_refs[k].dtype)


def join_split(weight, parts):
    count = len(parts)
    n = parts[0].shape[1]
    width = weight.shape[1]
    return pl.pallas_call(
        functools.partial(join_split_kernel, count),
        out_shape=tuple(
            jax.ShapeDtypeStruct((n, width), BF if k else F32) for k in range(count)
        ),
        in_specs=[whole()] * (1 + count),
        out_specs=(whole(),) * count,
        scratch_shapes=[pltpu.VMEM((count * n, weight.shape[0]), BF)],
        compiler_params=params(12),
        cost_estimate=cost(4e8),
        name="join",
    )(weight, *parts)


def norm_kernel(hidden_ref, gain_ref, own_ref, *refs):
    others, (mixed_ref, normed_ref) = refs[:-2], refs[-2:]
    mixed = hidden_ref[...].astype(F32) + own_ref[...]
    for other in others:
        mixed = mixed + other[...].astype(F32)
    mixed_ref[...] = mixed
    square = jnp.mean(mixed * mixed, axis=-1, keepdims=True)
    normed_ref[...] = (mixed * lax.rsqrt(square + 1e-06) * gain_ref[...]).astype(BF)


def norm(hidden_in, gain, own, others):
    return pl.pallas_call(
        norm_kernel,
        out_shape=(
            jax.ShapeDtypeStruct(hidden_in.shape, F32),
            jax.ShapeDtypeStruct(hidden_in.shape, BF),
        ),
        in_specs=[whole()] * (3 + len(others)),
        out_specs=(whole(), whole()),
        compiler_params=params(4),
        cost_estimate=cost(1e6),
        name="norm",
    )(hidden_in, gain, own, *others)


def join_kernel(count, *refs):
    parts, rest = refs[:count], refs[count:]
    shares = 2 * count - 1
    pieces, rest = rest[:shares], rest[shares:]
    hidden_ref, gain_ref, mixed_ref, normed_ref, att, weight, sems = rest
    n = hidden_ref.shape[0]
    depth = pieces[0].shape[0]
    half = depth // CORES
    width = QH * HD
    me = lax.axis_index("tensor")
    core = lax.axis_index("dp") % CORES
    starts = [me * depth]
    for k in range(1, count):
        starts += [(me ^ k) * depth + core * half, (me ^ k) * depth + (1 - core) * half]
    copies = []
    for j, (piece, start) in enumerate(zip(pieces, starts)):
        rows = weight.at[pl.ds(pl.multiple_of(start, 16), piece.shape[0]), :]
        copies.append(pltpu.make_async_copy(piece, rows, sems.at[j]))
        copies[-1].start()
    stats = [p[:, width:].astype(F32) for p in parts]
    top = stats[0]
    for s in stats[1:]:
        top = jnp.maximum(top, s)
    scales = [jnp.exp2(s - top) for s in stats]
    total = jnp.zeros((n, LANES), F32)
    for s, scale in zip(stats, scales):
        sums = pltpu.roll(s, LANES - QH, axis=1) + pltpu.roll(s, LANES - 2 * QH, axis=1)
        total = total + scale * sums
    inverse = 1.0 / total
    scales = [scale * inverse for scale in scales]
    low = lane_index((n, LANES)) < HD

    for b in range(PAIRS):
        joined = []
        for i in range(GROUPS):
            block = GROUPS * b + i
            acc = jnp.zeros((n, LANES), F32)
            for p, scale in zip(parts, scales):
                by = jnp.where(
                    low, scale[:, 2 * block : 2 * block + 1], scale[:, 2 * block + 1 : 2 * block + 2]
                )
                acc = acc + by * p[:, block * LANES : (block + 1) * LANES].astype(F32)
            joined.append(acc)
        turned = pltpu.roll(joined[1], HD, axis=1)
        back = (
            jnp.where(low, joined[0], turned),
            jnp.where(low, joined[2], joined[0]),
            jnp.where(low, turned, joined[2]),
        )
        for i in range(GROUPS):
            block = GROUPS * b + i
            att[:, block * LANES : (block + 1) * LANES] = back[i].astype(BF)
    for copy in copies:
        copy.wait()
    attended = jnp.dot(att[...], weight[...], preferred_element_type=F32)
    mixed = hidden_ref[...].astype(F32) + attended
    mixed_ref[...] = mixed
    square = jnp.mean(mixed * mixed, axis=-1, keepdims=True)
    normed_ref[...] = (mixed * lax.rsqrt(square + 1e-06) * gain_ref[...]).astype(BF)


def join(parts, pieces, hidden_in, gain):
    n, width = hidden_in.shape
    count = len(parts)
    inner = QH * HD
    return pl.pallas_call(
        functools.partial(join_kernel, count),
        out_shape=(
            jax.ShapeDtypeStruct((n, width), F32),
            jax.ShapeDtypeStruct((n, width), BF),
        ),
        in_specs=[whole()] * count
        + [pl.BlockSpec(memory_space=pl.ANY)] * len(pieces)
        + [whole(), whole()],
        out_specs=(whole(), whole()),
        scratch_shapes=[
            pltpu.VMEM((n, inner), BF),
            pltpu.VMEM((inner, width), BF),
            pltpu.SemaphoreType.DMA((len(pieces),)),
        ],
        compiler_params=params(14),
        name="join",
    )(*parts, *pieces, hidden_in, gain)


def experts_kernel(
    step, bias_ref, route_ref, wg, wu, wd, a_ref, b_ref, own_ref, other_ref
):
    n, width = a_ref.shape
    local = wg.shape[0]
    experts = bias_ref.shape[2]
    me = lax.axis_index("dp")
    x = jnp.concatenate([a_ref[...], b_ref[...]], axis=0)
    logits = lax.dot_general(
        x, route_ref[...], (((1,), (1,)), ((), ())), preferred_element_type=F32
    )
    logits = logits[:, :experts] + logits[:, experts:]
    first = CORES * step
    logits = logits + jnp.concatenate([bias_ref[me ^ first], bias_ref[me ^ (first + 1)]], axis=0)
    gates = jnp.exp(logits - jnp.max(logits, axis=-1, keepdims=True))
    gates = gates / jnp.sum(gates, axis=-1, keepdims=True)
    lane = lane_index(gates.shape)
    acc = None
    for e in range(local):
        gate_hidden = jnp.dot(x, wg[e], preferred_element_type=F32)
        up_hidden = jnp.dot(x, wu[e], preferred_element_type=F32)
        activated = (gate_hidden / (1.0 + jnp.exp(-gate_hidden)) * up_hidden).astype(BF)
        made = jnp.dot(activated, wd[e], preferred_element_type=F32).astype(BF).astype(F32)
        gate = jnp.sum(jnp.where(lane == me * local + e, gates, 0.0), axis=-1, keepdims=True)
        acc = gate * made if acc is None else acc + gate * made
    own_ref[...] = acc[:n]
    other_ref[...] = acc[n:].astype(BF)


def experts_part(step, bias, route, w_gate, w_up, w_down, a, b):
    n, width = a.shape
    return pl.pallas_call(
        functools.partial(experts_kernel, step),
        out_shape=(
            jax.ShapeDtypeStruct((n, width), F32),
            jax.ShapeDtypeStruct((n, width), BF),
        ),
        in_specs=[whole()] * 7,
        out_specs=(whole(), whole()),
        compiler_params=params(12),
        cost_estimate=cost(12e8),
        name="experts",
    )(bias, route, w_gate, w_up, w_down, a, b)


def accepted_kernel(n, picks_ref, out_ref):
    requests, entries, _ = out_ref.shape
    count = picks_ref.shape[0] // entries
    draft = count * n // requests
    out_ref[...] = jnp.zeros(out_ref.shape, out_ref.dtype)
    for k in range(count):
        request = (lax.axis_index("tensor") ^ k) * n // draft
        out_ref[request] = out_ref[request] + picks_ref[k * entries : (k + 1) * entries, :]


def accepted(picks, requests, entries, n):
    return pl.pallas_call(
        functools.partial(accepted_kernel, n),
        out_shape=jax.ShapeDtypeStruct((requests, entries, picks.shape[1]), BF),
        in_specs=[whole()],
        out_specs=whole(),
        compiler_params=params(4),
        cost_estimate=cost(1e6),
        name="accepted",
    )(picks)


def rows_by_lane_block(kv):
    lead, (tokens, two, width) = kv.shape[:-3], kv.shape[-3:]
    split = kv.reshape(*lead, tokens, two, width // LANES, LANES)
    return jnp.swapaxes(split, -3, -2).reshape(*lead, tokens * two * width // LANES, LANES)


def body(
    hidden_in, queries, draft_kv, cache_kv, cache_len, parents, path, routes,
    w_out, router, norm_gain, w_gate, w_up, w_down,
):
    tensor = lax.axis_size("tensor")
    data = lax.axis_size("dp")
    n = queries.shape[0]
    requests, draft = parents.shape
    payload, keys, vals, ancestry, pos, limit, packed, picks = prelude(
        cache_len,
        path,
        parents,
        queries,
        rows_by_lane_block(draft_kv),
        rows_by_lane_block(cache_kv),
    )
    payloads = [payload] + [exchange(payload, "tensor", tensor, k) for k in range(1, tensor)]
    unpacked = unpack(packed)
    tables = jnp.swapaxes(routes, 1, 2), router.T
    gain = norm_gain.reshape(1, -1)
    if n == draft and tensor == PAIRS:
        parts = ()
        for k in range(tensor):
            parts = attend_split(
                k, tensor, payloads[k], unpacked, keys, vals, ancestry, pos, limit, parts
            )
        tables = lax.optimization_barrier((*tables, parts[0]))[:2]
        parts = [parts[0]] + [exchange(parts[j], "tensor", tensor, j) for j in range(1, tensor)]
        bias, route = routing(*tables)
        parts, bias, route = lax.optimization_barrier((parts, bias, route))
        products = join_split(w_out, parts)
        others = [exchange(products[k], "tensor", tensor, k) for k in range(1, tensor)]
        mixed, normed = norm(hidden_in, gain, products[0], others)
    else:
        half = w_out.shape[0] // CORES
        mine = lax.dynamic_slice_in_dim(w_out, lax.axis_index("dp") % CORES * half, half, 0)
        mine = lax.optimization_barrier((mine, *payloads[1:]))[0]
        fetched = [exchange(mine, "tensor", tensor, k) for k in range(1, tensor)]
        parts = []
        for k in range(tensor):
            near = k < max(1, draft // n)
            part = attend(k, near, payloads[k], unpacked, keys, vals, ancestry, pos, limit)
            parts.append(part if k == 0 else exchange(part, "tensor", tensor, k))
        pieces = [w_out]
        for piece in fetched:
            pieces += [piece, exchange(piece, "dp", data, 1)]
        mixed, normed = join(parts, pieces, hidden_in, gain)
        bias, route = routing(*tables)

    steps = data // CORES
    lines = {0: normed}
    reach = steps // 2
    while reach:
        for k in [k for k in lines if k % (2 * reach) == 0]:
            lines[k + reach] = exchange(lines[k], "dp", data, CORES * reach)
        reach //= 2
    single = [k for k in lines if k and k & (k - 1) == 0]
    far = []
    last = None
    for k in sorted(lines, key=lambda k: (bin(k).count("1"), -k)):
        if k == max(single) or (k and k not in single):
            names = single if k in single else [k]
            held = [last] if k in single else [last, base]
            tied = lax.optimization_barrier([lines[name] for name in names] + held)
            lines.update(zip(names, tied))
            if k not in single:
                base = tied[-1]
        line = lines[k]
        twin = exchange(line, "dp", data, 1)
        own, other = experts_part(k, bias, route, w_gate, w_up, w_down, line, twin)
        last = own
        if k == 1:
            picks = lax.optimization_barrier((picks, own))[0]
        chip = own + exchange(other, "dp", data, 1).astype(F32)
        if k:
            chip = chip.astype(BF)
            chip = exchange(chip, "dp", data, CORES * k).astype(F32)
        if k:
            far.append(chip)
        else:
            base = mixed + chip
    reach = 1
    while reach < tensor:
        picks = jnp.concatenate([picks, exchange(picks, "tensor", tensor, reach)], axis=0)
        reach *= 2
    compacted = accepted(picks, requests, path.shape[1], n)
    return functools.reduce(jnp.add, far, base).astype(BF), compacted


def solution(mesh):
    in_specs = (
        P(("dp", "tensor"), None),
        P(("dp", "tensor"), None),
        P(("dp", "tensor"), None, None),
        P("dp", "tensor", None, None),
        P("dp"),
        P("dp", None),
        P("dp", None),
        P(None, "tensor", None),
        P("tensor", None),
        P(),
        P(),
        P("dp", None, None),
        P("dp", None, None),
        P("dp", None, None),
    )
    out_specs = (P(("dp", "tensor"), None), P("dp", None, None))
    return jax.shard_map(body, mesh=mesh, in_specs=in_specs, out_specs=out_specs, check_vma=False)
```
